128 devices in a mesh: tm: 8 (over z_lo, x), azim: 16 (over y, z_hi, core).
Axes of the slice: x: 4, y: 4, z: 4 (z_hi: 2, z_lo: 2; z = z_hi * 2 + z_lo), core: 2. Of those that a mesh axis runs over, the one named last changes fastest.
Arguments:
- initial_state: float32 [3, 64, 96, 256], P(None, 'azim'), may hold values from -6 to 6
- forcing: float32 [3, 64, 96, 256], P(None, 'azim'), may hold values from -12 to 12
- forward_radial: float32 [96, 96], replicated, may hold values from -0.21875 to 0.21875
- backward_radial: float32 [96, 96], replicated, may hold values from -0.21875 to 0.21875
- forward_axial: float32 [256, 256], replicated, may hold values from -0.125 to 0.125
- backward_axial: float32 [256, 256], replicated, may hold values from -0.125 to 0.125
- forward_radial_coarse: float32 [48, 48], replicated, may hold values from -0.3125 to 0.3125
- backward_radial_coarse: float32 [48, 48], replicated, may hold values from -0.3125 to 0.3125
- forward_axial_coarse: float32 [128, 128], replicated, may hold values from -0.1875 to 0.1875
- backward_axial_coarse: float32 [128, 128], replicated, may hold values from -0.1875 to 0.1875
- decay_radial: float32 [96], replicated, may hold values from 0.01 to 10
- decay_axial: float32 [256], replicated, may hold values from 0.01 to 10
- advection: float32 [96, 256], replicated, may hold values from -0.6 to 0.6
- diffusion: float32 [96], replicated, may hold values from 0.05 to 0.4
Outputs:
- end_states: float32 [8, 3, 64, 96, 256], P('tm', None, 'azim')
The draws below stay inside these ranges and needn't reach their ends.
All inputs are finite; a program needn't handle non-finite values.
Results may differ from the reference program's by a relative error of at most 0.0001.
Values sent between devices are 32-bit elements; how exact they have to be, the bound alone decides.
No kernel may reach another device: no remote copies, remote signals or barrier semaphores. Data moves between devices by JAX's collectives and lax.ppermute only.
A program may use at most 64 MiB of HBM per device.

```python
import math
import jax
import jax.numpy as jnp
from jax import lax

RADIAL = 96
AXIAL = 256
ITERS = 2
AZIMUTH = 64
SLICES = 8
RADIAL_C = 48
AXIAL_C = 128


def block_scale(key, dims, pieces, low, high):
    level, own = 1.0, jax.random.fold_in(key, 6)
    for axis_at, blocks in pieces:
        steps = jnp.exp(jax.random.uniform(jax.random.fold_in(own, axis_at), (blocks,), jnp.float32, low / len(pieces), high / len(pieces)))
        level = level * jnp.repeat(steps, dims[axis_at] // blocks).reshape([-1 if axis == axis_at else 1 for axis in range(len(dims))])
    return level


def centred(stream_key, shape, scale, bound, cuts=(), kind=jnp.bfloat16):
    drawn = jax.random.normal(stream_key, shape, jnp.float32) * scale
    if len(cuts) > 0:
        drawn = block_scale(stream_key, shape, cuts, -0.22, 0.18) * drawn
    return jnp.clip(drawn, min=-bound, max=bound).astype(kind)


def setup_inputs(seed: int = 0) -> dict:
    splits = jax.random.split(jax.random.key(seed), 15)
    initial_state = centred(splits[0], (3, AZIMUTH, RADIAL, AXIAL), 1.0, 6.0, ((1, 16),), jnp.float32)
    forcing = centred(splits[1], (3, AZIMUTH, RADIAL, AXIAL), 2.0, 12.0, ((1, 16),), jnp.float32)
    forward_radial = centred(splits[2], (RADIAL, RADIAL), (8 * RADIAL) ** -0.5, 0.21875, (), jnp.float32)
    backward_radial = centred(splits[3], (RADIAL, RADIAL), (8 * RADIAL) ** -0.5, 0.21875, (), jnp.float32)
    forward_axial = centred(splits[4], (AXIAL, AXIAL), (8 * AXIAL) ** -0.5, 0.125, (), jnp.float32)
    backward_axial = centred(splits[5], (AXIAL, AXIAL), (8 * AXIAL) ** -0.5, 0.125, (), jnp.float32)
    forward_radial_coarse = centred(splits[6], (RADIAL_C, RADIAL_C), (8 * RADIAL_C) ** -0.5, 0.3125, (), jnp.float32)
    backward_radial_coarse = centred(splits[7], (RADIAL_C, RADIAL_C), (8 * RADIAL_C) ** -0.5, 0.3125, (), jnp.float32)
    forward_axial_coarse = centred(splits[8], (AXIAL_C, AXIAL_C), (8 * AXIAL_C) ** -0.5, 0.1875, (), jnp.float32)
    backward_axial_coarse = centred(splits[9], (AXIAL_C, AXIAL_C), (8 * AXIAL_C) ** -0.5, 0.1875, (), jnp.float32)
    decay_radial = jnp.clip(jnp.exp(jax.random.uniform(splits[10], (RADIAL,), jnp.float32, math.log(0.01), math.log(10.0))), 0.01, 10.0)
    decay_axial = jnp.clip(jnp.exp(jax.random.uniform(splits[11], (AXIAL,), jnp.float32, math.log(0.01), math.log(10.0))), 0.01, 10.0)
    advection = jnp.clip(jax.random.uniform(splits[12], (RADIAL, AXIAL), jnp.float32, -0.6, 0.6), -0.6, 0.6)
    diffusion = jnp.clip(jnp.exp(jax.random.uniform(splits[13], (RADIAL,), jnp.float32, math.log(0.05), math.log(0.4))), 0.05, 0.4)
    return {"initial_state": initial_state, "forcing": forcing, "forward_radial": forward_radial, "backward_radial": backward_radial, "forward_axial": forward_axial, "backward_axial": backward_axial, "forward_radial_coarse": forward_radial_coarse, "backward_radial_coarse": backward_radial_coarse, "forward_axial_coarse": forward_axial_coarse, "backward_axial_coarse": backward_axial_coarse, "decay_radial": decay_radial, "decay_axial": decay_axial, "advection": advection, "diffusion": diffusion}


HI = lax.Precision.HIGHEST
time_step = 0.1


def to_phys(modes, backward_r, backward_z):
    inner = jnp.einsum('...ij,zj->...iz', modes, backward_z, precision=HI)
    return jnp.einsum('ri,...iz->...rz', backward_r, inner, precision=HI)


def to_modal(field, forward_r, forward_z):
    inner = jnp.einsum('...rz,jz->...rj', field, forward_z, precision=HI)
    return jnp.einsum('ir,...rj->...ij', forward_r, inner, precision=HI)


def forces(field, upper, lower, advect, diffuse):
    spread = advect * (upper - lower) + diffuse[:, None] * (upper - 2.0 * field + lower)
    zero_part = jnp.zeros_like(field[..., 0, :, :, :])
    turning = jnp.stack([2.0 * field[..., 1, :, :, :], -2.0 * field[..., 0, :, :, :], zero_part], axis=-4)
    return spread + turning


def explicit(modes, operators):
    backward_r, backward_z, forward_r, forward_z, advect, diffuse = operators
    field = to_phys(modes, backward_r, backward_z)
    upper = jnp.roll(field, -1, axis=-3)
    lower = jnp.roll(field, 1, axis=-3)
    return to_modal(forces(field, upper, lower, advect, diffuse), forward_r, forward_z)


def reference(initial_state, forcing, forward_radial, backward_radial, forward_axial, backward_axial,
              forward_radial_coarse, backward_radial_coarse, forward_axial_coarse, backward_axial_coarse,
              decay_radial, decay_axial, advection, diffusion):
    radial = forward_radial.shape[0]
    axial = forward_axial.shape[0]
    radial_c = forward_radial_coarse.shape[0]
    axial_c = forward_axial_coarse.shape[0]
    eye_r = jnp.eye(radial, dtype=jnp.float32)
    eye_z = jnp.eye(axial, dtype=jnp.float32)
    eye_rc = jnp.eye(radial_c, dtype=jnp.float32)
    eye_zc = jnp.eye(axial_c, dtype=jnp.float32)
    fine_set = (eye_r + backward_radial, eye_z + backward_axial, eye_r + forward_radial, eye_z + forward_axial,
                advection, diffusion)
    coarse_set = (eye_rc + backward_radial_coarse, eye_zc + backward_axial_coarse, eye_rc + forward_radial_coarse,
                  eye_zc + forward_axial_coarse, advection[::2, ::2], diffusion[::2])
    spectrum = -(decay_radial[:, None] + decay_axial[None, :])
    coarse_spectrum = spectrum[:radial_c, :axial_c]
    half_step = 0.5 * time_step

    def propagate(state):
        return (state + time_step * explicit(state, coarse_set)) / (1.0 - time_step * coarse_spectrum)

    def widen(delta):
        widths = [(0, 0)] * (delta.ndim - 2) + [(0, radial - radial_c), (0, axial - axial_c)]
        return jnp.pad(delta, widths)

    base = jnp.broadcast_to(initial_state, (SLICES,) + initial_state.shape)
    base_push = explicit(initial_state, fine_set) + forcing
    pushes_all = jnp.broadcast_to(base_push, (SLICES,) + base_push.shape)
    nodes = [base, base, base]
    pushes = [pushes_all, pushes_all, pushes_all]
    start = base
    restricted_init = initial_state[:, :, :radial_c, :axial_c]
    for turn_index in range(ITERS):
        totals = [pushes[node_index] + spectrum * nodes[node_index] for node_index in range(3)]
        if turn_index == 0:
            start_push = pushes[0]
        else:
            start_push = explicit(start, fine_set) + forcing
        middle = (start + half_step * (start_push - pushes[0]) - half_step * spectrum * nodes[1]
                  + time_step * (5.0 / 24.0 * totals[0] + 1.0 / 3.0 * totals[1] - 1.0 / 24.0 * totals[2])) / (1.0 - half_step * spectrum)
        middle_push = explicit(middle, fine_set) + forcing
        ending = (middle + half_step * (middle_push - pushes[1]) - half_step * spectrum * nodes[2]
                  + time_step * (-1.0 / 24.0 * totals[0] + 1.0 / 3.0 * totals[1] + 5.0 / 24.0 * totals[2])) / (1.0 - half_step * spectrum)
        ending_push = explicit(ending, fine_set) + forcing
        nodes = [start, middle, ending]
        pushes = [start_push, middle_push, ending_push]
        totals = [pushes[node_index] + spectrum * nodes[node_index] for node_index in range(3)]
        integral = time_step * (totals[0] / 6.0 + 2.0 * totals[1] / 3.0 + totals[2] / 6.0)
        coarse_zero = nodes[0][..., :radial_c, :axial_c]
        coarse_one = nodes[2][..., :radial_c, :axial_c]
        constant = (integral[..., :radial_c, :axial_c] - time_step * explicit(coarse_zero, coarse_set)
                    - time_step * coarse_spectrum * coarse_one) / (1.0 - time_step * coarse_spectrum)
        previous = restricted_init
        begins = []
        endings = []
        for slice_index in range(SLICES):
            begins.append(previous)
            current = constant[slice_index] + propagate(previous)
            endings.append(current)
            previous = current
        delta_zero = jnp.stack(begins, axis=0) - coarse_zero
        delta_one = jnp.stack(endings, axis=0) - coarse_one
        nodes = [nodes[0] + widen(delta_zero), nodes[1] + widen(0.5 * (delta_zero + delta_one)), nodes[2] + widen(delta_one)]
        if turn_index + 1 < ITERS:
            pushes = [explicit(nodes[node_index], fine_set) + forcing for node_index in range(3)]
            start = jnp.concatenate([initial_state[None], nodes[2][:-1]], axis=0)
    return nodes[2]
```

```python
import ml_dtypes
import numpy as np
import jax
import jax.numpy as jnp
from jax import lax
from jax.experimental import pallas as pl
from jax.experimental.pallas import tpu as pltpu
from jax.sharding import PartitionSpec as P

SLICES = 8
AZIMUTH = 64
RADIAL, AXIAL = 96, 256
RADIAL_C, AXIAL_C = 48, 128
BLOCKS = 16
UNITS = 96
STEP = 0.1
HALF = 0.05
F32 = jnp.float32
BF16 = jnp.bfloat16


def azimuth_transform():
    points = np.arange(AZIMUTH)
    rows = np.zeros((2, UNITS, 3, AZIMUTH))
    scalars = np.zeros((128, 4))
    for k in range(64):
        angle = 2.0 * np.pi * k / AZIMUTH
        cos, sin = np.cos(angle * points) / 8.0, np.sin(angle * points) / 8.0
        rows[0, k, 0], rows[0, k, 1] = cos, sin
        rows[1, k, 1], rows[1, k, 0] = cos, -sin
        second = 2.0 * np.cos(angle) - 2.0
        scalars[k] = (second, second, 2.0 * np.sin(angle), -2.0)
    rows[0, 64, 2] = 1.0 / 8.0
    rows[1, 64, 2] = (-1.0) ** points / 8.0
    scalars[64] = (0.0, -4.0, 0.0, 0.0)
    for k in range(1, 32):
        angle = 2.0 * np.pi * k / AZIMUTH
        rows[0, 64 + k, 2] = np.sqrt(2.0) * np.cos(angle * points) / 8.0
        rows[1, 64 + k, 2] = -np.sqrt(2.0) * np.sin(angle * points) / 8.0
        second = 2.0 * np.cos(angle) - 2.0
        scalars[64 + k] = (second, second, 2.0 * np.sin(angle), 0.0)
    matrix = rows.reshape(192, 3, BLOCKS, 4).transpose(0, 2, 1, 3).reshape(192, 192)
    return matrix, scalars.astype(np.float32)


def split_constant(matrix):
    single = matrix.astype(np.float32)
    high = single.astype(ml_dtypes.bfloat16)
    low = (single - high.astype(np.float32)).astype(ml_dtypes.bfloat16)
    return np.concatenate([high, high, low], axis=1)


TRANSFORM, SCALARS = azimuth_transform()
TO_UNITS = split_constant(TRANSFORM)
FROM_UNITS = split_constant(TRANSFORM.T.copy())


def split(value):
    high = value.astype(BF16)
    return high, (value - high.astype(F32)).astype(BF16)


def dot(left, right):
    return jnp.dot(left, right, preferred_element_type=F32)


def axial(value, weights):
    high, low = split(value)
    return dot(jnp.concatenate([high, low, high], axis=1), weights)


def radial(weights, value):
    high, low = split(value)
    return dot(weights, jnp.concatenate([high, low, high], axis=0))


def gather_kernel(initial_ref, forcing_ref, send_ref, block_ref, sem):
    tm = lax.axis_index("tm")
    rows = pl.ds(pl.multiple_of((tm % 4) * 24, 8), 24)

    @pl.when(tm < 4)
    def _():
        copy = pltpu.make_async_copy(initial_ref.at[:, rows, :], block_ref, sem)
        copy.start()
        copy.wait()

    @pl.when(tm >= 4)
    def _():
        copy = pltpu.make_async_copy(forcing_ref.at[:, rows, :], block_ref, sem)
        copy.start()
        copy.wait()

    for plane in range(12):
        for piece in range(6):
            half, row = piece // 3, (piece % 3) * 8
            values = block_ref[plane, row : row + 8, half * 128 : half * 128 + 128]
            group, first = piece // 2, (piece % 2) * 8
            send_ref[pl.ds(first * 40 + plane * 3 + group, 8, stride=40), :] = values


def to_units_kernel(transform_ref, received_ref, send_ref):
    columns = [received_ref[pl.ds(group, 192, stride=3), :] for group in range(3)]
    send_ref[UNITS * 8 :, :] = jnp.zeros((32 * 8, 128), F32)
    zero = jnp.zeros((UNITS, 128), F32)
    send_ref[pl.ds(6, UNITS, stride=8), :] = zero
    send_ref[pl.ds(7, UNITS, stride=8), :] = zero
    for group in range(3):
        units = radial(transform_ref[...], columns[group])
        for part in range(2):
            send_ref[pl.ds(part * 3 + group, UNITS, stride=8), :] = units[part * UNITS : (part + 1) * UNITS]


def column_of(row, size):
    at = lax.broadcasted_iota(jnp.int32, (size, size), 0) == lax.broadcasted_iota(jnp.int32, (size, size), 1)
    return jnp.sum(jnp.where(at, row, 0.0), axis=1, keepdims=True)


def identity_plus(value):
    size = value.shape[0]
    at = lax.broadcasted_iota(jnp.int32, (size, size), 0) == lax.broadcasted_iota(jnp.int32, (size, size), 1)
    return jnp.where(at, 1.0, 0.0) + value


def axial_weights(value):
    high, low = split(jnp.transpose(identity_plus(value)))
    return jnp.concatenate([high, high, low], axis=0)


def radial_weights(value):
    high, low = split(value)
    return jnp.concatenate([high, high, low], axis=1)


def units_kernel(
    scalars_ref,
    received_ref,
    forward_radial_ref,
    backward_radial_ref,
    forward_axial_ref,
    backward_axial_ref,
    forward_radial_c_ref,
    backward_radial_c_ref,
    forward_axial_c_ref,
    backward_axial_c_ref,
    decay_radial_ref,
    decay_axial_ref,
    advection_ref,
    diffusion_ref,
    out_ref,
    bz_ref,
    fz_ref,
    br_ref,
    fr_ref,
    bz_narrow_ref,
    br_narrow_ref,
    fz_narrow_ref,
    fr_narrow_ref,
    bzc_ref,
    fzc_ref,
    brc_ref,
    frc_ref,
    cross_ref,
    first_ref,
    second_ref,
    cross_c_ref,
    first_c_ref,
    second_c_ref,
    spectrum_ref,
    inverse_ref,
    inverse_c_ref,
    field_ref,
    coarse_ref,
    push_ref,
    ahead_ref,
    behind_ref,
    known_ref,
    const_ref,
    gain_ref,
):
    unit = lax.axis_index("tm") * BLOCKS + lax.axis_index("azim")
    scalar = [scalars_ref[unit, n] for n in range(4)]

    bz_ref[...] = axial_weights(backward_axial_ref[...])
    fz_ref[...] = axial_weights(forward_axial_ref[...])
    br_ref[...] = radial_weights(identity_plus(backward_radial_ref[...]))
    fr_ref[...] = radial_weights(identity_plus(forward_radial_ref[...]))
    bzc_ref[...] = axial_weights(backward_axial_c_ref[...])
    fzc_ref[...] = axial_weights(forward_axial_c_ref[...])
    brc_ref[...] = radial_weights(identity_plus(backward_radial_c_ref[...]))
    frc_ref[...] = radial_weights(identity_plus(forward_radial_c_ref[...]))
    for n in range(3):
        bz_narrow_ref[n * 128 : n * 128 + 128, :] = bz_ref[n * 256 : n * 256 + 128, :]
    fz_narrow_ref[...] = fz_ref[:, :128]
    fr_narrow_ref[...] = fr_ref[:48, :]
    br_narrow_ref[...] = radial_weights(identity_plus(backward_radial_ref[...])[:, :48])

    diffusion = column_of(diffusion_ref[...], RADIAL)
    cross_ref[...] = scalar[2] * advection_ref[...] + scalar[3]
    first_ref[...] = jnp.broadcast_to(scalar[0] * diffusion, (RADIAL, AXIAL))
    second_ref[...] = jnp.broadcast_to(scalar[1] * diffusion, (RADIAL, AXIAL))
    pick_lane = jnp.where(
        lax.broadcasted_iota(jnp.int32, (AXIAL, AXIAL_C), 0)
        == 2 * lax.broadcasted_iota(jnp.int32, (AXIAL, AXIAL_C), 1),
        1.0,
        0.0,
    )
    pick_row = jnp.where(
        lax.broadcasted_iota(jnp.int32, (RADIAL_C, RADIAL), 1)
        == 2 * lax.broadcasted_iota(jnp.int32, (RADIAL_C, RADIAL), 0),
        1.0,
        0.0,
    )
    exact = lax.Precision.HIGHEST
    advection_c = jnp.dot(
        jnp.dot(pick_row, advection_ref[...], precision=exact, preferred_element_type=F32),
        pick_lane,
        precision=exact,
        preferred_element_type=F32,
    )
    diffusion_c = jnp.sum(pick_row * diffusion_ref[...], axis=1, keepdims=True)
    cross_c_ref[...] = scalar[2] * advection_c + scalar[3]
    first_c_ref[...] = jnp.broadcast_to(scalar[0] * diffusion_c, (RADIAL_C, AXIAL_C))
    second_c_ref[...] = jnp.broadcast_to(scalar[1] * diffusion_c, (RADIAL_C, AXIAL_C))
    spectrum = -(column_of(decay_radial_ref[...], RADIAL) + decay_axial_ref[...])
    spectrum_ref[...] = spectrum
    inverse_ref[...] = 1.0 / (1.0 - HALF * spectrum)
    inverse_c_ref[...] = 1.0 / (1.0 - STEP * spectrum[:RADIAL_C, :AXIAL_C])

    for field in range(2):
        for part in range(2):
            for rows in range(4):
                source = (field * 4 + rows) * 16 * 8 + part * 3
                for piece in range(6):
                    half, row = piece // 3, (piece % 3) * 8
                    group, first = piece // 2, (piece % 2) * 8
                    field_ref[field, part, rows * 24 + row : rows * 24 + row + 8, half * 128 : half * 128 + 128] = (
                        received_ref[pl.ds(source + first * 8 + group, 8, stride=8), :]
                    )

    def forces(re, im, cross, first, second):
        return first * re - cross * im, second * im + cross * re

    def to_points(modes):
        inner = axial(modes.reshape(2 * RADIAL, AXIAL), bz_ref[...])
        return radial(br_ref[...], inner[:RADIAL]), radial(br_ref[...], inner[RADIAL:])

    def fine_forces(re, im):
        return forces(re, im, cross_ref[...], first_ref[...], second_ref[...])

    def to_modes(re, im):
        inner = axial(jnp.concatenate([re, im], axis=0), fz_ref[...])
        return jnp.stack([radial(fr_ref[...], inner[:RADIAL]), radial(fr_ref[...], inner[RADIAL:])])

    def explicit(modes):
        return to_modes(*fine_forces(*to_points(modes)))

    def explicit_of_coarse(modes):
        inner = axial(modes.reshape(2 * RADIAL_C, AXIAL_C), bz_narrow_ref[...])
        re, im = radial(br_narrow_ref[...], inner[:RADIAL_C]), radial(br_narrow_ref[...], inner[RADIAL_C:])
        return to_modes(*fine_forces(re, im))

    def restricted_explicit(modes):
        re, im = fine_forces(*to_points(modes))
        inner = jnp.concatenate([radial(fr_narrow_ref[...], re), radial(fr_narrow_ref[...], im)], axis=0)
        return axial(inner, fz_narrow_ref[...]).reshape(2, RADIAL_C, AXIAL_C)

    def coarse_explicit(modes):
        inner = axial(modes.reshape(2 * RADIAL_C, AXIAL_C), bzc_ref[...])
        both = radial(brc_ref[...], jnp.concatenate([inner[:RADIAL_C], inner[RADIAL_C:]], axis=1))
        re, im = forces(
            both[:, :AXIAL_C], both[:, AXIAL_C:], cross_c_ref[...], first_c_ref[...], second_c_ref[...]
        )
        both = radial(frc_ref[...], jnp.concatenate([re, im], axis=1))
        inner = jnp.concatenate([both[:, :AXIAL_C], both[:, AXIAL_C:]], axis=0)
        return axial(inner, fzc_ref[...]).reshape(2, RADIAL_C, AXIAL_C)

    def corner(value):
        return value[:, :RADIAL_C, :AXIAL_C]

    known_ref[0] = explicit(field_ref[0])
    spectrum = spectrum_ref[...]
    total0 = known_ref[0] + field_ref[1] + spectrum * field_ref[0]
    known_ref[3] = inverse_ref[...] * (field_ref[0] - HALF * spectrum * field_ref[0] + (0.5 * STEP) * total0)
    known_ref[1] = explicit(known_ref[3])
    known_ref[4] = inverse_ref[...] * (
        known_ref[3]
        + HALF * (known_ref[1] - known_ref[0])
        - HALF * spectrum_ref[...] * field_ref[0]
        + (0.5 * STEP) * (known_ref[0] + field_ref[1] + spectrum_ref[...] * field_ref[0])
    )
    known_ref[2] = explicit(known_ref[4])
    spectrum_c = spectrum_ref[:RADIAL_C, :AXIAL_C]
    coarse_known = [known_ref[n, :, :RADIAL_C, :AXIAL_C] for n in range(5)]
    start_c = field_ref[0, :, :RADIAL_C, :AXIAL_C]
    forcing_c = field_ref[1, :, :RADIAL_C, :AXIAL_C]
    gain_ref[0] = (
        STEP
        * (
            (coarse_known[0] + spectrum_c * start_c) / 6.0
            + (2.0 / 3.0) * (coarse_known[1] + spectrum_c * coarse_known[3])
            + (coarse_known[2] + spectrum_c * coarse_known[4]) / 6.0
            + forcing_c
        )
        - STEP * spectrum_c * coarse_known[4]
    )
    coarse_ref[0] = start_c
    coarse_ref[9] = coarse_known[4]
    coarse_ref[1] = inverse_c_ref[...] * (gain_ref[0] + start_c)

    def chain(n, carry):
        latest = coarse_ref[n]
        coarse_ref[n + 1] = inverse_c_ref[...] * (
            gain_ref[0] + latest + STEP * coarse_explicit(latest - coarse_ref[0])
        )
        return carry

    lax.fori_loop(1, SLICES, chain, 0)

    def spread(n, carry):
        state = coarse_ref[n]
        push = explicit_of_coarse(state)
        push_ref[n] = push[:, :RADIAL_C, :AXIAL_C]
        behind_ref[n] = (0.25 * HALF) * push
        ahead_ref[n] = (0.75 * HALF) * push
        damped = (0.25 * HALF) * spectrum_ref[:RADIAL_C, :AXIAL_C] * state
        behind_ref[n, :, :RADIAL_C, :AXIAL_C] = behind_ref[n, :, :RADIAL_C, :AXIAL_C] - damped
        ahead_ref[n, :, :RADIAL_C, :AXIAL_C] = ahead_ref[n, :, :RADIAL_C, :AXIAL_C] + damped + state
        return carry

    lax.fori_loop(0, SLICES + 2, spread, 0)

    def padded(value):
        return jnp.pad(value, ((0, 0), (0, RADIAL - RADIAL_C), (0, AXIAL - AXIAL_C)))

    spectrum = spectrum_ref[...]
    wide_start = padded(coarse_ref[0])
    wide_end = padded(coarse_ref[9])
    push_start = (ahead_ref[0] + behind_ref[0] - wide_start) * (1.0 / HALF)
    push_end = (ahead_ref[9] + behind_ref[9] - wide_end) * (1.0 / HALF)
    rhs_start = push_start + spectrum * wide_start
    rhs_end = push_end + spectrum * wide_end
    total0 = known_ref[0] + field_ref[1] + spectrum * field_ref[0]
    total1 = known_ref[1] + field_ref[1] + spectrum * known_ref[3]
    total2 = known_ref[2] + field_ref[1] + spectrum * known_ref[4]
    shared = -HALF * spectrum * (known_ref[3] - 0.5 * (wide_start + wide_end)) + STEP * (
        (5.0 / 24.0) * total0 + (1.0 / 3.0) * total1 - (1.0 / 24.0) * total2 - 0.375 * rhs_start - 0.125 * rhs_end
    )
    const_ref[0] = field_ref[0] - wide_start + shared
    const_ref[1] = known_ref[4] - wide_end + HALF * (known_ref[2] - push_end - known_ref[0] + push_start) + shared
    const_ref[2] = (
        -HALF * (known_ref[1] - 0.5 * (push_start + push_end))
        - HALF * spectrum * (known_ref[4] - wide_end)
        + STEP
        * (
            (-1.0 / 24.0) * total0
            + (1.0 / 3.0) * total1
            + (5.0 / 24.0) * total2
            - 0.125 * rhs_start
            - 0.375 * rhs_end
        )
    )
    gain_ref[8] = STEP * (forcing_c + (coarse_known[0] - push_ref[0]) / 6.0)
    gain_ref[9] = STEP * (forcing_c + (coarse_known[2] - push_ref[9]) / 6.0)

    def sweep(n, carry):
        later = jnp.minimum(n, 1)
        middle = inverse_ref[...] * (const_ref[later] + ahead_ref[n] + behind_ref[n + 1])
        middle_push = explicit(middle)
        ending = inverse_ref[...] * (middle + HALF * middle_push + const_ref[2] + behind_ref[n + 1] - behind_ref[n])
        ending_push = restricted_explicit(ending)
        spectrum_c = spectrum_ref[:RADIAL_C, :AXIAL_C]
        gain_ref[n] = (
            gain_ref[8 + later]
            + (STEP / 6.0) * (push_ref[n] + spectrum_c * coarse_ref[n])
            + (STEP * 2.0 / 3.0) * (corner(middle_push) + spectrum_c * corner(middle))
            + (STEP / 6.0) * ending_push
            - (STEP * 5.0 / 6.0) * spectrum_c * corner(ending)
        )
        for part in range(2):
            for half in range(2):
                for j in range(0 if half else 3, 6):
                    out_ref[n, pl.ds(part * 12 + half * 6 + j, 16, stride=24), :] = ending[
                        part, 16 * j : 16 * j + 16, half * 128 : half * 128 + 128
                    ]
        return carry

    lax.fori_loop(0, SLICES, sweep, 0)

    def place(n, state):
        for part in range(2):
            for j in range(3):
                out_ref[n, pl.ds(part * 12 + j, 16, stride=24), :] = state[part, 16 * j : 16 * j + 16, :]

    state = inverse_c_ref[...] * (gain_ref[0] + coarse_ref[0])
    place(0, state)

    def chain_again(n, state):
        after = inverse_c_ref[...] * (gain_ref[n] + state + STEP * coarse_explicit(state - coarse_ref[n]))
        place(n, after)
        return after

    lax.fori_loop(1, SLICES, chain_again, state)


def from_units_kernel(transform_ref, received_ref, send_ref):
    for pair in range(6):
        parts = []
        for part in range(2):
            parts.append(
                jnp.concatenate(
                    [received_ref[pl.ds(part * 12 + 2 * pair + n, UNITS, stride=24), :] for n in range(2)], axis=1
                )
            )
        planes = radial(transform_ref[...], jnp.concatenate(parts, axis=0))
        for n in range(2):
            send_ref[pl.ds(2 * pair + n, 192, stride=12), :] = planes[:, n * 128 : n * 128 + 128]


def place_kernel(received_ref, out_ref):
    for plane in range(12):
        for half in range(2):
            for j in range(6):
                out_ref[plane, 16 * j : 16 * j + 16, half * 128 : half * 128 + 128] = received_ref[
                    pl.ds(plane * 12 + half * 6 + j, 16, stride=144), :
                ]


VMEM = pl.BlockSpec(memory_space=pltpu.VMEM)
ANY = pl.BlockSpec(memory_space=pl.ANY)
SMEM = pl.BlockSpec(memory_space=pltpu.SMEM)
PARAMS = pltpu.CompilerParams(vmem_limit_bytes=48 << 20)


def array(*shape):
    return jax.ShapeDtypeStruct(shape, F32)


def exchange(value, axes, peers):
    rows = value.shape[0] // peers
    moved = lax.all_to_all(value.reshape(peers, rows, 128), axes, 0, 0)
    return moved.reshape(value.shape)


def per_device(
    initial_state,
    forcing,
    forward_radial,
    backward_radial,
    forward_axial,
    backward_axial,
    forward_radial_coarse,
    backward_radial_coarse,
    forward_axial_coarse,
    backward_axial_coarse,
    decay_radial,
    decay_axial,
    advection,
    diffusion,
):
    send = pl.pallas_call(
        gather_kernel,
        out_shape=array(BLOCKS * 40, 128),
        in_specs=[ANY, ANY],
        out_specs=VMEM,
        scratch_shapes=[pltpu.VMEM((12, 24, AXIAL), F32), pltpu.SemaphoreType.DMA],
        compiler_params=PARAMS,
        name="gather_points",
    )(initial_state.reshape(12, RADIAL, AXIAL), forcing.reshape(12, RADIAL, AXIAL))
    received = exchange(send, "azim", BLOCKS)
    received = received.reshape(BLOCKS, 40, 128)[:, :36].reshape(BLOCKS * 36, 128)
    send = pl.pallas_call(
        to_units_kernel,
        out_shape=array(128 * 8, 128),
        in_specs=[VMEM, VMEM],
        out_specs=VMEM,
        compiler_params=PARAMS,
        name="to_units",
    )(jnp.asarray(TO_UNITS), received)
    received = exchange(send, ("tm", "azim"), 128)

    def wide(rows, columns):
        return pltpu.VMEM((rows, columns), BF16)

    fine, coarse = (2, RADIAL, AXIAL), (2, RADIAL_C, AXIAL_C)
    send = pl.pallas_call(
        units_kernel,
        out_shape=array(SLICES, 16 * 24, 128),
        in_specs=[SMEM] + [VMEM] * 13,
        out_specs=VMEM,
        scratch_shapes=[
            wide(3 * AXIAL, AXIAL),
            wide(3 * AXIAL, AXIAL),
            wide(RADIAL, 3 * RADIAL),
            wide(RADIAL, 3 * RADIAL),
            wide(3 * AXIAL_C, AXIAL),
            wide(RADIAL, 3 * RADIAL_C),
            wide(3 * AXIAL, AXIAL_C),
            wide(RADIAL_C, 3 * RADIAL),
            wide(3 * AXIAL_C, AXIAL_C),
            wide(3 * AXIAL_C, AXIAL_C),
            wide(RADIAL_C, 3 * RADIAL_C),
            wide(RADIAL_C, 3 * RADIAL_C),
        ]
        + [pltpu.VMEM((RADIAL, AXIAL), F32)] * 3
        + [pltpu.VMEM((RADIAL_C, AXIAL_C), F32)] * 3
        + [
            pltpu.VMEM((RADIAL, AXIAL), F32),
            pltpu.VMEM((RADIAL, AXIAL), F32),
            pltpu.VMEM((RADIAL_C, AXIAL_C), F32),
            pltpu.VMEM((2,) + fine, F32),
            pltpu.VMEM((10,) + coarse, F32),
            pltpu.VMEM((10,) + coarse, F32),
            pltpu.VMEM((10,) + fine, F32),
            pltpu.VMEM((10,) + fine, F32),
            pltpu.VMEM((5,) + fine, F32),
            pltpu.VMEM((3,) + fine, F32),
            pltpu.VMEM((10,) + coarse, F32),
        ],
        compiler_params=PARAMS,
        name="units",
    )(
        jnp.asarray(SCALARS),
        received,
        forward_radial,
        backward_radial,
        forward_axial,
        backward_axial,
        forward_radial_coarse,
        backward_radial_coarse,
        forward_axial_coarse,
        backward_axial_coarse,
        decay_radial.reshape(1, RADIAL),
        decay_axial.reshape(1, AXIAL),
        advection,
        diffusion.reshape(1, RADIAL),
    )
    received = exchange(send.reshape(128 * 24, 128), ("tm", "azim"), 128)
    send = pl.pallas_call(
        from_units_kernel,
        out_shape=array(BLOCKS * 144, 128),
        in_specs=[VMEM, VMEM],
        out_specs=VMEM,
        compiler_params=PARAMS,
        name="from_units",
    )(jnp.asarray(FROM_UNITS), received)
    received = exchange(send, "azim", BLOCKS)
    planes = pl.pallas_call(
        place_kernel,
        out_shape=array(12, RADIAL, AXIAL),
        in_specs=[VMEM],
        out_specs=VMEM,
        compiler_params=PARAMS,
        name="place",
    )(received)
    return planes.reshape(1, 3, 4, RADIAL, AXIAL)


def solution(mesh):
    split_planes = P(None, "azim", None, None)
    return jax.shard_map(
        per_device,
        mesh=mesh,
        in_specs=(split_planes, split_planes) + (P(),) * 12,
        out_specs=P("tm", None, "azim", None, None),
        check_vma=False,
    )
```

```python
import ml_dtypes
import numpy as np
import jax
import jax.numpy as jnp
from jax import lax
from jax.experimental import pallas as pl
from jax.experimental.pallas import tpu as pltpu
from jax.sharding import PartitionSpec as P

SLICES = 8
AZIMUTH = 64
RADIAL, AXIAL = 96, 256
RADIAL_C, AXIAL_C = 48, 128
BLOCKS = 16
UNITS = 96
STEP = 0.1
HALF = 0.05
F32 = jnp.float32
BF16 = jnp.bfloat16


def azimuth_transform():
    points = np.arange(AZIMUTH)
    rows = np.zeros((2, UNITS, 3, AZIMUTH))
    scalars = np.zeros((128, 4))
    for k in range(64):
        angle = 2.0 * np.pi * k / AZIMUTH
        cos, sin = np.cos(angle * points) / 8.0, np.sin(angle * points) / 8.0
        rows[0, k, 0], rows[0, k, 1] = cos, sin
        rows[1, k, 1], rows[1, k, 0] = cos, -sin
        second = 2.0 * np.cos(angle) - 2.0
        scalars[k] = (second, second, 2.0 * np.sin(angle), -2.0)
    rows[0, 64, 2] = 1.0 / 8.0
    rows[1, 64, 2] = (-1.0) ** points / 8.0
    scalars[64] = (0.0, -4.0, 0.0, 0.0)
    for k in range(1, 32):
        angle = 2.0 * np.pi * k / AZIMUTH
        rows[0, 64 + k, 2] = np.sqrt(2.0) * np.cos(angle * points) / 8.0
        rows[1, 64 + k, 2] = -np.sqrt(2.0) * np.sin(angle * points) / 8.0
        second = 2.0 * np.cos(angle) - 2.0
        scalars[64 + k] = (second, second, 2.0 * np.sin(angle), 0.0)
    matrix = rows.reshape(192, 3, BLOCKS, 4).transpose(0, 2, 1, 3).reshape(192, 192)
    return matrix, scalars.astype(np.float32)


def split_constant(matrix):
    single = matrix.astype(np.float32)
    high = single.astype(ml_dtypes.bfloat16)
    low = (single - high.astype(np.float32)).astype(ml_dtypes.bfloat16)
    return np.concatenate([high, high, low], axis=1)


TRANSFORM, SCALARS = azimuth_transform()
TO_UNITS = split_constant(TRANSFORM)
FROM_UNITS = split_constant(TRANSFORM.T.copy())


def split(value):
    high = value.astype(BF16)
    return high, (value - high.astype(F32)).astype(BF16)


def dot(left, right):
    return jnp.dot(left, right, preferred_element_type=F32)


def axial(value, weights):
    high, low = split(value)
    return dot(jnp.concatenate([high, low, high], axis=1), weights)


def radial(weights, value):
    high, low = split(value)
    return dot(weights, jnp.concatenate([high, low, high], axis=0))


def gather_kernel(initial_ref, forcing_ref, send_ref, block_ref, sem):
    tm = lax.axis_index("tm")
    rows = pl.ds(pl.multiple_of((tm % 4) * 24, 8), 24)

    @pl.when(tm < 4)
    def _():
        copy = pltpu.make_async_copy(initial_ref.at[:, rows, :], block_ref, sem)
        copy.start()
        copy.wait()

    @pl.when(tm >= 4)
    def _():
        copy = pltpu.make_async_copy(forcing_ref.at[:, rows, :], block_ref, sem)
        copy.start()
        copy.wait()

    for plane in range(12):
        for piece in range(6):
            half, row = piece // 3, (piece % 3) * 8
            values = block_ref[plane, row : row + 8, half * 128 : half * 128 + 128]
            group, first = piece // 2, (piece % 2) * 8
            send_ref[pl.ds(first * 40 + plane * 3 + group, 8, stride=40), :] = values


def to_units_kernel(transform_ref, received_ref, send_ref):
    columns = [received_ref[pl.ds(group, 192, stride=3), :] for group in range(3)]
    send_ref[UNITS * 8 :, :] = jnp.zeros((32 * 8, 128), F32)
    zero = jnp.zeros((UNITS, 128), F32)
    send_ref[pl.ds(6, UNITS, stride=8), :] = zero
    send_ref[pl.ds(7, UNITS, stride=8), :] = zero
    for group in range(3):
        units = radial(transform_ref[...], columns[group])
        for part in range(2):
            send_ref[pl.ds(part * 3 + group, UNITS, stride=8), :] = units[part * UNITS : (part + 1) * UNITS]


def column_of(row, size):
    at = lax.broadcasted_iota(jnp.int32, (size, size), 0) == lax.broadcasted_iota(jnp.int32, (size, size), 1)
    return jnp.sum(jnp.where(at, row, 0.0), axis=1, keepdims=True)


def identity_plus(value):
    size = value.shape[0]
    at = lax.broadcasted_iota(jnp.int32, (size, size), 0) == lax.broadcasted_iota(jnp.int32, (size, size), 1)
    return jnp.where(at, 1.0, 0.0) + value


def axial_weights(value):
    high, low = split(jnp.transpose(identity_plus(value)))
    return jnp.concatenate([high, high, low], axis=0)


def radial_weights(value):
    high, low = split(value)
    return jnp.concatenate([high, high, low], axis=1)


OPERATORS = (
    ("axial", (6 * AXIAL, AXIAL), BF16),
    ("radial", (2 * RADIAL, 3 * RADIAL), BF16),
    ("axial_c", (6 * AXIAL_C, AXIAL_C), BF16),
    ("radial_c", (RADIAL + 2 * RADIAL_C, 3 * RADIAL_C), BF16),
    ("point", (5 * RADIAL, AXIAL), F32),
    ("point_c", (4 * RADIAL_C, AXIAL_C), F32),
)


def views(axial_ref, radial_ref, axial_c_ref, radial_c_ref, point_ref, point_c_ref):
    def parts(ref, *sizes):
        ends = np.cumsum(sizes)
        return [ref.at[int(end - size) : int(end), :] for size, end in zip(sizes, ends)]

    return (
        parts(axial_ref, *[3 * AXIAL] * 2)
        + parts(radial_ref, *[RADIAL] * 2)
        + parts(axial_c_ref, *[3 * AXIAL_C] * 2)
        + parts(radial_c_ref, RADIAL, RADIAL_C, RADIAL_C)
        + parts(point_ref, *[RADIAL] * 5)
        + parts(point_c_ref, *[RADIAL_C] * 4)
    )


def operators_kernel(
    scalars_ref,
    forward_radial_ref,
    backward_radial_ref,
    forward_axial_ref,
    backward_axial_ref,
    forward_radial_c_ref,
    backward_radial_c_ref,
    forward_axial_c_ref,
    backward_axial_c_ref,
    decay_radial_ref,
    decay_axial_ref,
    advection_ref,
    diffusion_ref,
    *operator_refs,
):
    all_views = views(*operator_refs)
    (bz_ref, fz_ref, br_ref, fr_ref, bzc_ref, fzc_ref, br_narrow_ref, brc_ref, frc_ref) = all_views[:9]
    (cross_ref, first_ref, second_ref, spectrum_ref, inverse_ref) = all_views[9:14]
    (cross_c_ref, first_c_ref, second_c_ref, inverse_c_ref) = all_views[14:]
    unit = lax.axis_index("tm") * BLOCKS + lax.axis_index("azim")
    scalar = [scalars_ref[unit, n] for n in range(4)]

    bz_ref[...] = axial_weights(backward_axial_ref[...])
    fz_ref[...] = axial_weights(forward_axial_ref[...])
    br_ref[...] = radial_weights(identity_plus(backward_radial_ref[...]))
    fr_ref[...] = radial_weights(identity_plus(forward_radial_ref[...]))
    bzc_ref[...] = axial_weights(backward_axial_c_ref[...])
    fzc_ref[...] = axial_weights(forward_axial_c_ref[...])
    brc_ref[...] = radial_weights(identity_plus(backward_radial_c_ref[...]))
    frc_ref[...] = radial_weights(identity_plus(forward_radial_c_ref[...]))
    br_narrow_ref[...] = radial_weights(identity_plus(backward_radial_ref[...])[:, :48])

    diffusion = column_of(diffusion_ref[...], RADIAL)
    cross_ref[...] = scalar[2] * advection_ref[...] + scalar[3]
    first_ref[...] = jnp.broadcast_to(scalar[0] * diffusion, (RADIAL, AXIAL))
    second_ref[...] = jnp.broadcast_to(scalar[1] * diffusion, (RADIAL, AXIAL))
    pick_lane = jnp.where(
        lax.broadcasted_iota(jnp.int32, (AXIAL, AXIAL_C), 0)
        == 2 * lax.broadcasted_iota(jnp.int32, (AXIAL, AXIAL_C), 1),
        1.0,
        0.0,
    )
    pick_row = jnp.where(
        lax.broadcasted_iota(jnp.int32, (RADIAL_C, RADIAL), 1)
        == 2 * lax.broadcasted_iota(jnp.int32, (RADIAL_C, RADIAL), 0),
        1.0,
        0.0,
    )
    exact = lax.Precision.HIGHEST
    advection_c = jnp.dot(
        jnp.dot(pick_row, advection_ref[...], precision=exact, preferred_element_type=F32),
        pick_lane,
        precision=exact,
        preferred_element_type=F32,
    )
    diffusion_c = jnp.sum(pick_row * diffusion_ref[...], axis=1, keepdims=True)
    cross_c_ref[...] = scalar[2] * advection_c + scalar[3]
    first_c_ref[...] = jnp.broadcast_to(scalar[0] * diffusion_c, (RADIAL_C, AXIAL_C))
    second_c_ref[...] = jnp.broadcast_to(scalar[1] * diffusion_c, (RADIAL_C, AXIAL_C))
    spectrum = -(column_of(decay_radial_ref[...], RADIAL) + decay_axial_ref[...])
    spectrum_ref[...] = spectrum
    inverse_ref[...] = 1.0 / (1.0 - HALF * spectrum)
    inverse_c_ref[...] = 1.0 / (1.0 - STEP * spectrum[:RADIAL_C, :AXIAL_C])


def units_kernel(
    received_ref,
    axial_ref,
    radial_ref,
    axial_c_ref,
    radial_c_ref,
    point_ref,
    point_c_ref,
    out_ref,
    field_ref,
    coarse_ref,
    push_ref,
    ahead_ref,
    behind_ref,
    known_ref,
    const_ref,
    gain_ref,
    state_ref,
):
    all_views = views(axial_ref, radial_ref, axial_c_ref, radial_c_ref, point_ref, point_c_ref)
    (bz_ref, fz_ref, br_ref, fr_ref, bzc_ref, fzc_ref, br_narrow_ref, brc_ref, frc_ref) = all_views[:9]
    (cross_ref, first_ref, second_ref, spectrum_ref, inverse_ref) = all_views[9:14]
    (cross_c_ref, first_c_ref, second_c_ref, inverse_c_ref) = all_views[14:]

    for field in range(2):
        for part in range(2):
            for rows in range(4):
                source = (field * 4 + rows) * 16 * 8 + part * 3
                for piece in range(6):
                    half, row = piece // 3, (piece % 3) * 8
                    group, first = piece // 2, (piece % 2) * 8
                    field_ref[field, part, rows * 24 + row : rows * 24 + row + 8, half * 128 : half * 128 + 128] = (
                        received_ref[pl.ds(source + first * 8 + group, 8, stride=8), :]
                    )

    def forces(re, im, cross, first, second):
        return first * re - cross * im, second * im + cross * re

    def radial_each(weights, rows, size):
        return [radial(weights, rows[n * size : n * size + size]) for n in range(rows.shape[0] // size)]

    def fine_forces(planes):
        moved = []
        for n in range(0, len(planes), 2):
            moved += forces(planes[n], planes[n + 1], cross_ref[...], first_ref[...], second_ref[...])
        return moved

    def flat(states):
        return jnp.concatenate([state.reshape(-1, state.shape[-1]) for state in states], axis=0)

    def pairs(planes):
        return [jnp.stack(planes[n : n + 2]) for n in range(0, len(planes), 2)]

    def to_points(states):
        return radial_each(br_ref[...], axial(flat(states), bz_ref[...]), RADIAL)

    def to_modes(planes):
        inner = axial(jnp.concatenate(planes, axis=0), fz_ref[...])
        return pairs(radial_each(fr_ref[...], inner, RADIAL))

    def explicit(states):
        return to_modes(fine_forces(to_points(states)))

    def explicit_of_coarse(states):
        narrow = jnp.concatenate([bz_ref[n * AXIAL : n * AXIAL + AXIAL_C, :] for n in range(3)], axis=0)
        inner = axial(flat(states), narrow)
        return to_modes(fine_forces(radial_each(br_narrow_ref[...], inner, RADIAL_C)))

    def restricted_explicit(states):
        planes = fine_forces(to_points(states))
        planes = [radial(fr_ref[:RADIAL_C, :], plane) for plane in planes]
        inner = axial(jnp.concatenate(planes, axis=0), fz_ref[:, :AXIAL_C])
        return pairs([inner[n * RADIAL_C : (n + 1) * RADIAL_C] for n in range(len(planes))])

    def coarse_explicit(modes):
        inner = axial(modes.reshape(2 * RADIAL_C, AXIAL_C), bzc_ref[...])
        both = radial(brc_ref[...], jnp.concatenate([inner[:RADIAL_C], inner[RADIAL_C:]], axis=1))
        re, im = forces(
            both[:, :AXIAL_C], both[:, AXIAL_C:], cross_c_ref[...], first_c_ref[...], second_c_ref[...]
        )
        both = radial(frc_ref[...], jnp.concatenate([re, im], axis=1))
        inner = jnp.concatenate([both[:, :AXIAL_C], both[:, AXIAL_C:]], axis=0)
        return axial(inner, fzc_ref[...]).reshape(2, RADIAL_C, AXIAL_C)

    def corner(value):
        return value[:, :RADIAL_C, :AXIAL_C]

    known_ref[0] = explicit([field_ref[0]])[0]
    spectrum = spectrum_ref[...]
    total0 = known_ref[0] + field_ref[1] + spectrum * field_ref[0]
    known_ref[3] = inverse_ref[...] * (field_ref[0] - HALF * spectrum * field_ref[0] + (0.5 * STEP) * total0)
    known_ref[1] = explicit([known_ref[3]])[0]
    known_ref[4] = inverse_ref[...] * (
        known_ref[3]
        + HALF * (known_ref[1] - known_ref[0])
        - HALF * spectrum_ref[...] * field_ref[0]
        + (0.5 * STEP) * (known_ref[0] + field_ref[1] + spectrum_ref[...] * field_ref[0])
    )
    known_ref[2] = explicit([known_ref[4]])[0]
    spectrum_c = spectrum_ref[:RADIAL_C, :AXIAL_C]
    coarse_known = [known_ref[n, :, :RADIAL_C, :AXIAL_C] for n in range(5)]
    start_c = field_ref[0, :, :RADIAL_C, :AXIAL_C]
    forcing_c = field_ref[1, :, :RADIAL_C, :AXIAL_C]
    gain_ref[0] = (
        STEP
        * (
            (coarse_known[0] + spectrum_c * start_c) / 6.0
            + (2.0 / 3.0) * (coarse_known[1] + spectrum_c * coarse_known[3])
            + (coarse_known[2] + spectrum_c * coarse_known[4]) / 6.0
            + forcing_c
        )
        - STEP * spectrum_c * coarse_known[4]
    )
    coarse_ref[0] = start_c
    coarse_ref[9] = coarse_known[4]
    coarse_ref[1] = inverse_c_ref[...] * (gain_ref[0] + start_c)

    def chain(latest):
        return inverse_c_ref[...] * (
            gain_ref[0] + latest + STEP * coarse_explicit(latest - coarse_ref[0])
        )

    def spread(places):
        states = [coarse_ref[n] for n in places]
        pushes = explicit_of_coarse(states)
        damping = (0.25 * HALF) * spectrum_ref[:RADIAL_C, :AXIAL_C]
        for n, state, push in zip(places, states, pushes):
            push_ref[n] = corner(push)
            behind_ref[n] = (0.25 * HALF) * push
            ahead_ref[n] = (0.75 * HALF) * push
            damped = damping * state
            behind_ref[n, :, :RADIAL_C, :AXIAL_C] = (0.25 * HALF) * corner(push) - damped
            ahead_ref[n, :, :RADIAL_C, :AXIAL_C] = (0.75 * HALF) * corner(push) + damped + state

    def chain_and_spread(n, carry):
        at = 2 * n
        after = chain(coarse_ref[at + 1])
        last = chain(after)
        spread([at, at + 1])
        coarse_ref[at + 2] = after
        coarse_ref[at + 3] = last
        return carry

    lax.fori_loop(0, 3, chain_and_spread, 0)
    last = chain(coarse_ref[7])
    spread([6, 7, 9])
    coarse_ref[8] = last
    spread([8])

    def padded(value):
        return jnp.pad(value, ((0, 0), (0, RADIAL - RADIAL_C), (0, AXIAL - AXIAL_C)))

    spectrum = spectrum_ref[...]
    wide_start = padded(coarse_ref[0])
    wide_end = padded(coarse_ref[9])
    push_start = (ahead_ref[0] + behind_ref[0] - wide_start) * (1.0 / HALF)
    push_end = (ahead_ref[9] + behind_ref[9] - wide_end) * (1.0 / HALF)
    rhs_start = push_start + spectrum * wide_start
    rhs_end = push_end + spectrum * wide_end
    total0 = known_ref[0] + field_ref[1] + spectrum * field_ref[0]
    total1 = known_ref[1] + field_ref[1] + spectrum * known_ref[3]
    total2 = known_ref[2] + field_ref[1] + spectrum * known_ref[4]
    shared = -HALF * spectrum * (known_ref[3] - 0.5 * (wide_start + wide_end)) + STEP * (
        (5.0 / 24.0) * total0 + (1.0 / 3.0) * total1 - (1.0 / 24.0) * total2 - 0.375 * rhs_start - 0.125 * rhs_end
    )
    const_ref[0] = field_ref[0] - wide_start + shared
    const_ref[1] = known_ref[4] - wide_end + HALF * (known_ref[2] - push_end - known_ref[0] + push_start) + shared
    const_ref[2] = (
        -HALF * (known_ref[1] - 0.5 * (push_start + push_end))
        - HALF * spectrum * (known_ref[4] - wide_end)
        + STEP
        * (
            (-1.0 / 24.0) * total0
            + (1.0 / 3.0) * total1
            + (5.0 / 24.0) * total2
            - 0.125 * rhs_start
            - 0.375 * rhs_end
        )
    )
    gain_ref[8] = STEP * (forcing_c + (coarse_known[0] - push_ref[0]) / 6.0)
    gain_ref[9] = STEP * (forcing_c + (coarse_known[2] - push_ref[9]) / 6.0)

    def sweep(places, kinds):
        middles = [
            inverse_ref[...] * (const_ref[kind] + ahead_ref[n] + behind_ref[n + 1])
            for n, kind in zip(places, kinds)
        ]
        middle_pushes = explicit(middles)
        endings = [
            inverse_ref[...] * (middle + HALF * push + const_ref[2] + behind_ref[n + 1] - behind_ref[n])
            for n, middle, push in zip(places, middles, middle_pushes)
        ]
        ending_pushes = restricted_explicit(endings)
        spectrum_c = spectrum_ref[:RADIAL_C, :AXIAL_C]
        for at, n in enumerate(places):
            middle, ending = middles[at], endings[at]
            gain_ref[n] = (
                gain_ref[8 + kinds[at]]
                + (STEP / 6.0) * (push_ref[n] + spectrum_c * coarse_ref[n])
                + (STEP * 2.0 / 3.0) * (corner(middle_pushes[at]) + spectrum_c * corner(middle))
                + (STEP / 6.0) * ending_pushes[at]
                - (STEP * 5.0 / 6.0) * spectrum_c * corner(ending)
            )
            for part in range(2):
                for half in range(2):
                    for j in range(0 if half else 3, 6):
                        out_ref[n, pl.ds(part * 12 + half * 6 + j, 16, stride=24), :] = ending[
                            part, 16 * j : 16 * j + 16, half * 128 : half * 128 + 128
                        ]

    def chain_again(n, state):
        after = inverse_c_ref[...] * (gain_ref[n] + state + STEP * coarse_explicit(state - coarse_ref[n]))
        for part in range(2):
            for j in range(3):
                out_ref[n, pl.ds(part * 12 + j, 16, stride=24), :] = after[part, 16 * j : 16 * j + 16, :]
        return after

    sweep([0, 1], [0, 1])
    state_ref[...] = coarse_ref[0]

    def sweep_and_chain(n, carry):
        at = 2 * n
        state_ref[...] = chain_again(at - 1, chain_again(at - 2, state_ref[...]))
        sweep([at, at + 1], [1, 1])
        return carry

    lax.fori_loop(1, 4, sweep_and_chain, 0)
    chain_again(7, chain_again(6, state_ref[...]))


def from_units_kernel(transform_ref, received_ref, send_ref):
    for pair in range(6):
        parts = []
        for part in range(2):
            parts.append(
                jnp.concatenate(
                    [received_ref[pl.ds(part * 12 + 2 * pair + n, UNITS, stride=24), :] for n in range(2)], axis=1
                )
            )
        planes = radial(transform_ref[...], jnp.concatenate(parts, axis=0))
        for n in range(2):
            send_ref[pl.ds(2 * pair + n, 192, stride=12), :] = planes[:, n * 128 : n * 128 + 128]


def place_kernel(received_ref, out_ref):
    for plane in range(12):
        for half in range(2):
            for j in range(6):
                out_ref[plane, 16 * j : 16 * j + 16, half * 128 : half * 128 + 128] = received_ref[
                    pl.ds(plane * 12 + half * 6 + j, 16, stride=144), :
                ]


VMEM = pl.BlockSpec(memory_space=pltpu.VMEM)
HBM = pl.BlockSpec(memory_space=pltpu.HBM)
SMEM = pl.BlockSpec(memory_space=pltpu.SMEM)


def params(mib):
    return pltpu.CompilerParams(vmem_limit_bytes=mib << 20)


def array(*shape):
    return jax.ShapeDtypeStruct(shape, F32)


def exchange(value, axes, peers):
    rows = value.shape[0] // peers
    moved = lax.all_to_all(value.reshape(peers, rows, 128), axes, 0, 0)
    return moved.reshape(value.shape)


def per_device(
    initial_state,
    forcing,
    forward_radial,
    backward_radial,
    forward_axial,
    backward_axial,
    forward_radial_coarse,
    backward_radial_coarse,
    forward_axial_coarse,
    backward_axial_coarse,
    decay_radial,
    decay_axial,
    advection,
    diffusion,
):
    operators = pl.pallas_call(
        operators_kernel,
        out_shape=[jax.ShapeDtypeStruct(shape, kind) for _, shape, kind in OPERATORS],
        in_specs=[SMEM] + [VMEM] * 12,
        out_specs=[VMEM] * len(OPERATORS),
        compiler_params=params(8),
        name="operators",
    )(
        jnp.asarray(SCALARS),
        forward_radial,
        backward_radial,
        forward_axial,
        backward_axial,
        forward_radial_coarse,
        backward_radial_coarse,
        forward_axial_coarse,
        backward_axial_coarse,
        decay_radial.reshape(1, RADIAL),
        decay_axial.reshape(1, AXIAL),
        advection,
        diffusion.reshape(1, RADIAL),
    )
    send = pl.pallas_call(
        gather_kernel,
        out_shape=array(BLOCKS * 40, 128),
        in_specs=[HBM, HBM],
        out_specs=VMEM,
        scratch_shapes=[pltpu.VMEM((12, 24, AXIAL), F32), pltpu.SemaphoreType.DMA],
        compiler_params=params(4),
        name="gather_points",
    )(
        *[
            pltpu.with_memory_space_constraint(field.reshape(12, RADIAL, AXIAL), pltpu.HBM)
            for field in (initial_state, forcing)
        ]
    )
    received = exchange(send, "azim", BLOCKS)
    received = received.reshape(BLOCKS, 40, 128)[:, :36].reshape(BLOCKS * 36, 128)
    send = pl.pallas_call(
        to_units_kernel,
        out_shape=array(128 * 8, 128),
        in_specs=[VMEM, VMEM],
        out_specs=VMEM,
        compiler_params=params(4),
        name="to_units",
    )(jnp.asarray(TO_UNITS), received)
    received = exchange(send, ("tm", "azim"), 128)

    fine, coarse = (2, RADIAL, AXIAL), (2, RADIAL_C, AXIAL_C)
    send = pl.pallas_call(
        units_kernel,
        out_shape=array(SLICES, 16 * 24, 128),
        in_specs=[VMEM] * (1 + len(OPERATORS)),
        out_specs=VMEM,
        scratch_shapes=[
            pltpu.VMEM((2,) + fine, F32),
            pltpu.VMEM((10,) + coarse, F32),
            pltpu.VMEM((10,) + coarse, F32),
            pltpu.VMEM((10,) + fine, F32),
            pltpu.VMEM((10,) + fine, F32),
            pltpu.VMEM((5,) + fine, F32),
            pltpu.VMEM((3,) + fine, F32),
            pltpu.VMEM((10,) + coarse, F32),
            pltpu.VMEM(coarse, F32),
        ],
        compiler_params=params(28),
        name="units",
    )(received, *operators)
    received = exchange(send.reshape(128 * 24, 128), ("tm", "azim"), 128)
    send = pl.pallas_call(
        from_units_kernel,
        out_shape=array(BLOCKS * 144, 128),
        in_specs=[VMEM, VMEM],
        out_specs=VMEM,
        compiler_params=params(8),
        name="from_units",
    )(jnp.asarray(FROM_UNITS), received)
    received = exchange(send, "azim", BLOCKS)
    planes = pl.pallas_call(
        place_kernel,
        out_shape=array(12, RADIAL, AXIAL),
        in_specs=[VMEM],
        out_specs=VMEM,
        compiler_params=params(6),
        name="place",
    )(received)
    return planes.reshape(1, 3, 4, RADIAL, AXIAL)


def solution(mesh):
    split_planes = P(None, "azim", None, None)
    return jax.shard_map(
        per_device,
        mesh=mesh,
        in_specs=(split_planes, split_planes) + (P(),) * 12,
        out_specs=P("tm", None, "azim", None, None),
        check_vma=False,
    )
```

```python
import ml_dtypes
import numpy as np
import jax
import jax.numpy as jnp
from jax import lax
from jax.experimental import pallas as pl
from jax.experimental.pallas import tpu as pltpu
from jax.sharding import PartitionSpec as P

SLICES = 8
AZIMUTH = 64
RADIAL, AXIAL = 96, 256
RADIAL_C, AXIAL_C = 48, 128
BLOCKS = 16
UNITS = 96
STEP = 0.1
HALF = 0.05
F32 = jnp.float32
BF16 = jnp.bfloat16


def azimuth_transform():
    points = np.arange(AZIMUTH)
    rows = np.zeros((2, UNITS, 3, AZIMUTH))
    scalars = np.zeros((128, 4))
    for k in range(64):
        angle = 2.0 * np.pi * k / AZIMUTH
        cos, sin = np.cos(angle * points) / 8.0, np.sin(angle * points) / 8.0
        rows[0, k, 0], rows[0, k, 1] = cos, sin
        rows[1, k, 1], rows[1, k, 0] = cos, -sin
        second = 2.0 * np.cos(angle) - 2.0
        scalars[k] = (second, second, 2.0 * np.sin(angle), -2.0)
    rows[0, 64, 2] = 1.0 / 8.0
    rows[1, 64, 2] = (-1.0) ** points / 8.0
    scalars[64] = (0.0, -4.0, 0.0, 0.0)
    for k in range(1, 32):
        angle = 2.0 * np.pi * k / AZIMUTH
        rows[0, 64 + k, 2] = np.sqrt(2.0) * np.cos(angle * points) / 8.0
        rows[1, 64 + k, 2] = -np.sqrt(2.0) * np.sin(angle * points) / 8.0
        second = 2.0 * np.cos(angle) - 2.0
        scalars[64 + k] = (second, second, 2.0 * np.sin(angle), 0.0)
    matrix = rows.reshape(192, 3, BLOCKS, 4).transpose(0, 2, 1, 3).reshape(192, 192)
    return matrix, scalars.astype(np.float32)


def split_constant(matrix):
    single = matrix.astype(np.float32)
    high = single.astype(ml_dtypes.bfloat16)
    low = (single - high.astype(np.float32)).astype(ml_dtypes.bfloat16)
    return np.concatenate([high, high, low], axis=1)


TRANSFORM, SCALARS = azimuth_transform()
TO_UNITS = split_constant(TRANSFORM)
FROM_UNITS = split_constant(TRANSFORM.T.copy())


def split(value):
    high = value.astype(BF16)
    return high, (value - high.astype(F32)).astype(BF16)


def dot(left, right):
    return jnp.dot(left, right, preferred_element_type=F32)


def axial(value, weights):
    high, low = split(value)
    return dot(jnp.concatenate([high, low, high], axis=1), weights)


def radial(weights, value):
    high, low = split(value)
    return dot(weights, jnp.concatenate([high, low, high], axis=0))


def radial_stacked(weights, value):
    products = dot(weights, jnp.concatenate(split(value), axis=0))
    half = weights.shape[0] // 2
    return products[:half] + products[half:]


def gather_kernel(initial_ref, forcing_ref, send_ref, block_ref, sem):
    tm = lax.axis_index("tm")
    rows = pl.ds(pl.multiple_of((tm % 4) * 24, 8), 24)

    @pl.when(tm < 4)
    def _():
        copy = pltpu.make_async_copy(initial_ref.at[:, rows, :], block_ref, sem)
        copy.start()
        copy.wait()

    @pl.when(tm >= 4)
    def _():
        copy = pltpu.make_async_copy(forcing_ref.at[:, rows, :], block_ref, sem)
        copy.start()
        copy.wait()

    for plane in range(12):
        for piece in range(6):
            half, row = piece // 3, (piece % 3) * 8
            values = block_ref[plane, row : row + 8, half * 128 : half * 128 + 128]
            group, first = piece // 2, (piece % 2) * 8
            send_ref[pl.ds(first * 40 + plane * 3 + group, 8, stride=40), :] = values


def to_units_kernel(transform_ref, received_ref, send_ref):
    columns = [received_ref[pl.ds(group, 192, stride=3), :] for group in range(3)]
    send_ref[UNITS * 8 :, :] = jnp.zeros((32 * 8, 128), F32)
    zero = jnp.zeros((UNITS, 128), F32)
    send_ref[pl.ds(6, UNITS, stride=8), :] = zero
    send_ref[pl.ds(7, UNITS, stride=8), :] = zero
    for group in range(3):
        units = radial(transform_ref[...], columns[group])
        for part in range(2):
            send_ref[pl.ds(part * 3 + group, UNITS, stride=8), :] = units[part * UNITS : (part + 1) * UNITS]


def column_of(row, size):
    at = lax.broadcasted_iota(jnp.int32, (size, size), 0) == lax.broadcasted_iota(jnp.int32, (size, size), 1)
    return jnp.sum(jnp.where(at, row, 0.0), axis=1, keepdims=True)


def identity_plus(value):
    size = value.shape[0]
    at = lax.broadcasted_iota(jnp.int32, (size, size), 0) == lax.broadcasted_iota(jnp.int32, (size, size), 1)
    return jnp.where(at, 1.0, 0.0) + value


def axial_weights(value):
    high, low = split(jnp.transpose(identity_plus(value)))
    return jnp.concatenate([high, high, low], axis=0)


def radial_weights(value):
    high, low = split(value)
    return jnp.concatenate([high, high, low], axis=1)


def stacked_weights(value):
    high, low = split(value)
    return jnp.concatenate(
        [jnp.concatenate([high, high], axis=1), jnp.concatenate([low, jnp.zeros_like(low)], axis=1)], axis=0
    )


OPERATORS = (
    ("axial", (6 * AXIAL, AXIAL), BF16),
    ("radial", (4 * RADIAL, 2 * RADIAL), BF16),
    ("axial_c", (6 * AXIAL_C, AXIAL_C), BF16),
    ("radial_c", (RADIAL + 2 * RADIAL_C, 3 * RADIAL_C), BF16),
    ("point", (5 * RADIAL, AXIAL), F32),
    ("point_c", (4 * RADIAL_C, AXIAL_C), F32),
)


def views(axial_ref, radial_ref, axial_c_ref, radial_c_ref, point_ref, point_c_ref):
    def parts(ref, *sizes):
        ends = np.cumsum(sizes)
        return [ref.at[int(end - size) : int(end), :] for size, end in zip(sizes, ends)]

    return (
        parts(axial_ref, *[3 * AXIAL] * 2)
        + parts(radial_ref, *[2 * RADIAL] * 2)
        + parts(axial_c_ref, *[3 * AXIAL_C] * 2)
        + parts(radial_c_ref, RADIAL, RADIAL_C, RADIAL_C)
        + parts(point_ref, *[RADIAL] * 5)
        + parts(point_c_ref, *[RADIAL_C] * 4)
    )


def operators_kernel(
    scalars_ref,
    forward_radial_ref,
    backward_radial_ref,
    forward_axial_ref,
    backward_axial_ref,
    forward_radial_c_ref,
    backward_radial_c_ref,
    forward_axial_c_ref,
    backward_axial_c_ref,
    decay_radial_ref,
    decay_axial_ref,
    advection_ref,
    diffusion_ref,
    *operator_refs,
):
    all_views = views(*operator_refs)
    (bz_ref, fz_ref, br_ref, fr_ref, bzc_ref, fzc_ref, br_narrow_ref, brc_ref, frc_ref) = all_views[:9]
    (cross_ref, first_ref, second_ref, spectrum_ref, inverse_ref) = all_views[9:14]
    (cross_c_ref, first_c_ref, second_c_ref, inverse_c_ref) = all_views[14:]
    unit = lax.axis_index("tm") * BLOCKS + lax.axis_index("azim")
    scalar = [scalars_ref[unit, n] for n in range(4)]

    bz_ref[...] = axial_weights(backward_axial_ref[...])
    fz_ref[...] = axial_weights(forward_axial_ref[...])
    br_ref[...] = stacked_weights(identity_plus(backward_radial_ref[...]))
    fr_ref[...] = stacked_weights(identity_plus(forward_radial_ref[...]))
    bzc_ref[...] = axial_weights(backward_axial_c_ref[...])
    fzc_ref[...] = axial_weights(forward_axial_c_ref[...])
    brc_ref[...] = radial_weights(identity_plus(backward_radial_c_ref[...]))
    frc_ref[...] = radial_weights(identity_plus(forward_radial_c_ref[...]))
    br_narrow_ref[...] = radial_weights(identity_plus(backward_radial_ref[...])[:, :RADIAL_C])

    diffusion = column_of(diffusion_ref[...], RADIAL)
    cross_ref[...] = scalar[2] * advection_ref[...] + scalar[3]
    first_ref[...] = jnp.broadcast_to(scalar[0] * diffusion, (RADIAL, AXIAL))
    second_ref[...] = jnp.broadcast_to(scalar[1] * diffusion, (RADIAL, AXIAL))
    pick_lane = jnp.where(
        lax.broadcasted_iota(jnp.int32, (AXIAL, AXIAL_C), 0)
        == 2 * lax.broadcasted_iota(jnp.int32, (AXIAL, AXIAL_C), 1),
        1.0,
        0.0,
    )
    pick_row = jnp.where(
        lax.broadcasted_iota(jnp.int32, (RADIAL_C, RADIAL), 1)
        == 2 * lax.broadcasted_iota(jnp.int32, (RADIAL_C, RADIAL), 0),
        1.0,
        0.0,
    )
    exact = lax.Precision.HIGHEST
    advection_c = jnp.dot(
        jnp.dot(pick_row, advection_ref[...], precision=exact, preferred_element_type=F32),
        pick_lane,
        precision=exact,
        preferred_element_type=F32,
    )
    diffusion_c = jnp.sum(pick_row * diffusion_ref[...], axis=1, keepdims=True)
    cross_c_ref[...] = scalar[2] * advection_c + scalar[3]
    first_c_ref[...] = jnp.broadcast_to(scalar[0] * diffusion_c, (RADIAL_C, AXIAL_C))
    second_c_ref[...] = jnp.broadcast_to(scalar[1] * diffusion_c, (RADIAL_C, AXIAL_C))
    spectrum = -(column_of(decay_radial_ref[...], RADIAL) + decay_axial_ref[...])
    spectrum_ref[...] = spectrum
    inverse_ref[...] = 1.0 / (1.0 - HALF * spectrum)
    inverse_c_ref[...] = 1.0 / (1.0 - STEP * spectrum[:RADIAL_C, :AXIAL_C])


def units_kernel(
    received_ref,
    axial_ref,
    radial_ref,
    axial_c_ref,
    radial_c_ref,
    point_ref,
    point_c_ref,
    out_ref,
    field_ref,
    coarse_ref,
    push_ref,
    ahead_ref,
    behind_ref,
    known_ref,
    const_ref,
    gain_ref,
    state_ref,
):
    all_views = views(axial_ref, radial_ref, axial_c_ref, radial_c_ref, point_ref, point_c_ref)
    (bz_ref, fz_ref, br_ref, fr_ref, bzc_ref, fzc_ref, br_narrow_ref, brc_ref, frc_ref) = all_views[:9]
    (cross_ref, first_ref, second_ref, spectrum_ref, inverse_ref) = all_views[9:14]
    (cross_c_ref, first_c_ref, second_c_ref, inverse_c_ref) = all_views[14:]

    for field in range(2):
        for part in range(2):
            for rows in range(4):
                source = (field * 4 + rows) * 16 * 8 + part * 3
                for piece in range(6):
                    half, row = piece // 3, (piece % 3) * 8
                    group, first = piece // 2, (piece % 2) * 8
                    field_ref[field, part, rows * 24 + row : rows * 24 + row + 8, half * 128 : half * 128 + 128] = (
                        received_ref[pl.ds(source + first * 8 + group, 8, stride=8), :]
                    )

    def forces(re, im, cross, first, second):
        return first * re - cross * im, second * im + cross * re

    def blocks(rows, size):
        return [rows[n : n + size] for n in range(0, rows.shape[0], size)]

    def fine_forces(planes):
        moved = []
        for n in range(0, len(planes), 2):
            moved += forces(planes[n], planes[n + 1], cross_ref[...], first_ref[...], second_ref[...])
        return moved

    def flat(states):
        return jnp.concatenate([state.reshape(-1, state.shape[-1]) for state in states], axis=0)

    def pairs(planes):
        return [jnp.stack(planes[n : n + 2]) for n in range(0, len(planes), 2)]

    def to_points(states):
        inner = axial(flat(states), bz_ref[...])
        yield
        planes = []
        for plane in blocks(inner, RADIAL):
            planes.append(radial_stacked(br_ref[...], plane))
            yield
        return planes

    def to_modes(planes):
        inner = axial(jnp.concatenate(planes, axis=0), fz_ref[...])
        yield
        planes = []
        for plane in blocks(inner, RADIAL):
            planes.append(radial_stacked(fr_ref[...], plane))
            yield
        return pairs(planes)

    def explicit(states):
        planes = yield from to_points(states)
        return (yield from to_modes(fine_forces(planes)))

    def explicit_of_coarse(states):
        narrow = jnp.concatenate([bz_ref[n * AXIAL : n * AXIAL + AXIAL_C, :] for n in range(3)], axis=0)
        inner = axial(flat(states), narrow)
        yield
        planes = []
        for plane in blocks(inner, RADIAL_C):
            planes.append(radial(br_narrow_ref[...], plane))
            yield
        return (yield from to_modes(fine_forces(planes)))

    def restricted_explicit(states):
        planes = fine_forces((yield from to_points(states)))
        rows = jnp.concatenate([fr_ref[:RADIAL_C, :], fr_ref[RADIAL : RADIAL + RADIAL_C, :]], axis=0)
        narrow = []
        for plane in planes:
            narrow.append(radial_stacked(rows, plane))
            yield
        inner = axial(jnp.concatenate(narrow, axis=0), fz_ref[:, :AXIAL_C])
        yield
        return pairs(blocks(inner, RADIAL_C))

    def coarse_explicit(modes):
        inner = axial(modes.reshape(2 * RADIAL_C, AXIAL_C), bzc_ref[...])
        yield
        both = radial(brc_ref[...], jnp.concatenate([inner[:RADIAL_C], inner[RADIAL_C:]], axis=1))
        yield
        re, im = forces(
            both[:, :AXIAL_C], both[:, AXIAL_C:], cross_c_ref[...], first_c_ref[...], second_c_ref[...]
        )
        both = radial(frc_ref[...], jnp.concatenate([re, im], axis=1))
        yield
        inner = axial(jnp.concatenate([both[:, :AXIAL_C], both[:, AXIAL_C:]], axis=0), fzc_ref[...])
        yield
        return inner.reshape(2, RADIAL_C, AXIAL_C)

    def side_by_side(*streams):
        left = [[stream, 0, count, None] for stream, count in streams]
        while any(entry[0] is not None for entry in left):
            entry = min((e for e in left if e[0] is not None), key=lambda e: e[1] / e[2])
            try:
                next(entry[0])
                entry[1] += 1
            except StopIteration as end:
                entry[0], entry[3] = None, end.value
        return [entry[3] for entry in left]

    def alone(stream):
        return side_by_side((stream, 1))[0]

    def corner(value):
        return value[:, :RADIAL_C, :AXIAL_C]

    known_ref[0] = alone(explicit([field_ref[0]]))[0]
    spectrum = spectrum_ref[...]
    total0 = known_ref[0] + field_ref[1] + spectrum * field_ref[0]
    known_ref[3] = inverse_ref[...] * (field_ref[0] - HALF * spectrum * field_ref[0] + (0.5 * STEP) * total0)
    known_ref[1] = alone(explicit([known_ref[3]]))[0]
    known_ref[4] = inverse_ref[...] * (
        known_ref[3]
        + HALF * (known_ref[1] - known_ref[0])
        - HALF * spectrum_ref[...] * field_ref[0]
        + (0.5 * STEP) * (known_ref[0] + field_ref[1] + spectrum_ref[...] * field_ref[0])
    )
    known_ref[2] = alone(explicit([known_ref[4]]))[0]
    spectrum_c = spectrum_ref[:RADIAL_C, :AXIAL_C]
    coarse_known = [known_ref[n, :, :RADIAL_C, :AXIAL_C] for n in range(5)]
    start_c = field_ref[0, :, :RADIAL_C, :AXIAL_C]
    forcing_c = field_ref[1, :, :RADIAL_C, :AXIAL_C]
    gain_ref[0] = (
        STEP
        * (
            (coarse_known[0] + spectrum_c * start_c) / 6.0
            + (2.0 / 3.0) * (coarse_known[1] + spectrum_c * coarse_known[3])
            + (coarse_known[2] + spectrum_c * coarse_known[4]) / 6.0
            + forcing_c
        )
        - STEP * spectrum_c * coarse_known[4]
    )
    coarse_ref[0] = start_c
    coarse_ref[9] = coarse_known[4]
    coarse_ref[1] = inverse_c_ref[...] * (gain_ref[0] + start_c)

    def chain(*places):
        for n in places:
            latest = coarse_ref[n - 1]
            push = yield from coarse_explicit(latest - coarse_ref[0])
            coarse_ref[n] = inverse_c_ref[...] * (gain_ref[0] + latest + STEP * push)

    def spread(places):
        states = [coarse_ref[n] for n in places]
        pushes = yield from explicit_of_coarse(states)
        damping = (0.25 * HALF) * spectrum_ref[:RADIAL_C, :AXIAL_C]
        for n, state, push in zip(places, states, pushes):
            push_ref[n] = corner(push)
            behind_ref[n] = (0.25 * HALF) * push
            ahead_ref[n] = (0.75 * HALF) * push
            damped = damping * state
            behind_ref[n, :, :RADIAL_C, :AXIAL_C] = (0.25 * HALF) * corner(push) - damped
            ahead_ref[n, :, :RADIAL_C, :AXIAL_C] = (0.75 * HALF) * corner(push) + damped + state

    def chaining(*places):
        return chain(*places), 4 * len(places)

    def spreading(*places):
        return spread(places), 2 + 4 * len(places)

    side_by_side(chaining(2, 3, 4), spreading(0, 1, 9))
    side_by_side(chaining(5, 6), spreading(2, 3, 4))

    def padded(value):
        return jnp.pad(value, ((0, 0), (0, RADIAL - RADIAL_C), (0, AXIAL - AXIAL_C)))

    spectrum = spectrum_ref[...]
    wide_start = padded(coarse_ref[0])
    wide_end = padded(coarse_ref[9])
    push_start = (ahead_ref[0] + behind_ref[0] - wide_start) * (1.0 / HALF)
    push_end = (ahead_ref[9] + behind_ref[9] - wide_end) * (1.0 / HALF)
    rhs_start = push_start + spectrum * wide_start
    rhs_end = push_end + spectrum * wide_end
    total0 = known_ref[0] + field_ref[1] + spectrum * field_ref[0]
    total1 = known_ref[1] + field_ref[1] + spectrum * known_ref[3]
    total2 = known_ref[2] + field_ref[1] + spectrum * known_ref[4]
    shared = -HALF * spectrum * (known_ref[3] - 0.5 * (wide_start + wide_end)) + STEP * (
        (5.0 / 24.0) * total0 + (1.0 / 3.0) * total1 - (1.0 / 24.0) * total2 - 0.375 * rhs_start - 0.125 * rhs_end
    )
    const_ref[0] = field_ref[0] - wide_start + shared
    const_ref[1] = known_ref[4] - wide_end + HALF * (known_ref[2] - push_end - known_ref[0] + push_start) + shared
    const_ref[2] = (
        -HALF * (known_ref[1] - 0.5 * (push_start + push_end))
        - HALF * spectrum * (known_ref[4] - wide_end)
        + STEP
        * (
            (-1.0 / 24.0) * total0
            + (1.0 / 3.0) * total1
            + (5.0 / 24.0) * total2
            - 0.125 * rhs_start
            - 0.375 * rhs_end
        )
    )
    gain_ref[8] = STEP * (forcing_c + (coarse_known[0] - push_ref[0]) / 6.0)
    gain_ref[9] = STEP * (forcing_c + (coarse_known[2] - push_ref[9]) / 6.0)

    def sweep(places, kinds):
        middles = [
            inverse_ref[...] * (const_ref[kind] + ahead_ref[n] + behind_ref[n + 1])
            for n, kind in zip(places, kinds)
        ]
        middle_pushes = yield from explicit(middles)
        endings = [
            inverse_ref[...] * (middle + HALF * push + const_ref[2] + behind_ref[n + 1] - behind_ref[n])
            for n, middle, push in zip(places, middles, middle_pushes)
        ]
        ending_pushes = yield from restricted_explicit(endings)
        spectrum_c = spectrum_ref[:RADIAL_C, :AXIAL_C]
        for at, n in enumerate(places):
            middle, ending = middles[at], endings[at]
            gain_ref[n] = (
                gain_ref[8 + kinds[at]]
                + (STEP / 6.0) * (push_ref[n] + spectrum_c * coarse_ref[n])
                + (STEP * 2.0 / 3.0) * (corner(middle_pushes[at]) + spectrum_c * corner(middle))
                + (STEP / 6.0) * ending_pushes[at]
                - (STEP * 5.0 / 6.0) * spectrum_c * corner(ending)
            )
            for part in range(2):
                for half in range(2):
                    for j in range(0 if half else 3, 6):
                        out_ref[n, pl.ds(part * 12 + half * 6 + j, 16, stride=24), :] = ending[
                            part, 16 * j : 16 * j + 16, half * 128 : half * 128 + 128
                        ]

    def chain_again(places):
        for n in places:
            state = state_ref[...]
            push = yield from coarse_explicit(state - coarse_ref[n])
            after = inverse_c_ref[...] * (gain_ref[n] + state + STEP * push)
            state_ref[...] = after
            for part in range(2):
                for j in range(3):
                    out_ref[n, pl.ds(part * 12 + j, 16, stride=24), :] = after[part, 16 * j : 16 * j + 16, :]

    def sweeping(*places):
        return sweep(places, [min(n, 1) for n in places]), 4 + 8 * len(places)

    def chaining_again(*places):
        return chain_again(places), 4 * len(places)

    state_ref[...] = coarse_ref[0]
    side_by_side(chaining(7, 8), sweeping(0, 1, 2), spreading(5, 6))
    side_by_side(sweeping(3, 4, 5), chaining_again(0, 1, 2), spreading(7, 8))
    side_by_side(sweeping(6, 7), chaining_again(3, 4, 5))
    side_by_side(chaining_again(6, 7))


def from_units_kernel(transform_ref, received_ref, send_ref):
    for pair in range(6):
        parts = []
        for part in range(2):
            parts.append(
                jnp.concatenate(
                    [received_ref[pl.ds(part * 12 + 2 * pair + n, UNITS, stride=24), :] for n in range(2)], axis=1
                )
            )
        planes = radial(transform_ref[...], jnp.concatenate(parts, axis=0))
        for n in range(2):
            send_ref[pl.ds(2 * pair + n, 192, stride=12), :] = planes[:, n * 128 : n * 128 + 128]


def place_kernel(received_ref, out_ref):
    for plane in range(12):
        for half in range(2):
            for j in range(6):
                out_ref[plane, 16 * j : 16 * j + 16, half * 128 : half * 128 + 128] = received_ref[
                    pl.ds(plane * 12 + half * 6 + j, 16, stride=144), :
                ]


VMEM = pl.BlockSpec(memory_space=pltpu.VMEM)
HBM = pl.BlockSpec(memory_space=pltpu.HBM)
SMEM = pl.BlockSpec(memory_space=pltpu.SMEM)


def params(mib):
    return pltpu.CompilerParams(vmem_limit_bytes=mib << 20)


def array(*shape):
    return jax.ShapeDtypeStruct(shape, F32)


def exchange(value, axes, peers):
    rows = value.shape[0] // peers
    moved = lax.all_to_all(value.reshape(peers, rows, 128), axes, 0, 0)
    return moved.reshape(value.shape)


def per_device(
    initial_state,
    forcing,
    forward_radial,
    backward_radial,
    forward_axial,
    backward_axial,
    forward_radial_coarse,
    backward_radial_coarse,
    forward_axial_coarse,
    backward_axial_coarse,
    decay_radial,
    decay_axial,
    advection,
    diffusion,
):
    operators = pl.pallas_call(
        operators_kernel,
        out_shape=[jax.ShapeDtypeStruct(shape, kind) for _, shape, kind in OPERATORS],
        in_specs=[SMEM] + [VMEM] * 12,
        out_specs=[VMEM] * len(OPERATORS),
        compiler_params=params(8),
        name="operators",
    )(
        jnp.asarray(SCALARS),
        forward_radial,
        backward_radial,
        forward_axial,
        backward_axial,
        forward_radial_coarse,
        backward_radial_coarse,
        forward_axial_coarse,
        backward_axial_coarse,
        decay_radial.reshape(1, RADIAL),
        decay_axial.reshape(1, AXIAL),
        advection,
        diffusion.reshape(1, RADIAL),
    )
    send = pl.pallas_call(
        gather_kernel,
        out_shape=array(BLOCKS * 40, 128),
        in_specs=[HBM, HBM],
        out_specs=VMEM,
        scratch_shapes=[pltpu.VMEM((12, 24, AXIAL), F32), pltpu.SemaphoreType.DMA],
        compiler_params=params(4),
        name="gather_points",
    )(
        *[
            pltpu.with_memory_space_constraint(field.reshape(12, RADIAL, AXIAL), pltpu.HBM)
            for field in (initial_state, forcing)
        ]
    )
    received = exchange(send, "azim", BLOCKS)
    received = received.reshape(BLOCKS, 40, 128)[:, :36].reshape(BLOCKS * 36, 128)
    send = pl.pallas_call(
        to_units_kernel,
        out_shape=array(128 * 8, 128),
        in_specs=[VMEM, VMEM],
        out_specs=VMEM,
        compiler_params=params(4),
        name="to_units",
    )(jnp.asarray(TO_UNITS), received)
    received = exchange(send, ("tm", "azim"), 128)

    fine, coarse = (2, RADIAL, AXIAL), (2, RADIAL_C, AXIAL_C)
    send = pl.pallas_call(
        units_kernel,
        out_shape=array(SLICES, 16 * 24, 128),
        in_specs=[VMEM] * (1 + len(OPERATORS)),
        out_specs=VMEM,
        scratch_shapes=[
            pltpu.VMEM((2,) + fine, F32),
            pltpu.VMEM((10,) + coarse, F32),
            pltpu.VMEM((10,) + coarse, F32),
            pltpu.VMEM((10,) + fine, F32),
            pltpu.VMEM((10,) + fine, F32),
            pltpu.VMEM((5,) + fine, F32),
            pltpu.VMEM((3,) + fine, F32),
            pltpu.VMEM((10,) + coarse, F32),
            pltpu.VMEM(coarse, F32),
        ],
        compiler_params=params(28),
        name="units",
    )(received, *operators)
    received = exchange(send.reshape(128 * 24, 128), ("tm", "azim"), 128)
    send = pl.pallas_call(
        from_units_kernel,
        out_shape=array(BLOCKS * 144, 128),
        in_specs=[VMEM, VMEM],
        out_specs=VMEM,
        compiler_params=params(8),
        name="from_units",
    )(jnp.asarray(FROM_UNITS), received)
    received = exchange(send, "azim", BLOCKS)
    planes = pl.pallas_call(
        place_kernel,
        out_shape=array(12, RADIAL, AXIAL),
        in_specs=[VMEM],
        out_specs=VMEM,
        compiler_params=params(6),
        name="place",
    )(received)
    return planes.reshape(1, 3, 4, RADIAL, AXIAL)


def solution(mesh):
    split_planes = P(None, "azim", None, None)
    return jax.shard_map(
        per_device,
        mesh=mesh,
        in_specs=(split_planes, split_planes) + (P(),) * 12,
        out_specs=P("tm", None, "azim", None, None),
        check_vma=False,
    )
```

```python
import ml_dtypes
import numpy as np
import jax
import jax.numpy as jnp
from jax import lax
from jax.experimental import pallas as pl
from jax.experimental.pallas import tpu as pltpu
from jax.sharding import PartitionSpec as P

SLICES = 8
AZIMUTH = 64
RADIAL, AXIAL = 96, 256
RADIAL_C, AXIAL_C = 48, 128
BLOCKS = 16
UNITS = 96
STEP = 0.1
HALF = 0.05
F32 = jnp.float32
BF16 = jnp.bfloat16


def azimuth_transform():
    points = np.arange(AZIMUTH)
    rows = np.zeros((2, UNITS, 3, AZIMUTH))
    scalars = np.zeros((128, 4))
    for k in range(64):
        angle = 2.0 * np.pi * k / AZIMUTH
        cos, sin = np.cos(angle * points) / 8.0, np.sin(angle * points) / 8.0
        rows[0, k, 0], rows[0, k, 1] = cos, sin
        rows[1, k, 1], rows[1, k, 0] = cos, -sin
        second = 2.0 * np.cos(angle) - 2.0
        scalars[k] = (second, second, 2.0 * np.sin(angle), -2.0)
    rows[0, 64, 2] = 1.0 / 8.0
    rows[1, 64, 2] = (-1.0) ** points / 8.0
    scalars[64] = (0.0, -4.0, 0.0, 0.0)
    for k in range(1, 32):
        angle = 2.0 * np.pi * k / AZIMUTH
        rows[0, 64 + k, 2] = np.sqrt(2.0) * np.cos(angle * points) / 8.0
        rows[1, 64 + k, 2] = -np.sqrt(2.0) * np.sin(angle * points) / 8.0
        second = 2.0 * np.cos(angle) - 2.0
        scalars[64 + k] = (second, second, 2.0 * np.sin(angle), 0.0)
    matrix = rows.reshape(192, 3, BLOCKS, 4).transpose(0, 2, 1, 3).reshape(192, 192)
    return matrix, scalars.astype(np.float32)


def split_constant(matrix):
    single = matrix.astype(np.float32)
    high = single.astype(ml_dtypes.bfloat16)
    low = (single - high.astype(np.float32)).astype(ml_dtypes.bfloat16)
    return np.concatenate([high, high, low], axis=1)


TRANSFORM, SCALARS = azimuth_transform()
TO_UNITS = split_constant(TRANSFORM)
FROM_UNITS = split_constant(TRANSFORM.T.copy())


def split(value):
    high = value.astype(BF16)
    return high, (value - high.astype(F32)).astype(BF16)


def dot(left, right):
    return jnp.dot(left, right, preferred_element_type=F32)


def axial(value, weights):
    high, low = split(value)
    depth = weights.shape[0] // 3
    products = dot(jnp.concatenate([high, low], axis=0), weights[:depth])
    return products[: value.shape[0]] + products[value.shape[0] :] + dot(high, weights[2 * depth :])


def radial(weights, value):
    high, low = split(value)
    return dot(weights, jnp.concatenate([high, low, high], axis=0))


def radial_stacked(weights, value):
    products = dot(weights, jnp.concatenate(split(value), axis=0))
    half = weights.shape[0] // 2
    return products[:half] + products[half:]


def gather_kernel(initial_ref, forcing_ref, send_ref, block_ref, sems):
    tm = lax.axis_index("tm")
    rows = pl.ds(pl.multiple_of((tm % 4) * 24, 8), 24)

    def copies(source_ref):
        for group in range(4):
            own = pl.ds(3 * group, 3)
            yield pltpu.make_async_copy(source_ref.at[own, rows, :], block_ref.at[own], sems.at[group])

    @pl.when(tm < 4)
    def _():
        for copy in copies(initial_ref):
            copy.start()

    @pl.when(tm >= 4)
    def _():
        for copy in copies(forcing_ref):
            copy.start()

    waits = list(copies(initial_ref))
    for plane in range(12):
        if plane % 3 == 0:
            waits[plane // 3].wait()
        for piece in range(6):
            half, row = piece // 3, (piece % 3) * 8
            values = block_ref[plane, row : row + 8, half * 128 : half * 128 + 128]
            group, first = piece // 2, (piece % 2) * 8
            send_ref[pl.ds(first * 40 + plane * 3 + group, 8, stride=40), :] = values


def to_units_kernel(transform_ref, received_ref, send_ref):
    columns = [received_ref[pl.ds(group, 192, stride=3), :] for group in range(3)]
    send_ref[UNITS * 8 :, :] = jnp.zeros((32 * 8, 128), F32)
    zero = jnp.zeros((UNITS, 128), F32)
    send_ref[pl.ds(6, UNITS, stride=8), :] = zero
    send_ref[pl.ds(7, UNITS, stride=8), :] = zero
    for group in range(3):
        units = radial(transform_ref[...], columns[group])
        for part in range(2):
            send_ref[pl.ds(part * 3 + group, UNITS, stride=8), :] = units[part * UNITS : (part + 1) * UNITS]


def column_of(row, size):
    at = lax.broadcasted_iota(jnp.int32, (size, size), 0) == lax.broadcasted_iota(jnp.int32, (size, size), 1)
    return jnp.sum(jnp.where(at, row, 0.0), axis=1, keepdims=True)


def identity_plus(value):
    size = value.shape[0]
    at = lax.broadcasted_iota(jnp.int32, (size, size), 0) == lax.broadcasted_iota(jnp.int32, (size, size), 1)
    return jnp.where(at, 1.0, 0.0) + value


def axial_weights(value):
    high, low = split(jnp.transpose(identity_plus(value)))
    return jnp.concatenate([high, high, low], axis=0)


def radial_weights(value):
    high, low = split(value)
    return jnp.concatenate([high, high, low], axis=1)


def stacked_weights(value):
    high, low = split(value)
    return jnp.concatenate(
        [jnp.concatenate([high, high], axis=1), jnp.concatenate([low, jnp.zeros_like(low)], axis=1)], axis=0
    )


OPERATORS = (
    ("axial", (6 * AXIAL, AXIAL), BF16),
    ("radial", (4 * RADIAL, 2 * RADIAL), BF16),
    ("axial_c", (6 * AXIAL_C, AXIAL_C), BF16),
    ("radial_c", (RADIAL + 2 * RADIAL_C, 3 * RADIAL_C), BF16),
    ("point", (5 * RADIAL, AXIAL), F32),
    ("point_c", (4 * RADIAL_C, AXIAL_C), F32),
)


def views(axial_ref, radial_ref, axial_c_ref, radial_c_ref, point_ref, point_c_ref):
    def parts(ref, *sizes):
        ends = np.cumsum(sizes)
        return [ref.at[int(end - size) : int(end), :] for size, end in zip(sizes, ends)]

    return (
        parts(axial_ref, *[3 * AXIAL] * 2)
        + parts(radial_ref, *[2 * RADIAL] * 2)
        + parts(axial_c_ref, *[3 * AXIAL_C] * 2)
        + parts(radial_c_ref, RADIAL, RADIAL_C, RADIAL_C)
        + parts(point_ref, *[RADIAL] * 5)
        + parts(point_c_ref, *[RADIAL_C] * 4)
    )


def operators_kernel(
    scalars_ref,
    forward_radial_ref,
    backward_radial_ref,
    forward_axial_ref,
    backward_axial_ref,
    forward_radial_c_ref,
    backward_radial_c_ref,
    forward_axial_c_ref,
    backward_axial_c_ref,
    decay_radial_ref,
    decay_axial_ref,
    advection_ref,
    diffusion_ref,
    *operator_refs,
):
    all_views = views(*operator_refs)
    (bz_ref, fz_ref, br_ref, fr_ref, bzc_ref, fzc_ref, br_narrow_ref, brc_ref, frc_ref) = all_views[:9]
    (cross_ref, first_ref, second_ref, spectrum_ref, inverse_ref) = all_views[9:14]
    (cross_c_ref, first_c_ref, second_c_ref, inverse_c_ref) = all_views[14:]
    unit = lax.axis_index("tm") * BLOCKS + lax.axis_index("azim")
    scalar = [scalars_ref[unit, n] for n in range(4)]

    bz_ref[...] = axial_weights(backward_axial_ref[...])
    fz_ref[...] = axial_weights(forward_axial_ref[...])
    br_ref[...] = stacked_weights(identity_plus(backward_radial_ref[...]))
    fr_ref[...] = stacked_weights(identity_plus(forward_radial_ref[...]))
    bzc_ref[...] = axial_weights(backward_axial_c_ref[...])
    fzc_ref[...] = axial_weights(forward_axial_c_ref[...])
    brc_ref[...] = radial_weights(identity_plus(backward_radial_c_ref[...]))
    frc_ref[...] = radial_weights(identity_plus(forward_radial_c_ref[...]))
    br_narrow_ref[...] = radial_weights(identity_plus(backward_radial_ref[...])[:, :RADIAL_C])

    diffusion = column_of(diffusion_ref[...], RADIAL)
    cross_ref[...] = scalar[2] * advection_ref[...] + scalar[3]
    first_ref[...] = jnp.broadcast_to(scalar[0] * diffusion, (RADIAL, AXIAL))
    second_ref[...] = jnp.broadcast_to(scalar[1] * diffusion, (RADIAL, AXIAL))
    pick_lane = jnp.where(
        lax.broadcasted_iota(jnp.int32, (AXIAL, AXIAL_C), 0)
        == 2 * lax.broadcasted_iota(jnp.int32, (AXIAL, AXIAL_C), 1),
        1.0,
        0.0,
    )
    pick_row = jnp.where(
        lax.broadcasted_iota(jnp.int32, (RADIAL_C, RADIAL), 1)
        == 2 * lax.broadcasted_iota(jnp.int32, (RADIAL_C, RADIAL), 0),
        1.0,
        0.0,
    )
    exact = lax.Precision.HIGHEST
    advection_c = jnp.dot(
        jnp.dot(pick_row, advection_ref[...], precision=exact, preferred_element_type=F32),
        pick_lane,
        precision=exact,
        preferred_element_type=F32,
    )
    diffusion_c = jnp.sum(pick_row * diffusion_ref[...], axis=1, keepdims=True)
    cross_c_ref[...] = scalar[2] * advection_c + scalar[3]
    first_c_ref[...] = jnp.broadcast_to(scalar[0] * diffusion_c, (RADIAL_C, AXIAL_C))
    second_c_ref[...] = jnp.broadcast_to(scalar[1] * diffusion_c, (RADIAL_C, AXIAL_C))
    spectrum = -(column_of(decay_radial_ref[...], RADIAL) + decay_axial_ref[...])
    spectrum_ref[...] = spectrum
    inverse_ref[...] = 1.0 / (1.0 - HALF * spectrum)
    inverse_c_ref[...] = 1.0 / (1.0 - STEP * spectrum[:RADIAL_C, :AXIAL_C])


def units_kernel(
    received_ref,
    axial_ref,
    radial_ref,
    axial_c_ref,
    radial_c_ref,
    point_ref,
    point_c_ref,
    out_ref,
    field_ref,
    coarse_ref,
    push_ref,
    ahead_ref,
    behind_ref,
    known_ref,
    const_ref,
    gain_ref,
    state_ref,
):
    all_views = views(axial_ref, radial_ref, axial_c_ref, radial_c_ref, point_ref, point_c_ref)
    (bz_ref, fz_ref, br_ref, fr_ref, bzc_ref, fzc_ref, br_narrow_ref, brc_ref, frc_ref) = all_views[:9]
    (cross_ref, first_ref, second_ref, spectrum_ref, inverse_ref) = all_views[9:14]
    (cross_c_ref, first_c_ref, second_c_ref, inverse_c_ref) = all_views[14:]

    for field in range(2):
        for part in range(2):
            for rows in range(4):
                source = (field * 4 + rows) * 16 * 8 + part * 3
                for piece in range(6):
                    half, row = piece // 3, (piece % 3) * 8
                    group, first = piece // 2, (piece % 2) * 8
                    field_ref[field, part, rows * 24 + row : rows * 24 + row + 8, half * 128 : half * 128 + 128] = (
                        received_ref[pl.ds(source + first * 8 + group, 8, stride=8), :]
                    )

    def forces(re, im, cross, first, second):
        return first * re - cross * im, second * im + cross * re

    def blocks(rows, size):
        return [rows[n : n + size] for n in range(0, rows.shape[0], size)]

    def fine_forces(planes):
        moved = []
        for n in range(0, len(planes), 2):
            moved += forces(planes[n], planes[n + 1], cross_ref[...], first_ref[...], second_ref[...])
        return moved

    def flat(states):
        return jnp.concatenate([state.reshape(-1, state.shape[-1]) for state in states], axis=0)

    def pairs(planes):
        return [jnp.stack(planes[n : n + 2]) for n in range(0, len(planes), 2)]

    def to_points(states):
        inner = axial(flat(states), bz_ref[...])
        yield
        planes = []
        for plane in blocks(inner, RADIAL):
            planes.append(radial_stacked(br_ref[...], plane))
            yield
        return planes

    def to_modes(planes):
        inner = axial(jnp.concatenate(planes, axis=0), fz_ref[...])
        yield
        planes = []
        for plane in blocks(inner, RADIAL):
            planes.append(radial_stacked(fr_ref[...], plane))
            yield
        return pairs(planes)

    def explicit(states):
        planes = yield from to_points(states)
        return (yield from to_modes(fine_forces(planes)))

    def explicit_of_coarse(states):
        narrow = jnp.concatenate([bz_ref[n * AXIAL : n * AXIAL + AXIAL_C, :] for n in range(3)], axis=0)
        inner = axial(flat(states), narrow)
        yield
        planes = []
        for plane in blocks(inner, RADIAL_C):
            planes.append(radial(br_narrow_ref[...], plane))
            yield
        return (yield from to_modes(fine_forces(planes)))

    def restricted_explicit(states):
        planes = fine_forces((yield from to_points(states)))
        rows = jnp.concatenate([fr_ref[:RADIAL_C, :], fr_ref[RADIAL : RADIAL + RADIAL_C, :]], axis=0)
        narrow = []
        for plane in planes:
            narrow.append(radial_stacked(rows, plane))
            yield
        inner = axial(jnp.concatenate(narrow, axis=0), fz_ref[:, :AXIAL_C])
        yield
        return pairs(blocks(inner, RADIAL_C))

    def coarse_explicit(modes):
        inner = axial(modes.reshape(2 * RADIAL_C, AXIAL_C), bzc_ref[...])
        yield
        both = radial(brc_ref[...], jnp.concatenate([inner[:RADIAL_C], inner[RADIAL_C:]], axis=1))
        yield
        re, im = forces(
            both[:, :AXIAL_C], both[:, AXIAL_C:], cross_c_ref[...], first_c_ref[...], second_c_ref[...]
        )
        both = radial(frc_ref[...], jnp.concatenate([re, im], axis=1))
        yield
        inner = axial(jnp.concatenate([both[:, :AXIAL_C], both[:, AXIAL_C:]], axis=0), fzc_ref[...])
        yield
        return inner.reshape(2, RADIAL_C, AXIAL_C)

    done = set()

    def side_by_side(*tasks):
        waiting = list(tasks)
        while waiting:
            ready = [task for task in waiting if all(need in done for need in task[0])]
            for task in reversed(ready):
                try:
                    next(task[2])
                except StopIteration:
                    done.update(task[1])
                    waiting.remove(task)

    def corner(value):
        return value[:, :RADIAL_C, :AXIAL_C]

    spectrum_c = spectrum_ref[:RADIAL_C, :AXIAL_C]
    start_c = field_ref[0, :, :RADIAL_C, :AXIAL_C]
    forcing_c = field_ref[1, :, :RADIAL_C, :AXIAL_C]
    coarse_ref[0] = start_c

    def first_iteration():
        known_ref[0] = (yield from explicit([field_ref[0]]))[0]
        spectrum = spectrum_ref[...]
        total0 = known_ref[0] + field_ref[1] + spectrum * field_ref[0]
        known_ref[3] = inverse_ref[...] * (field_ref[0] - HALF * spectrum * field_ref[0] + (0.5 * STEP) * total0)
        known_ref[1] = (yield from explicit([known_ref[3]]))[0]
        known_ref[4] = inverse_ref[...] * (
            known_ref[3]
            + HALF * (known_ref[1] - known_ref[0])
            - HALF * spectrum_ref[...] * field_ref[0]
            + (0.5 * STEP) * (known_ref[0] + field_ref[1] + spectrum_ref[...] * field_ref[0])
        )
        coarse_ref[9] = known_ref[4, :, :RADIAL_C, :AXIAL_C]
        done.add("S9")
        known_ref[2] = (yield from explicit([known_ref[4]]))[0]
        coarse_known = [known_ref[n, :, :RADIAL_C, :AXIAL_C] for n in range(5)]
        gain_ref[0] = (
            STEP
            * (
                (coarse_known[0] + spectrum_c * start_c) / 6.0
                + (2.0 / 3.0) * (coarse_known[1] + spectrum_c * coarse_known[3])
                + (coarse_known[2] + spectrum_c * coarse_known[4]) / 6.0
                + forcing_c
            )
            - STEP * spectrum_c * coarse_known[4]
        )
        coarse_ref[1] = inverse_c_ref[...] * (gain_ref[0] + start_c)
        gain_ref[10] = gain_ref[0]


    def chain(*places):
        for n in places:
            latest = coarse_ref[n - 1]
            push = yield from coarse_explicit(latest - coarse_ref[0])
            coarse_ref[n] = inverse_c_ref[...] * (gain_ref[10] + latest + STEP * push)

    def spread(places):
        states = [coarse_ref[n] for n in places]
        pushes = yield from explicit_of_coarse(states)
        damping = (0.25 * HALF) * spectrum_ref[:RADIAL_C, :AXIAL_C]
        for n, state, push in zip(places, states, pushes):
            push_ref[n] = corner(push)
            behind_ref[n] = (0.25 * HALF) * push
            ahead_ref[n] = (0.75 * HALF) * push
            damped = damping * state
            behind_ref[n, :, :RADIAL_C, :AXIAL_C] = (0.25 * HALF) * corner(push) - damped
            ahead_ref[n, :, :RADIAL_C, :AXIAL_C] = (0.75 * HALF) * corner(push) + damped + state

    def padded(value):
        return jnp.pad(value, ((0, 0), (0, RADIAL - RADIAL_C), (0, AXIAL - AXIAL_C)))

    def constants():
        spectrum = spectrum_ref[...]
        wide_start = padded(coarse_ref[0])
        wide_end = padded(coarse_ref[9])
        push_start = (ahead_ref[0] + behind_ref[0] - wide_start) * (1.0 / HALF)
        push_end = (ahead_ref[9] + behind_ref[9] - wide_end) * (1.0 / HALF)
        rhs_start = push_start + spectrum * wide_start
        rhs_end = push_end + spectrum * wide_end
        total0 = known_ref[0] + field_ref[1] + spectrum * field_ref[0]
        total1 = known_ref[1] + field_ref[1] + spectrum * known_ref[3]
        total2 = known_ref[2] + field_ref[1] + spectrum * known_ref[4]
        shared = -HALF * spectrum * (known_ref[3] - 0.5 * (wide_start + wide_end)) + STEP * (
            (5.0 / 24.0) * total0 + (1.0 / 3.0) * total1 - (1.0 / 24.0) * total2 - 0.375 * rhs_start - 0.125 * rhs_end
        )
        const_ref[0] = field_ref[0] - wide_start + shared
        const_ref[1] = known_ref[4] - wide_end + HALF * (known_ref[2] - push_end - known_ref[0] + push_start) + shared
        const_ref[2] = (
            -HALF * (known_ref[1] - 0.5 * (push_start + push_end))
            - HALF * spectrum * (known_ref[4] - wide_end)
            + STEP
            * (
                (-1.0 / 24.0) * total0
                + (1.0 / 3.0) * total1
                + (5.0 / 24.0) * total2
                - 0.125 * rhs_start
                - 0.375 * rhs_end
            )
        )
        coarse_known = [known_ref[n, :, :RADIAL_C, :AXIAL_C] for n in (0, 2)]
        gain_ref[8] = STEP * (forcing_c + (coarse_known[0] - push_ref[0]) / 6.0)
        gain_ref[9] = STEP * (forcing_c + (coarse_known[1] - push_ref[9]) / 6.0)
        return
        yield

    def sweep(places, kinds):
        middles = [
            inverse_ref[...] * (const_ref[kind] + ahead_ref[n] + behind_ref[n + 1])
            for n, kind in zip(places, kinds)
        ]
        middle_pushes = yield from explicit(middles)
        endings = [
            inverse_ref[...] * (middle + HALF * push + const_ref[2] + behind_ref[n + 1] - behind_ref[n])
            for n, middle, push in zip(places, middles, middle_pushes)
        ]
        ending_pushes = yield from restricted_explicit(endings)
        spectrum_c = spectrum_ref[:RADIAL_C, :AXIAL_C]
        for at, n in enumerate(places):
            middle, ending = middles[at], endings[at]
            gain_ref[n] = (
                gain_ref[8 + kinds[at]]
                + (STEP / 6.0) * (push_ref[n] + spectrum_c * coarse_ref[n])
                + (STEP * 2.0 / 3.0) * (corner(middle_pushes[at]) + spectrum_c * corner(middle))
                + (STEP / 6.0) * ending_pushes[at]
                - (STEP * 5.0 / 6.0) * spectrum_c * corner(ending)
            )
            for part in range(2):
                for half in range(2):
                    for j in range(0 if half else 3, 6):
                        out_ref[n, pl.ds(part * 12 + half * 6 + j, 16, stride=24), :] = ending[
                            part, 16 * j : 16 * j + 16, half * 128 : half * 128 + 128
                        ]

    def chain_again(places):
        for n in places:
            state = state_ref[...]
            push = yield from coarse_explicit(state - coarse_ref[n])
            after = inverse_c_ref[...] * (gain_ref[n] + state + STEP * push)
            state_ref[...] = after
            for part in range(2):
                for j in range(3):
                    out_ref[n, pl.ds(part * 12 + j, 16, stride=24), :] = after[part, 16 * j : 16 * j + 16, :]

    def chaining(n):
        return ["S%d" % (n - 1)], ["S%d" % n], chain(n)

    def spreading(*places):
        return ["S%d" % n for n in places], ["E%d" % n for n in places], spread(places)

    def sweeping(*places):
        needs = ["E%d" % n for n in range(places[0], places[-1] + 2)] + ["constants"]
        return needs, ["J%d" % n for n in places], sweep(places, [min(n, 1) for n in places])

    def chaining_again(n):
        return ["J%d" % n, "T%d" % n], ["T%d" % (n + 1)], chain_again([n])

    state_ref[...] = coarse_ref[0]
    done.update(["S0", "T0"])
    side_by_side(
        ([], ["first", "S1"], first_iteration()),
        *[chaining(n) for n in range(2, 9)],
        *[chaining_again(n) for n in range(8)],
        spreading(0),
        spreading(9),
        (["first", "E0", "E9"], ["constants"], constants()),
        *[spreading(n) for n in range(1, 9)],
        *[sweeping(n) for n in range(8)],
    )


def from_units_kernel(transform_ref, received_ref, send_ref):
    for pair in range(6):
        parts = []
        for part in range(2):
            parts.append(
                jnp.concatenate(
                    [received_ref[pl.ds(part * 12 + 2 * pair + n, UNITS, stride=24), :] for n in range(2)], axis=1
                )
            )
        planes = radial(transform_ref[...], jnp.concatenate(parts, axis=0))
        for n in range(2):
            send_ref[pl.ds(2 * pair + n, 192, stride=12), :] = planes[:, n * 128 : n * 128 + 128]


def place_kernel(received_ref, out_ref, planes_ref, sems):
    def copy(group):
        own = pl.ds(3 * group, 3)
        return pltpu.make_async_copy(planes_ref.at[own], out_ref.at[own], sems.at[group])

    for plane in range(12):
        for half in range(2):
            for j in range(6):
                planes_ref[plane, 16 * j : 16 * j + 16, half * 128 : half * 128 + 128] = received_ref[
                    pl.ds(plane * 12 + half * 6 + j, 16, stride=144), :
                ]
        if plane % 3 == 2:
            copy(plane // 3).start()
    for group in range(4):
        copy(group).wait()


VMEM = pl.BlockSpec(memory_space=pltpu.VMEM)
HBM = pl.BlockSpec(memory_space=pltpu.HBM)
SMEM = pl.BlockSpec(memory_space=pltpu.SMEM)


def params(mib):
    return pltpu.CompilerParams(vmem_limit_bytes=mib << 20)


def array(*shape):
    return jax.ShapeDtypeStruct(shape, F32)


def exchange(value, axes, peers):
    rows = value.shape[0] // peers
    moved = lax.all_to_all(value.reshape(peers, rows, 128), axes, 0, 0)
    return moved.reshape(value.shape)


def per_device(
    initial_state,
    forcing,
    forward_radial,
    backward_radial,
    forward_axial,
    backward_axial,
    forward_radial_coarse,
    backward_radial_coarse,
    forward_axial_coarse,
    backward_axial_coarse,
    decay_radial,
    decay_axial,
    advection,
    diffusion,
):
    operators = pl.pallas_call(
        operators_kernel,
        out_shape=[jax.ShapeDtypeStruct(shape, kind) for _, shape, kind in OPERATORS],
        in_specs=[SMEM] + [VMEM] * 12,
        out_specs=[VMEM] * len(OPERATORS),
        compiler_params=params(8),
        name="operators",
    )(
        jnp.asarray(SCALARS),
        forward_radial,
        backward_radial,
        forward_axial,
        backward_axial,
        forward_radial_coarse,
        backward_radial_coarse,
        forward_axial_coarse,
        backward_axial_coarse,
        decay_radial.reshape(1, RADIAL),
        decay_axial.reshape(1, AXIAL),
        advection,
        diffusion.reshape(1, RADIAL),
    )
    send = pl.pallas_call(
        gather_kernel,
        out_shape=array(BLOCKS * 40, 128),
        in_specs=[HBM, HBM],
        out_specs=VMEM,
        scratch_shapes=[pltpu.VMEM((12, 24, AXIAL), F32), pltpu.SemaphoreType.DMA((4,))],
        compiler_params=params(4),
        name="gather_points",
    )(
        *[
            pltpu.with_memory_space_constraint(field.reshape(12, RADIAL, AXIAL), pltpu.HBM)
            for field in (initial_state, forcing)
        ]
    )
    received = exchange(send, "azim", BLOCKS)
    received = received.reshape(BLOCKS, 40, 128)[:, :36].reshape(BLOCKS * 36, 128)
    send = pl.pallas_call(
        to_units_kernel,
        out_shape=array(128 * 8, 128),
        in_specs=[VMEM, VMEM],
        out_specs=VMEM,
        compiler_params=params(4),
        name="to_units",
    )(jnp.asarray(TO_UNITS), received)
    received = exchange(send, ("tm", "azim"), 128)

    fine, coarse = (2, RADIAL, AXIAL), (2, RADIAL_C, AXIAL_C)
    send = pl.pallas_call(
        units_kernel,
        out_shape=array(SLICES, 16 * 24, 128),
        in_specs=[VMEM] * (1 + len(OPERATORS)),
        out_specs=VMEM,
        scratch_shapes=[
            pltpu.VMEM((2,) + fine, F32),
            pltpu.VMEM((10,) + coarse, F32),
            pltpu.VMEM((10,) + coarse, F32),
            pltpu.VMEM((10,) + fine, F32),
            pltpu.VMEM((10,) + fine, F32),
            pltpu.VMEM((5,) + fine, F32),
            pltpu.VMEM((3,) + fine, F32),
            pltpu.VMEM((11,) + coarse, F32),
            pltpu.VMEM(coarse, F32),
        ],
        compiler_params=params(28),
        name="units",
    )(received, *operators)
    received = exchange(send.reshape(128 * 24, 128), ("tm", "azim"), 128)
    send = pl.pallas_call(
        from_units_kernel,
        out_shape=array(BLOCKS * 144, 128),
        in_specs=[VMEM, VMEM],
        out_specs=VMEM,
        compiler_params=params(8),
        name="from_units",
    )(jnp.asarray(FROM_UNITS), received)
    received = exchange(send, "azim", BLOCKS)
    planes = pl.pallas_call(
        place_kernel,
        out_shape=array(12, RADIAL, AXIAL),
        in_specs=[VMEM],
        out_specs=HBM,
        scratch_shapes=[pltpu.VMEM((12, RADIAL, AXIAL), F32), pltpu.SemaphoreType.DMA((4,))],
        compiler_params=params(6),
        name="place",
    )(received)
    return planes.reshape(1, 3, 4, RADIAL, AXIAL)


def solution(mesh):
    split_planes = P(None, "azim", None, None)
    return jax.shard_map(
        per_device,
        mesh=mesh,
        in_specs=(split_planes, split_planes) + (P(),) * 12,
        out_specs=P("tm", None, "azim", None, None),
        check_vma=False,
    )
```

```python
import ml_dtypes
import numpy as np
import jax
import jax.numpy as jnp
from jax import lax
from jax.experimental import pallas as pl
from jax.experimental.pallas import tpu as pltpu
from jax.sharding import PartitionSpec as P

SLICES = 8
AZIMUTH = 64
RADIAL, AXIAL = 96, 256
RADIAL_C, AXIAL_C = 48, 128
BLOCKS = 16
UNITS = 96
STEP = 0.1
HALF = 0.05
F32 = jnp.float32
BF16 = jnp.bfloat16


def azimuth_transform():
    points = np.arange(AZIMUTH)
    rows = np.zeros((2, UNITS, 3, AZIMUTH))
    scalars = np.zeros((128, 4))
    for k in range(64):
        angle = 2.0 * np.pi * k / AZIMUTH
        cos, sin = np.cos(angle * points) / 8.0, np.sin(angle * points) / 8.0
        rows[0, k, 0], rows[0, k, 1] = cos, sin
        rows[1, k, 1], rows[1, k, 0] = cos, -sin
        second = 2.0 * np.cos(angle) - 2.0
        scalars[k] = (second, second, 2.0 * np.sin(angle), -2.0)
    rows[0, 64, 2] = 1.0 / 8.0
    rows[1, 64, 2] = (-1.0) ** points / 8.0
    scalars[64] = (0.0, -4.0, 0.0, 0.0)
    for k in range(1, 32):
        angle = 2.0 * np.pi * k / AZIMUTH
        rows[0, 64 + k, 2] = np.sqrt(2.0) * np.cos(angle * points) / 8.0
        rows[1, 64 + k, 2] = -np.sqrt(2.0) * np.sin(angle * points) / 8.0
        second = 2.0 * np.cos(angle) - 2.0
        scalars[64 + k] = (second, second, 2.0 * np.sin(angle), 0.0)
    matrix = rows.reshape(192, 3, BLOCKS, 4).transpose(0, 2, 1, 3).reshape(192, 192)
    return matrix, scalars.astype(np.float32)


def split_constant(matrix):
    single = matrix.astype(np.float32)
    high = single.astype(ml_dtypes.bfloat16)
    low = (single - high.astype(np.float32)).astype(ml_dtypes.bfloat16)
    return np.concatenate([high, high, low], axis=1)


TRANSFORM, SCALARS = azimuth_transform()
TO_UNITS = split_constant(TRANSFORM)
FROM_UNITS = split_constant(TRANSFORM.T.copy())


def split(value):
    high = value.astype(BF16)
    return high, (value - high.astype(F32)).astype(BF16)


def dot(left, right):
    return jnp.dot(left, right, preferred_element_type=F32)


def axial(value, weights):
    high, low = split(value)
    depth = weights.shape[0] // 3
    products = dot(jnp.concatenate([high, low], axis=0), weights[:depth])
    return products[: value.shape[0]] + products[value.shape[0] :] + dot(high, weights[2 * depth :])


def radial(weights, value):
    high, low = split(value)
    return dot(weights, jnp.concatenate([high, low, high], axis=0))


def radial_stacked(weights, value):
    products = dot(weights, jnp.concatenate(split(value), axis=0))
    half = weights.shape[0] // 2
    return products[:half] + products[half:]


def gather_kernel(initial_ref, forcing_ref, send_ref, block_ref, sems):
    tm = lax.axis_index("tm")
    rows = pl.ds(pl.multiple_of((tm % 4) * 24, 8), 24)

    def copies(source_ref):
        for group in range(4):
            own = pl.ds(3 * group, 3)
            yield pltpu.make_async_copy(source_ref.at[own, rows, :], block_ref.at[own], sems.at[group])

    @pl.when(tm < 4)
    def _():
        for copy in copies(initial_ref):
            copy.start()

    @pl.when(tm >= 4)
    def _():
        for copy in copies(forcing_ref):
            copy.start()

    waits = list(copies(initial_ref))
    for plane in range(12):
        if plane % 3 == 0:
            waits[plane // 3].wait()
        for piece in range(6):
            half, row = piece // 3, (piece % 3) * 8
            values = block_ref[plane, row : row + 8, half * 128 : half * 128 + 128]
            group, first = piece // 2, (piece % 2) * 8
            send_ref[pl.ds(first * 40 + plane * 3 + group, 8, stride=40), :] = values


def to_units_kernel(transform_ref, received_ref, send_ref):
    columns = [received_ref[pl.ds(group, 192, stride=3), :] for group in range(3)]
    send_ref[UNITS * 8 :, :] = jnp.zeros((32 * 8, 128), F32)
    zero = jnp.zeros((UNITS, 128), F32)
    send_ref[pl.ds(6, UNITS, stride=8), :] = zero
    send_ref[pl.ds(7, UNITS, stride=8), :] = zero
    for group in range(3):
        units = radial(transform_ref[...], columns[group])
        for part in range(2):
            send_ref[pl.ds(part * 3 + group, UNITS, stride=8), :] = units[part * UNITS : (part + 1) * UNITS]


def column_of(row, size):
    at = lax.broadcasted_iota(jnp.int32, (size, size), 0) == lax.broadcasted_iota(jnp.int32, (size, size), 1)
    return jnp.sum(jnp.where(at, row, 0.0), axis=1, keepdims=True)


def identity_plus(value):
    size = value.shape[0]
    at = lax.broadcasted_iota(jnp.int32, (size, size), 0) == lax.broadcasted_iota(jnp.int32, (size, size), 1)
    return jnp.where(at, 1.0, 0.0) + value


def axial_weights(value):
    high, low = split(jnp.transpose(identity_plus(value)))
    return jnp.concatenate([high, high, low], axis=0)


def radial_weights(value):
    high, low = split(value)
    return jnp.concatenate([high, high, low], axis=1)


def stacked_weights(value):
    high, low = split(value)
    return jnp.concatenate(
        [jnp.concatenate([high, high], axis=1), jnp.concatenate([low, jnp.zeros_like(low)], axis=1)], axis=0
    )


OPERATORS = (
    ("axial", (6 * AXIAL, AXIAL), BF16),
    ("radial", (4 * RADIAL, 2 * RADIAL), BF16),
    ("axial_c", (6 * AXIAL_C, AXIAL_C), BF16),
    ("radial_c", (RADIAL + 2 * RADIAL_C, 3 * RADIAL_C), BF16),
    ("point", (5 * RADIAL, AXIAL), F32),
    ("point_c", (4 * RADIAL_C, AXIAL_C), F32),
)


def views(axial_ref, radial_ref, axial_c_ref, radial_c_ref, point_ref, point_c_ref):
    def parts(ref, *sizes):
        ends = np.cumsum(sizes)
        return [ref.at[int(end - size) : int(end), :] for size, end in zip(sizes, ends)]

    return (
        parts(axial_ref, *[3 * AXIAL] * 2)
        + parts(radial_ref, *[2 * RADIAL] * 2)
        + parts(axial_c_ref, *[3 * AXIAL_C] * 2)
        + parts(radial_c_ref, RADIAL, RADIAL_C, RADIAL_C)
        + parts(point_ref, *[RADIAL] * 5)
        + parts(point_c_ref, *[RADIAL_C] * 4)
    )


def operators_kernel(
    scalars_ref,
    forward_radial_ref,
    backward_radial_ref,
    forward_axial_ref,
    backward_axial_ref,
    forward_radial_c_ref,
    backward_radial_c_ref,
    forward_axial_c_ref,
    backward_axial_c_ref,
    decay_radial_ref,
    decay_axial_ref,
    advection_ref,
    diffusion_ref,
    *operator_refs,
):
    all_views = views(*operator_refs)
    (bz_ref, fz_ref, br_ref, fr_ref, bzc_ref, fzc_ref, br_narrow_ref, brc_ref, frc_ref) = all_views[:9]
    (cross_ref, first_ref, second_ref, spectrum_ref, inverse_ref) = all_views[9:14]
    (cross_c_ref, first_c_ref, second_c_ref, inverse_c_ref) = all_views[14:]
    unit = lax.axis_index("tm") * BLOCKS + lax.axis_index("azim")
    scalar = [scalars_ref[unit, n] for n in range(4)]

    bz_ref[...] = axial_weights(backward_axial_ref[...])
    fz_ref[...] = axial_weights(forward_axial_ref[...])
    br_ref[...] = stacked_weights(identity_plus(backward_radial_ref[...]))
    fr_ref[...] = stacked_weights(identity_plus(forward_radial_ref[...]))
    bzc_ref[...] = axial_weights(backward_axial_c_ref[...])
    fzc_ref[...] = axial_weights(forward_axial_c_ref[...])
    brc_ref[...] = radial_weights(identity_plus(backward_radial_c_ref[...]))
    frc_ref[...] = radial_weights(identity_plus(forward_radial_c_ref[...]))
    br_narrow_ref[...] = radial_weights(identity_plus(backward_radial_ref[...])[:, :RADIAL_C])

    diffusion = column_of(diffusion_ref[...], RADIAL)
    cross_ref[...] = scalar[2] * advection_ref[...] + scalar[3]
    first_ref[...] = jnp.broadcast_to(scalar[0] * diffusion, (RADIAL, AXIAL))
    second_ref[...] = jnp.broadcast_to(scalar[1] * diffusion, (RADIAL, AXIAL))
    pick_lane = jnp.where(
        lax.broadcasted_iota(jnp.int32, (AXIAL, AXIAL_C), 0)
        == 2 * lax.broadcasted_iota(jnp.int32, (AXIAL, AXIAL_C), 1),
        1.0,
        0.0,
    )
    pick_row = jnp.where(
        lax.broadcasted_iota(jnp.int32, (RADIAL_C, RADIAL), 1)
        == 2 * lax.broadcasted_iota(jnp.int32, (RADIAL_C, RADIAL), 0),
        1.0,
        0.0,
    )
    exact = lax.Precision.HIGHEST
    advection_c = jnp.dot(
        jnp.dot(pick_row, advection_ref[...], precision=exact, preferred_element_type=F32),
        pick_lane,
        precision=exact,
        preferred_element_type=F32,
    )
    diffusion_c = jnp.sum(pick_row * diffusion_ref[...], axis=1, keepdims=True)
    cross_c_ref[...] = scalar[2] * advection_c + scalar[3]
    first_c_ref[...] = jnp.broadcast_to(scalar[0] * diffusion_c, (RADIAL_C, AXIAL_C))
    second_c_ref[...] = jnp.broadcast_to(scalar[1] * diffusion_c, (RADIAL_C, AXIAL_C))
    spectrum = -(column_of(decay_radial_ref[...], RADIAL) + decay_axial_ref[...])
    spectrum_ref[...] = spectrum
    inverse_ref[...] = 1.0 / (1.0 - HALF * spectrum)
    inverse_c_ref[...] = 1.0 / (1.0 - STEP * spectrum[:RADIAL_C, :AXIAL_C])


def units_kernel(
    received_ref,
    axial_ref,
    radial_ref,
    axial_c_ref,
    radial_c_ref,
    point_ref,
    point_c_ref,
    out_ref,
    field_ref,
    coarse_ref,
    push_ref,
    ahead_ref,
    behind_ref,
    known_ref,
    const_ref,
    gain_ref,
    state_ref,
):
    all_views = views(axial_ref, radial_ref, axial_c_ref, radial_c_ref, point_ref, point_c_ref)
    (bz_ref, fz_ref, br_ref, fr_ref, bzc_ref, fzc_ref, br_narrow_ref, brc_ref, frc_ref) = all_views[:9]
    (cross_ref, first_ref, second_ref, spectrum_ref, inverse_ref) = all_views[9:14]
    (cross_c_ref, first_c_ref, second_c_ref, inverse_c_ref) = all_views[14:]

    for field in range(2):
        for part in range(2):
            for rows in range(4):
                source = (field * 4 + rows) * 16 * 8 + part * 3
                for piece in range(6):
                    half, row = piece // 3, (piece % 3) * 8
                    group, first = piece // 2, (piece % 2) * 8
                    field_ref[field, part, rows * 24 + row : rows * 24 + row + 8, half * 128 : half * 128 + 128] = (
                        received_ref[pl.ds(source + first * 8 + group, 8, stride=8), :]
                    )

    def forces(re, im, cross, first, second):
        return first * re - cross * im, second * im + cross * re

    def blocks(rows, size):
        return [rows[n : n + size] for n in range(0, rows.shape[0], size)]

    def fine_forces(planes):
        moved = []
        for n in range(0, len(planes), 2):
            moved += forces(planes[n], planes[n + 1], cross_ref[...], first_ref[...], second_ref[...])
        return moved

    def flat(states):
        return jnp.concatenate([state.reshape(-1, state.shape[-1]) for state in states], axis=0)

    def pairs(planes):
        return [jnp.stack(planes[n : n + 2]) for n in range(0, len(planes), 2)]

    def to_points(states):
        inner = []
        for plane in blocks(flat(states), RADIAL):
            inner.append(axial(plane, bz_ref[...]))
            yield
        planes = []
        for plane in inner:
            planes.append(radial_stacked(br_ref[...], plane))
            yield
        return planes

    def to_modes(planes):
        inner = []
        for plane in planes:
            inner.append(axial(plane, fz_ref[...]))
            yield
        planes = []
        for plane in inner:
            planes.append(radial_stacked(fr_ref[...], plane))
            yield
        return pairs(planes)

    def explicit(states):
        planes = yield from to_points(states)
        return (yield from to_modes(fine_forces(planes)))

    def explicit_of_coarse(states):
        narrow = jnp.concatenate([bz_ref[n * AXIAL : n * AXIAL + AXIAL_C, :] for n in range(3)], axis=0)
        inner = axial(flat(states), narrow)
        yield
        planes = []
        for plane in blocks(inner, RADIAL_C):
            planes.append(radial(br_narrow_ref[...], plane))
            yield
        return (yield from to_modes(fine_forces(planes)))

    def restricted_explicit(states):
        planes = fine_forces((yield from to_points(states)))
        rows = jnp.concatenate([fr_ref[:RADIAL_C, :], fr_ref[RADIAL : RADIAL + RADIAL_C, :]], axis=0)
        narrow = []
        for plane in planes:
            narrow.append(radial_stacked(rows, plane))
            yield
        inner = axial(jnp.concatenate(narrow, axis=0), fz_ref[:, :AXIAL_C])
        yield
        return pairs(blocks(inner, RADIAL_C))

    def coarse_explicit(modes):
        inner = axial(modes.reshape(2 * RADIAL_C, AXIAL_C), bzc_ref[...])
        yield
        both = radial(brc_ref[...], jnp.concatenate([inner[:RADIAL_C], inner[RADIAL_C:]], axis=1))
        yield
        re, im = forces(
            both[:, :AXIAL_C], both[:, AXIAL_C:], cross_c_ref[...], first_c_ref[...], second_c_ref[...]
        )
        both = radial(frc_ref[...], jnp.concatenate([re, im], axis=1))
        yield
        inner = axial(jnp.concatenate([both[:, :AXIAL_C], both[:, AXIAL_C:]], axis=0), fzc_ref[...])
        yield
        return inner.reshape(2, RADIAL_C, AXIAL_C)

    done = set()

    def side_by_side(*tasks):
        waiting = list(tasks)
        while waiting:
            ready = [task for task in waiting if all(need in done for need in task[0])]
            for task in reversed(ready):
                try:
                    next(task[2])
                except StopIteration:
                    done.update(task[1])
                    waiting.remove(task)

    def corner(value):
        return value[:, :RADIAL_C, :AXIAL_C]

    spectrum_c = spectrum_ref[:RADIAL_C, :AXIAL_C]
    start_c = field_ref[0, :, :RADIAL_C, :AXIAL_C]
    forcing_c = field_ref[1, :, :RADIAL_C, :AXIAL_C]
    coarse_ref[0] = start_c

    def first_iteration():
        known_ref[0] = (yield from explicit([field_ref[0]]))[0]
        spectrum = spectrum_ref[...]
        total0 = known_ref[0] + field_ref[1] + spectrum * field_ref[0]
        known_ref[3] = inverse_ref[...] * (field_ref[0] - HALF * spectrum * field_ref[0] + (0.5 * STEP) * total0)
        known_ref[1] = (yield from explicit([known_ref[3]]))[0]
        known_ref[4] = inverse_ref[...] * (
            known_ref[3]
            + HALF * (known_ref[1] - known_ref[0])
            - HALF * spectrum_ref[...] * field_ref[0]
            + (0.5 * STEP) * (known_ref[0] + field_ref[1] + spectrum_ref[...] * field_ref[0])
        )
        coarse_ref[9] = known_ref[4, :, :RADIAL_C, :AXIAL_C]
        done.add("S9")
        known_ref[2] = (yield from explicit([known_ref[4]]))[0]
        coarse_known = [known_ref[n, :, :RADIAL_C, :AXIAL_C] for n in range(5)]
        gain_ref[0] = (
            STEP
            * (
                (coarse_known[0] + spectrum_c * start_c) / 6.0
                + (2.0 / 3.0) * (coarse_known[1] + spectrum_c * coarse_known[3])
                + (coarse_known[2] + spectrum_c * coarse_known[4]) / 6.0
                + forcing_c
            )
            - STEP * spectrum_c * coarse_known[4]
        )
        coarse_ref[1] = inverse_c_ref[...] * (gain_ref[0] + start_c)
        gain_ref[10] = gain_ref[0]


    def chain(*places):
        for n in places:
            latest = coarse_ref[n - 1]
            push = yield from coarse_explicit(latest - coarse_ref[0])
            coarse_ref[n] = inverse_c_ref[...] * (gain_ref[10] + latest + STEP * push)

    def spread(places):
        states = [coarse_ref[n] for n in places]
        pushes = yield from explicit_of_coarse(states)
        damping = (0.25 * HALF) * spectrum_ref[:RADIAL_C, :AXIAL_C]
        for n, state, push in zip(places, states, pushes):
            push_ref[n] = corner(push)
            behind_ref[n] = (0.25 * HALF) * push
            ahead_ref[n] = (0.75 * HALF) * push
            damped = damping * state
            behind_ref[n, :, :RADIAL_C, :AXIAL_C] = (0.25 * HALF) * corner(push) - damped
            ahead_ref[n, :, :RADIAL_C, :AXIAL_C] = (0.75 * HALF) * corner(push) + damped + state

    def padded(value):
        return jnp.pad(value, ((0, 0), (0, RADIAL - RADIAL_C), (0, AXIAL - AXIAL_C)))

    def constants():
        spectrum = spectrum_ref[...]
        wide_start = padded(coarse_ref[0])
        wide_end = padded(coarse_ref[9])
        push_start = (ahead_ref[0] + behind_ref[0] - wide_start) * (1.0 / HALF)
        push_end = (ahead_ref[9] + behind_ref[9] - wide_end) * (1.0 / HALF)
        rhs_start = push_start + spectrum * wide_start
        rhs_end = push_end + spectrum * wide_end
        total0 = known_ref[0] + field_ref[1] + spectrum * field_ref[0]
        total1 = known_ref[1] + field_ref[1] + spectrum * known_ref[3]
        total2 = known_ref[2] + field_ref[1] + spectrum * known_ref[4]
        shared = -HALF * spectrum * (known_ref[3] - 0.5 * (wide_start + wide_end)) + STEP * (
            (5.0 / 24.0) * total0 + (1.0 / 3.0) * total1 - (1.0 / 24.0) * total2 - 0.375 * rhs_start - 0.125 * rhs_end
        )
        const_ref[0] = field_ref[0] - wide_start + shared
        const_ref[1] = known_ref[4] - wide_end + HALF * (known_ref[2] - push_end - known_ref[0] + push_start) + shared
        const_ref[2] = (
            -HALF * (known_ref[1] - 0.5 * (push_start + push_end))
            - HALF * spectrum * (known_ref[4] - wide_end)
            + STEP
            * (
                (-1.0 / 24.0) * total0
                + (1.0 / 3.0) * total1
                + (5.0 / 24.0) * total2
                - 0.125 * rhs_start
                - 0.375 * rhs_end
            )
        )
        coarse_known = [known_ref[n, :, :RADIAL_C, :AXIAL_C] for n in (0, 2)]
        gain_ref[8] = STEP * (forcing_c + (coarse_known[0] - push_ref[0]) / 6.0)
        gain_ref[9] = STEP * (forcing_c + (coarse_known[1] - push_ref[9]) / 6.0)
        return
        yield

    def sweep(places, kinds):
        middles = [
            inverse_ref[...] * (const_ref[kind] + ahead_ref[n] + behind_ref[n + 1])
            for n, kind in zip(places, kinds)
        ]
        middle_pushes = yield from explicit(middles)
        endings = [
            inverse_ref[...] * (middle + HALF * push + const_ref[2] + behind_ref[n + 1] - behind_ref[n])
            for n, middle, push in zip(places, middles, middle_pushes)
        ]
        ending_pushes = yield from restricted_explicit(endings)
        spectrum_c = spectrum_ref[:RADIAL_C, :AXIAL_C]
        for at, n in enumerate(places):
            middle, ending = middles[at], endings[at]
            gain_ref[n] = (
                gain_ref[8 + kinds[at]]
                + (STEP / 6.0) * (push_ref[n] + spectrum_c * coarse_ref[n])
                + (STEP * 2.0 / 3.0) * (corner(middle_pushes[at]) + spectrum_c * corner(middle))
                + (STEP / 6.0) * ending_pushes[at]
                - (STEP * 5.0 / 6.0) * spectrum_c * corner(ending)
            )
            for part in range(2):
                for half in range(2):
                    for j in range(0 if half else 3, 6):
                        out_ref[n, pl.ds(part * 12 + half * 6 + j, 16, stride=24), :] = ending[
                            part, 16 * j : 16 * j + 16, half * 128 : half * 128 + 128
                        ]

    def chain_again(places):
        for n in places:
            state = state_ref[...]
            push = yield from coarse_explicit(state - coarse_ref[n])
            after = inverse_c_ref[...] * (gain_ref[n] + state + STEP * push)
            state_ref[...] = after
            for part in range(2):
                for j in range(3):
                    out_ref[n, pl.ds(part * 12 + j, 16, stride=24), :] = after[part, 16 * j : 16 * j + 16, :]

    def chaining(n):
        return ["S%d" % (n - 1)], ["S%d" % n], chain(n)

    def spreading(*places):
        return ["S%d" % n for n in places], ["E%d" % n for n in places], spread(places)

    def sweeping(*places):
        needs = ["E%d" % n for n in range(places[0], places[-1] + 2)] + ["constants"]
        return needs, ["J%d" % n for n in places], sweep(places, [min(n, 1) for n in places])

    def chaining_again(n):
        return ["J%d" % n, "T%d" % n], ["T%d" % (n + 1)], chain_again([n])

    state_ref[...] = coarse_ref[0]
    done.update(["S0", "T0"])
    side_by_side(
        ([], ["first", "S1"], first_iteration()),
        *[chaining(n) for n in range(2, 9)],
        *[chaining_again(n) for n in range(8)],
        spreading(0),
        spreading(9),
        (["first", "E0", "E9"], ["constants"], constants()),
        *[spreading(n) for n in range(1, 9)],
        *[sweeping(n) for n in range(8)],
    )


def from_units_kernel(transform_ref, received_ref, send_ref):
    for pair in range(6):
        parts = []
        for part in range(2):
            parts.append(
                jnp.concatenate(
                    [received_ref[pl.ds(part * 12 + 2 * pair + n, UNITS, stride=24), :] for n in range(2)], axis=1
                )
            )
        planes = radial(transform_ref[...], jnp.concatenate(parts, axis=0))
        for n in range(2):
            send_ref[pl.ds(2 * pair + n, 192, stride=12), :] = planes[:, n * 128 : n * 128 + 128]


def place_kernel(received_ref, out_ref, planes_ref, sems):
    def copy(group):
        own = pl.ds(3 * group, 3)
        return pltpu.make_async_copy(planes_ref.at[own], out_ref.at[own], sems.at[group])

    for plane in range(12):
        for half in range(2):
            for j in range(6):
                planes_ref[plane, 16 * j : 16 * j + 16, half * 128 : half * 128 + 128] = received_ref[
                    pl.ds(plane * 12 + half * 6 + j, 16, stride=144), :
                ]
        if plane % 3 == 2:
            copy(plane // 3).start()
    for group in range(4):
        copy(group).wait()


VMEM = pl.BlockSpec(memory_space=pltpu.VMEM)
HBM = pl.BlockSpec(memory_space=pltpu.HBM)
SMEM = pl.BlockSpec(memory_space=pltpu.SMEM)


def params(mib):
    return pltpu.CompilerParams(vmem_limit_bytes=mib << 20)


def array(*shape):
    return jax.ShapeDtypeStruct(shape, F32)


def exchange(value, axes, peers):
    rows = value.shape[0] // peers
    moved = lax.all_to_all(value.reshape(peers, rows, 128), axes, 0, 0)
    return moved.reshape(value.shape)


def per_device(
    initial_state,
    forcing,
    forward_radial,
    backward_radial,
    forward_axial,
    backward_axial,
    forward_radial_coarse,
    backward_radial_coarse,
    forward_axial_coarse,
    backward_axial_coarse,
    decay_radial,
    decay_axial,
    advection,
    diffusion,
):
    operators = pl.pallas_call(
        operators_kernel,
        out_shape=[jax.ShapeDtypeStruct(shape, kind) for _, shape, kind in OPERATORS],
        in_specs=[SMEM] + [VMEM] * 12,
        out_specs=[VMEM] * len(OPERATORS),
        compiler_params=params(8),
        name="operators",
    )(
        jnp.asarray(SCALARS),
        forward_radial,
        backward_radial,
        forward_axial,
        backward_axial,
        forward_radial_coarse,
        backward_radial_coarse,
        forward_axial_coarse,
        backward_axial_coarse,
        decay_radial.reshape(1, RADIAL),
        decay_axial.reshape(1, AXIAL),
        advection,
        diffusion.reshape(1, RADIAL),
    )
    send = pl.pallas_call(
        gather_kernel,
        out_shape=array(BLOCKS * 40, 128),
        in_specs=[HBM, HBM],
        out_specs=VMEM,
        scratch_shapes=[pltpu.VMEM((12, 24, AXIAL), F32), pltpu.SemaphoreType.DMA((4,))],
        compiler_params=params(4),
        name="gather_points",
    )(
        *[
            pltpu.with_memory_space_constraint(field.reshape(12, RADIAL, AXIAL), pltpu.HBM)
            for field in (initial_state, forcing)
        ]
    )
    received = exchange(send, "azim", BLOCKS)
    received = received.reshape(BLOCKS, 40, 128)[:, :36].reshape(BLOCKS * 36, 128)
    send = pl.pallas_call(
        to_units_kernel,
        out_shape=array(128 * 8, 128),
        in_specs=[VMEM, VMEM],
        out_specs=VMEM,
        compiler_params=params(4),
        name="to_units",
    )(jnp.asarray(TO_UNITS), received)
    received = exchange(send, ("tm", "azim"), 128)

    fine, coarse = (2, RADIAL, AXIAL), (2, RADIAL_C, AXIAL_C)
    send = pl.pallas_call(
        units_kernel,
        out_shape=array(SLICES, 16 * 24, 128),
        in_specs=[VMEM] * (1 + len(OPERATORS)),
        out_specs=VMEM,
        scratch_shapes=[
            pltpu.VMEM((2,) + fine, F32),
            pltpu.VMEM((10,) + coarse, F32),
            pltpu.VMEM((10,) + coarse, F32),
            pltpu.VMEM((10,) + fine, F32),
            pltpu.VMEM((10,) + fine, F32),
            pltpu.VMEM((5,) + fine, F32),
            pltpu.VMEM((3,) + fine, F32),
            pltpu.VMEM((11,) + coarse, F32),
            pltpu.VMEM(coarse, F32),
        ],
        compiler_params=params(28),
        name="units",
    )(received, *operators)
    received = exchange(send.reshape(128 * 24, 128), ("tm", "azim"), 128)
    send = pl.pallas_call(
        from_units_kernel,
        out_shape=array(BLOCKS * 144, 128),
        in_specs=[VMEM, VMEM],
        out_specs=VMEM,
        compiler_params=params(8),
        name="from_units",
    )(jnp.asarray(FROM_UNITS), received)
    received = exchange(send, "azim", BLOCKS)
    planes = pl.pallas_call(
        place_kernel,
        out_shape=array(12, RADIAL, AXIAL),
        in_specs=[VMEM],
        out_specs=HBM,
        scratch_shapes=[pltpu.VMEM((12, RADIAL, AXIAL), F32), pltpu.SemaphoreType.DMA((4,))],
        compiler_params=params(6),
        name="place",
    )(received)
    return planes.reshape(1, 3, 4, RADIAL, AXIAL)


def solution(mesh):
    split_planes = P(None, "azim", None, None)
    return jax.shard_map(
        per_device,
        mesh=mesh,
        in_specs=(split_planes, split_planes) + (P(),) * 12,
        out_specs=P("tm", None, "azim", None, None),
        check_vma=False,
    )
```

```python
import ml_dtypes
import numpy as np
import jax
import jax.numpy as jnp
from jax import lax
from jax.experimental import pallas as pl
from jax.experimental.pallas import tpu as pltpu
from jax.sharding import PartitionSpec as P

SLICES = 8
AZIMUTH = 64
RADIAL, AXIAL = 96, 256
RADIAL_C, AXIAL_C = 48, 128
BLOCKS = 16
UNITS = 96
STEP = 0.1
HALF = 0.05
F32 = jnp.float32
BF16 = jnp.bfloat16


def azimuth_transform():
    points = np.arange(AZIMUTH)
    rows = np.zeros((2, UNITS, 3, AZIMUTH))
    scalars = np.zeros((128, 4))
    for k in range(64):
        angle = 2.0 * np.pi * k / AZIMUTH
        cos, sin = np.cos(angle * points) / 8.0, np.sin(angle * points) / 8.0
        rows[0, k, 0], rows[0, k, 1] = cos, sin
        rows[1, k, 1], rows[1, k, 0] = cos, -sin
        second = 2.0 * np.cos(angle) - 2.0
        scalars[k] = (second, second, 2.0 * np.sin(angle), -2.0)
    rows[0, 64, 2] = 1.0 / 8.0
    rows[1, 64, 2] = (-1.0) ** points / 8.0
    scalars[64] = (0.0, -4.0, 0.0, 0.0)
    for k in range(1, 32):
        angle = 2.0 * np.pi * k / AZIMUTH
        rows[0, 64 + k, 2] = np.sqrt(2.0) * np.cos(angle * points) / 8.0
        rows[1, 64 + k, 2] = -np.sqrt(2.0) * np.sin(angle * points) / 8.0
        second = 2.0 * np.cos(angle) - 2.0
        scalars[64 + k] = (second, second, 2.0 * np.sin(angle), 0.0)
    matrix = rows.reshape(192, 3, BLOCKS, 4).transpose(0, 2, 1, 3).reshape(192, 192)
    return matrix, scalars.astype(np.float32)


def split_constant(matrix):
    single = matrix.astype(np.float32)
    high = single.astype(ml_dtypes.bfloat16)
    low = (single - high.astype(np.float32)).astype(ml_dtypes.bfloat16)
    return np.concatenate([high, high, low], axis=1)


TRANSFORM, SCALARS = azimuth_transform()
TO_UNITS = split_constant(TRANSFORM)
FROM_UNITS = split_constant(TRANSFORM.T.copy())


def split(value):
    high = value.astype(BF16)
    return high, (value - high.astype(F32)).astype(BF16)


def dot(left, right):
    return jnp.dot(left, right, preferred_element_type=F32)


def axial(value, weights):
    high, low = split(value)
    depth = weights.shape[0] // 3
    products = dot(jnp.concatenate([high, low], axis=0), weights[:depth])
    return products[: value.shape[0]] + products[value.shape[0] :] + dot(high, weights[2 * depth :])


def radial(weights, value):
    high, low = split(value)
    return dot(weights, jnp.concatenate([high, low, high], axis=0))


def radial_stacked(weights, value):
    products = dot(weights, jnp.concatenate(split(value), axis=0))
    half = weights.shape[0] // 2
    return products[:half] + products[half:]


def gather_kernel(initial_ref, forcing_ref, send_ref, block_ref, sems):
    tm = lax.axis_index("tm")
    rows = pl.ds(pl.multiple_of((tm % 4) * 24, 8), 24)

    def copies(source_ref):
        for group in range(4):
            own = pl.ds(3 * group, 3)
            yield pltpu.make_async_copy(source_ref.at[own, rows, :], block_ref.at[own], sems.at[group])

    @pl.when(tm < 4)
    def _():
        for copy in copies(initial_ref):
            copy.start()

    @pl.when(tm >= 4)
    def _():
        for copy in copies(forcing_ref):
            copy.start()

    waits = list(copies(initial_ref))
    for plane in range(12):
        if plane % 3 == 0:
            waits[plane // 3].wait()
        for piece in range(6):
            half, row = piece // 3, (piece % 3) * 8
            values = block_ref[plane, row : row + 8, half * 128 : half * 128 + 128]
            group, first = piece // 2, (piece % 2) * 8
            send_ref[pl.ds(first * 40 + plane * 3 + group, 8, stride=40), :] = values


def to_units_kernel(transform_ref, received_ref, out_ref, send_ref, sems):
    def copy(piece, first, size):
        own = pl.ds(first * 8, size * 8)
        return pltpu.make_async_copy(send_ref.at[own], out_ref.at[own], sems.at[piece])

    copies = [copy(0, UNITS, 128 - UNITS), copy(1, 0, UNITS // 2), copy(2, UNITS // 2, UNITS // 2)]
    send_ref[UNITS * 8 :, :] = jnp.zeros((32 * 8, 128), F32)
    copies[0].start()
    columns = jnp.concatenate([received_ref[pl.ds(group, 192, stride=3), :] for group in range(3)], axis=1)
    size = UNITS // 2
    zero = jnp.zeros((size, 128), F32)
    for half in range(2):
        rows = [transform_ref[part * UNITS + half * size : part * UNITS + half * size + size, :] for part in range(2)]
        units = radial(jnp.concatenate(rows, axis=0), columns)
        for row in range(8):
            part, group = row // 3, row % 3
            send_ref[pl.ds(half * size * 8 + row, size, stride=8), :] = (
                units[part * size : part * size + size, group * 128 : group * 128 + 128] if row < 6 else zero
            )
        copies[1 + half].start()
    for made in copies:
        made.wait()


def column_of(row, size):
    at = lax.broadcasted_iota(jnp.int32, (size, size), 0) == lax.broadcasted_iota(jnp.int32, (size, size), 1)
    return jnp.sum(jnp.where(at, row, 0.0), axis=1, keepdims=True)


def identity_plus(value):
    size = value.shape[0]
    at = lax.broadcasted_iota(jnp.int32, (size, size), 0) == lax.broadcasted_iota(jnp.int32, (size, size), 1)
    return jnp.where(at, 1.0, 0.0) + value


def axial_weights(value):
    high, low = split(jnp.transpose(identity_plus(value)))
    return jnp.concatenate([high, high, low], axis=0)


def radial_weights(value):
    high, low = split(value)
    return jnp.concatenate([high, high, low], axis=1)


def stacked_weights(value):
    high, low = split(value)
    return jnp.concatenate(
        [jnp.concatenate([high, high], axis=1), jnp.concatenate([low, jnp.zeros_like(low)], axis=1)], axis=0
    )


OPERATORS = (
    ("axial", (6 * AXIAL, AXIAL), BF16),
    ("radial", (4 * RADIAL, 2 * RADIAL), BF16),
    ("axial_c", (6 * AXIAL_C, AXIAL_C), BF16),
    ("radial_c", (RADIAL + 2 * RADIAL_C, 3 * RADIAL_C), BF16),
    ("point", (5 * RADIAL, AXIAL), F32),
    ("point_c", (4 * RADIAL_C, AXIAL_C), F32),
)


def views(axial_ref, radial_ref, axial_c_ref, radial_c_ref, point_ref, point_c_ref):
    def parts(ref, *sizes):
        ends = np.cumsum(sizes)
        return [ref.at[int(end - size) : int(end), :] for size, end in zip(sizes, ends)]

    return (
        parts(axial_ref, *[3 * AXIAL] * 2)
        + parts(radial_ref, *[2 * RADIAL] * 2)
        + parts(axial_c_ref, *[3 * AXIAL_C] * 2)
        + parts(radial_c_ref, RADIAL, RADIAL_C, RADIAL_C)
        + parts(point_ref, *[RADIAL] * 5)
        + parts(point_c_ref, *[RADIAL_C] * 4)
    )


def operators_kernel(
    scalars_ref,
    forward_radial_ref,
    backward_radial_ref,
    forward_axial_ref,
    backward_axial_ref,
    forward_radial_c_ref,
    backward_radial_c_ref,
    forward_axial_c_ref,
    backward_axial_c_ref,
    decay_radial_ref,
    decay_axial_ref,
    advection_ref,
    diffusion_ref,
    *operator_refs,
):
    all_views = views(*operator_refs)
    (bz_ref, fz_ref, br_ref, fr_ref, bzc_ref, fzc_ref, br_narrow_ref, brc_ref, frc_ref) = all_views[:9]
    (cross_ref, first_ref, second_ref, spectrum_ref, inverse_ref) = all_views[9:14]
    (cross_c_ref, first_c_ref, second_c_ref, inverse_c_ref) = all_views[14:]
    unit = lax.axis_index("tm") * BLOCKS + lax.axis_index("azim")
    scalar = [scalars_ref[unit, n] for n in range(4)]

    bz_ref[...] = axial_weights(backward_axial_ref[...])
    fz_ref[...] = axial_weights(forward_axial_ref[...])
    br_ref[...] = stacked_weights(identity_plus(backward_radial_ref[...]))
    fr_ref[...] = stacked_weights(identity_plus(forward_radial_ref[...]))
    bzc_ref[...] = axial_weights(backward_axial_c_ref[...])
    fzc_ref[...] = axial_weights(forward_axial_c_ref[...])
    brc_ref[...] = radial_weights(identity_plus(backward_radial_c_ref[...]))
    frc_ref[...] = radial_weights(identity_plus(forward_radial_c_ref[...]))
    br_narrow_ref[...] = radial_weights(identity_plus(backward_radial_ref[...])[:, :RADIAL_C])

    diffusion = column_of(diffusion_ref[...], RADIAL)
    cross_ref[...] = scalar[2] * advection_ref[...] + scalar[3]
    first_ref[...] = jnp.broadcast_to(scalar[0] * diffusion, (RADIAL, AXIAL))
    second_ref[...] = jnp.broadcast_to(scalar[1] * diffusion, (RADIAL, AXIAL))
    pick_lane = jnp.where(
        lax.broadcasted_iota(jnp.int32, (AXIAL, AXIAL_C), 0)
        == 2 * lax.broadcasted_iota(jnp.int32, (AXIAL, AXIAL_C), 1),
        1.0,
        0.0,
    )
    pick_row = jnp.where(
        lax.broadcasted_iota(jnp.int32, (RADIAL_C, RADIAL), 1)
        == 2 * lax.broadcasted_iota(jnp.int32, (RADIAL_C, RADIAL), 0),
        1.0,
        0.0,
    )
    exact = lax.Precision.HIGHEST
    advection_c = jnp.dot(
        jnp.dot(pick_row, advection_ref[...], precision=exact, preferred_element_type=F32),
        pick_lane,
        precision=exact,
        preferred_element_type=F32,
    )
    diffusion_c = jnp.sum(pick_row * diffusion_ref[...], axis=1, keepdims=True)
    cross_c_ref[...] = scalar[2] * advection_c + scalar[3]
    first_c_ref[...] = jnp.broadcast_to(scalar[0] * diffusion_c, (RADIAL_C, AXIAL_C))
    second_c_ref[...] = jnp.broadcast_to(scalar[1] * diffusion_c, (RADIAL_C, AXIAL_C))
    spectrum = -(column_of(decay_radial_ref[...], RADIAL) + decay_axial_ref[...])
    spectrum_ref[...] = spectrum
    inverse_ref[...] = 1.0 / (1.0 - HALF * spectrum)
    inverse_c_ref[...] = 1.0 / (1.0 - STEP * spectrum[:RADIAL_C, :AXIAL_C])


def units_kernel(
    received_ref,
    axial_ref,
    radial_ref,
    axial_c_ref,
    radial_c_ref,
    point_ref,
    point_c_ref,
    out_ref,
    field_ref,
    coarse_ref,
    push_ref,
    ahead_ref,
    behind_ref,
    known_ref,
    const_ref,
    gain_ref,
    state_ref,
):
    all_views = views(axial_ref, radial_ref, axial_c_ref, radial_c_ref, point_ref, point_c_ref)
    (bz_ref, fz_ref, br_ref, fr_ref, bzc_ref, fzc_ref, br_narrow_ref, brc_ref, frc_ref) = all_views[:9]
    (cross_ref, first_ref, second_ref, spectrum_ref, inverse_ref) = all_views[9:14]
    (cross_c_ref, first_c_ref, second_c_ref, inverse_c_ref) = all_views[14:]

    for field in range(2):
        for part in range(2):
            for rows in range(4):
                source = (field * 4 + rows) * 16 * 8 + part * 3
                for piece in range(6):
                    half, row = piece // 3, (piece % 3) * 8
                    group, first = piece // 2, (piece % 2) * 8
                    field_ref[field, part, rows * 24 + row : rows * 24 + row + 8, half * 128 : half * 128 + 128] = (
                        received_ref[pl.ds(source + first * 8 + group, 8, stride=8), :]
                    )

    def forces(re, im, cross, first, second):
        return first * re - cross * im, second * im + cross * re

    def blocks(rows, size):
        return [rows[n : n + size] for n in range(0, rows.shape[0], size)]

    def fine_forces(planes):
        moved = []
        for re, im in zip(planes[::2], planes[1::2]):
            moved.append(lambda re=re, im=im: first_ref[...] * re - cross_ref[...] * im)
            moved.append(lambda re=re, im=im: second_ref[...] * im + cross_ref[...] * re)
        return moved

    def flat(states):
        return jnp.concatenate([state.reshape(-1, state.shape[-1]) for state in states], axis=0)

    def pairs(planes):
        return [jnp.stack(planes[n : n + 2]) for n in range(0, len(planes), 2)]

    def to_points(planes):
        inner = []
        for plane in planes:
            inner.append(axial(plane(), bz_ref[...]))
            yield
        points = []
        for plane in inner:
            points.append(radial_stacked(br_ref[...], plane))
            yield
        return points

    def to_modes(planes, finish=lambda part, plane: plane):
        inner = []
        for plane in planes:
            inner.append(axial(plane(), fz_ref[...]))
            yield
        modes = []
        for part, plane in enumerate(inner):
            modes.append(finish(part, radial_stacked(fr_ref[...], plane)))
            yield
        return modes

    def explicit(states):
        planes = [lambda state=state, part=part: state[part] for state in states for part in range(2)]
        points = yield from to_points(planes)
        return pairs((yield from to_modes(fine_forces(points))))

    def explicit_of_coarse(states):
        narrow = jnp.concatenate([bz_ref[n * AXIAL : n * AXIAL + AXIAL_C, :] for n in range(3)], axis=0)
        inner = axial(flat(states), narrow)
        yield
        planes = []
        for plane in blocks(inner, RADIAL_C):
            planes.append(radial(br_narrow_ref[...], plane))
            yield
        return pairs((yield from to_modes(fine_forces(planes))))

    def restricted_explicit(planes):
        points = yield from to_points(planes)
        rows = jnp.concatenate([fr_ref[:RADIAL_C, :], fr_ref[RADIAL : RADIAL + RADIAL_C, :]], axis=0)
        narrow = []
        for plane in fine_forces(points):
            narrow.append(radial_stacked(rows, plane()))
            yield
        inner = axial(jnp.concatenate(narrow, axis=0), fz_ref[:, :AXIAL_C])
        yield
        return inner.reshape(2, RADIAL_C, AXIAL_C)

    def coarse_explicit(modes):
        inner = axial(modes.reshape(2 * RADIAL_C, AXIAL_C), bzc_ref[...])
        yield
        both = radial(brc_ref[...], jnp.concatenate([inner[:RADIAL_C], inner[RADIAL_C:]], axis=1))
        yield
        re, im = forces(
            both[:, :AXIAL_C], both[:, AXIAL_C:], cross_c_ref[...], first_c_ref[...], second_c_ref[...]
        )
        both = radial(frc_ref[...], jnp.concatenate([re, im], axis=1))
        yield
        inner = axial(jnp.concatenate([both[:, :AXIAL_C], both[:, AXIAL_C:]], axis=0), fzc_ref[...])
        yield
        return inner.reshape(2, RADIAL_C, AXIAL_C)

    done = set()

    def side_by_side(*tasks):
        waiting = list(tasks)
        while waiting:
            ready = [task for task in waiting if all(need in done for need in task[0])]
            for task in reversed(ready):
                try:
                    next(task[2])
                except StopIteration:
                    done.update(task[1])
                    waiting.remove(task)

    def corner(value):
        return value[:, :RADIAL_C, :AXIAL_C]

    spectrum_c = spectrum_ref[:RADIAL_C, :AXIAL_C]
    start_c = field_ref[0, :, :RADIAL_C, :AXIAL_C]
    forcing_c = field_ref[1, :, :RADIAL_C, :AXIAL_C]
    coarse_ref[0] = start_c

    def first_iteration():
        known_ref[0] = (yield from explicit([field_ref[0]]))[0]
        spectrum = spectrum_ref[...]
        total0 = known_ref[0] + field_ref[1] + spectrum * field_ref[0]
        known_ref[3] = inverse_ref[...] * (field_ref[0] - HALF * spectrum * field_ref[0] + (0.5 * STEP) * total0)
        known_ref[1] = (yield from explicit([known_ref[3]]))[0]
        known_ref[4] = inverse_ref[...] * (
            known_ref[3]
            + HALF * (known_ref[1] - known_ref[0])
            - HALF * spectrum_ref[...] * field_ref[0]
            + (0.5 * STEP) * (known_ref[0] + field_ref[1] + spectrum_ref[...] * field_ref[0])
        )
        coarse_ref[9] = known_ref[4, :, :RADIAL_C, :AXIAL_C]
        done.add("S9")
        known_ref[2] = (yield from explicit([known_ref[4]]))[0]
        coarse_known = [known_ref[n, :, :RADIAL_C, :AXIAL_C] for n in range(5)]
        gain_ref[0] = (
            STEP
            * (
                (coarse_known[0] + spectrum_c * start_c) / 6.0
                + (2.0 / 3.0) * (coarse_known[1] + spectrum_c * coarse_known[3])
                + (coarse_known[2] + spectrum_c * coarse_known[4]) / 6.0
                + forcing_c
            )
            - STEP * spectrum_c * coarse_known[4]
        )
        coarse_ref[1] = inverse_c_ref[...] * (gain_ref[0] + start_c)
        gain_ref[10] = gain_ref[0]


    def chain(*places):
        for n in places:
            latest = coarse_ref[n - 1]
            push = yield from coarse_explicit(latest - coarse_ref[0])
            coarse_ref[n] = inverse_c_ref[...] * (gain_ref[10] + latest + STEP * push)

    def spread(places):
        states = [coarse_ref[n] for n in places]
        pushes = yield from explicit_of_coarse(states)
        damping = (0.25 * HALF) * spectrum_ref[:RADIAL_C, :AXIAL_C]
        for n, state, push in zip(places, states, pushes):
            push_ref[n] = corner(push)
            behind_ref[n] = (0.25 * HALF) * push
            ahead_ref[n] = (0.75 * HALF) * push
            damped = damping * state
            behind_ref[n, :, :RADIAL_C, :AXIAL_C] = (0.25 * HALF) * corner(push) - damped
            ahead_ref[n, :, :RADIAL_C, :AXIAL_C] = (0.75 * HALF) * corner(push) + damped + state

    def padded(value):
        return jnp.pad(value, ((0, 0), (0, RADIAL - RADIAL_C), (0, AXIAL - AXIAL_C)))

    def constants():
        spectrum = spectrum_ref[...]
        wide_start = padded(coarse_ref[0])
        wide_end = padded(coarse_ref[9])
        push_start = (ahead_ref[0] + behind_ref[0] - wide_start) * (1.0 / HALF)
        push_end = (ahead_ref[9] + behind_ref[9] - wide_end) * (1.0 / HALF)
        rhs_start = push_start + spectrum * wide_start
        rhs_end = push_end + spectrum * wide_end
        total0 = known_ref[0] + field_ref[1] + spectrum * field_ref[0]
        total1 = known_ref[1] + field_ref[1] + spectrum * known_ref[3]
        total2 = known_ref[2] + field_ref[1] + spectrum * known_ref[4]
        shared = -HALF * spectrum * (known_ref[3] - 0.5 * (wide_start + wide_end)) + STEP * (
            (5.0 / 24.0) * total0 + (1.0 / 3.0) * total1 - (1.0 / 24.0) * total2 - 0.375 * rhs_start - 0.125 * rhs_end
        )
        const_ref[0] = field_ref[0] - wide_start + shared
        const_ref[1] = known_ref[4] - wide_end + HALF * (known_ref[2] - push_end - known_ref[0] + push_start) + shared
        const_ref[2] = (
            -HALF * (known_ref[1] - 0.5 * (push_start + push_end))
            - HALF * spectrum * (known_ref[4] - wide_end)
            + STEP
            * (
                (-1.0 / 24.0) * total0
                + (1.0 / 3.0) * total1
                + (5.0 / 24.0) * total2
                - 0.125 * rhs_start
                - 0.375 * rhs_end
            )
        )
        coarse_known = [known_ref[n, :, :RADIAL_C, :AXIAL_C] for n in (0, 2)]
        gain_ref[8] = STEP * (forcing_c + (coarse_known[0] - push_ref[0]) / 6.0)
        gain_ref[9] = STEP * (forcing_c + (coarse_known[1] - push_ref[9]) / 6.0)
        return
        yield

    def sweep(n, kind):
        middles, pushes, endings = {}, {}, {}

        def middle(part):
            middles[part] = inverse_ref[...] * (const_ref[kind, part] + ahead_ref[n, part] + behind_ref[n + 1, part])
            return middles[part]

        def ending(part, push):
            pushes[part] = push[:RADIAL_C, :AXIAL_C]
            endings[part] = inverse_ref[...] * (
                middles[part] + HALF * push + const_ref[2, part] + behind_ref[n + 1, part] - behind_ref[n, part]
            )
            for half in range(2):
                for j in range(0 if half else 3, 6):
                    out_ref[n, pl.ds(part * 12 + half * 6 + j, 16, stride=24), :] = endings[part][
                        16 * j : 16 * j + 16, half * 128 : half * 128 + 128
                    ]
            return endings[part]

        points = yield from to_points([lambda part=part: middle(part) for part in range(2)])
        yield from to_modes(fine_forces(points), ending)
        last = yield from restricted_explicit([lambda part=part: endings[part] for part in range(2)])
        spectrum_c = spectrum_ref[:RADIAL_C, :AXIAL_C]
        for part in range(2):
            gain_ref[n, part] = (
                gain_ref[8 + kind, part]
                + (STEP / 6.0) * (push_ref[n, part] + spectrum_c * coarse_ref[n, part])
                + (STEP * 2.0 / 3.0) * (pushes[part] + spectrum_c * middles[part][:RADIAL_C, :AXIAL_C])
                + (STEP / 6.0) * last[part]
                - (STEP * 5.0 / 6.0) * spectrum_c * endings[part][:RADIAL_C, :AXIAL_C]
            )

    def chain_again(places):
        for n in places:
            state = state_ref[...]
            push = yield from coarse_explicit(state - coarse_ref[n])
            after = inverse_c_ref[...] * (gain_ref[n] + state + STEP * push)
            state_ref[...] = after
            for part in range(2):
                for j in range(3):
                    out_ref[n, pl.ds(part * 12 + j, 16, stride=24), :] = after[part, 16 * j : 16 * j + 16, :]

    def chaining(n):
        return ["S%d" % (n - 1)], ["S%d" % n], chain(n)

    def spreading(*places):
        return ["S%d" % n for n in places], ["E%d" % n for n in places], spread(places)

    def sweeping(n):
        return ["E%d" % n, "E%d" % (n + 1), "constants"], ["J%d" % n], sweep(n, min(n, 1))

    def chaining_again(n):
        return ["J%d" % n, "T%d" % n], ["T%d" % (n + 1)], chain_again([n])

    state_ref[...] = coarse_ref[0]
    done.update(["S0", "T0"])
    side_by_side(
        ([], ["first", "S1"], first_iteration()),
        *[chaining(n) for n in range(2, 9)],
        *[chaining_again(n) for n in range(8)],
        spreading(0),
        spreading(9),
        (["first", "E0", "E9"], ["constants"], constants()),
        *[spreading(n) for n in range(1, 9)],
        *[sweeping(n) for n in range(8)],
    )


def from_units_kernel(transform_ref, received_ref, send_ref):
    for pair in range(6):
        parts = []
        for part in range(2):
            parts.append(
                jnp.concatenate(
                    [received_ref[pl.ds(part * 12 + 2 * pair + n, UNITS, stride=24), :] for n in range(2)], axis=1
                )
            )
        planes = radial(transform_ref[...], jnp.concatenate(parts, axis=0))
        for n in range(2):
            send_ref[pl.ds(2 * pair + n, 192, stride=12), :] = planes[:, n * 128 : n * 128 + 128]


def place_kernel(received_ref, out_ref, planes_ref, sems):
    def copy(group):
        own = pl.ds(3 * group, 3)
        return pltpu.make_async_copy(planes_ref.at[own], out_ref.at[own], sems.at[group])

    for plane in range(12):
        for half in range(2):
            for j in range(6):
                planes_ref[plane, 16 * j : 16 * j + 16, half * 128 : half * 128 + 128] = received_ref[
                    pl.ds(plane * 12 + half * 6 + j, 16, stride=144), :
                ]
        if plane % 3 == 2:
            copy(plane // 3).start()
    for group in range(4):
        copy(group).wait()


VMEM = pl.BlockSpec(memory_space=pltpu.VMEM)
HBM = pl.BlockSpec(memory_space=pltpu.HBM)
SMEM = pl.BlockSpec(memory_space=pltpu.SMEM)


def params(mib):
    return pltpu.CompilerParams(vmem_limit_bytes=mib << 20)


def array(*shape):
    return jax.ShapeDtypeStruct(shape, F32)


def exchange(value, axes, peers):
    rows = value.shape[0] // peers
    moved = lax.all_to_all(value.reshape(peers, rows, 128), axes, 0, 0)
    return moved.reshape(value.shape)


def per_device(
    initial_state,
    forcing,
    forward_radial,
    backward_radial,
    forward_axial,
    backward_axial,
    forward_radial_coarse,
    backward_radial_coarse,
    forward_axial_coarse,
    backward_axial_coarse,
    decay_radial,
    decay_axial,
    advection,
    diffusion,
):
    operators = pl.pallas_call(
        operators_kernel,
        out_shape=[jax.ShapeDtypeStruct(shape, kind) for _, shape, kind in OPERATORS],
        in_specs=[SMEM] + [VMEM] * 12,
        out_specs=[VMEM] * len(OPERATORS),
        compiler_params=params(8),
        name="operators",
    )(
        jnp.asarray(SCALARS),
        forward_radial,
        backward_radial,
        forward_axial,
        backward_axial,
        forward_radial_coarse,
        backward_radial_coarse,
        forward_axial_coarse,
        backward_axial_coarse,
        decay_radial.reshape(1, RADIAL),
        decay_axial.reshape(1, AXIAL),
        advection,
        diffusion.reshape(1, RADIAL),
    )
    send = pl.pallas_call(
        gather_kernel,
        out_shape=array(BLOCKS * 40, 128),
        in_specs=[HBM, HBM],
        out_specs=VMEM,
        scratch_shapes=[pltpu.VMEM((12, 24, AXIAL), F32), pltpu.SemaphoreType.DMA((4,))],
        compiler_params=params(4),
        name="gather_points",
    )(
        *[
            pltpu.with_memory_space_constraint(field.reshape(12, RADIAL, AXIAL), pltpu.HBM)
            for field in (initial_state, forcing)
        ]
    )
    received = exchange(send, "azim", BLOCKS)
    received = received.reshape(BLOCKS, 40, 128)[:, :36].reshape(BLOCKS * 36, 128)
    send = pl.pallas_call(
        to_units_kernel,
        out_shape=array(128 * 8, 128),
        in_specs=[VMEM, VMEM],
        out_specs=HBM,
        scratch_shapes=[pltpu.VMEM((128 * 8, 128), F32), pltpu.SemaphoreType.DMA((3,))],
        compiler_params=params(4),
        name="to_units",
    )(jnp.asarray(TO_UNITS), received)
    received = exchange(send, ("tm", "azim"), 128)

    fine, coarse = (2, RADIAL, AXIAL), (2, RADIAL_C, AXIAL_C)
    send = pl.pallas_call(
        units_kernel,
        out_shape=array(SLICES, 16 * 24, 128),
        in_specs=[VMEM] * (1 + len(OPERATORS)),
        out_specs=VMEM,
        scratch_shapes=[
            pltpu.VMEM((2,) + fine, F32),
            pltpu.VMEM((10,) + coarse, F32),
            pltpu.VMEM((10,) + coarse, F32),
            pltpu.VMEM((10,) + fine, F32),
            pltpu.VMEM((10,) + fine, F32),
            pltpu.VMEM((5,) + fine, F32),
            pltpu.VMEM((3,) + fine, F32),
            pltpu.VMEM((11,) + coarse, F32),
            pltpu.VMEM(coarse, F32),
        ],
        compiler_params=params(28),
        name="units",
    )(received, *operators)
    received = exchange(send.reshape(128 * 24, 128), ("tm", "azim"), 128)
    send = pl.pallas_call(
        from_units_kernel,
        out_shape=array(BLOCKS * 144, 128),
        in_specs=[VMEM, VMEM],
        out_specs=VMEM,
        compiler_params=params(8),
        name="from_units",
    )(jnp.asarray(FROM_UNITS), received)
    received = exchange(send, "azim", BLOCKS)
    planes = pl.pallas_call(
        place_kernel,
        out_shape=array(12, RADIAL, AXIAL),
        in_specs=[VMEM],
        out_specs=HBM,
        scratch_shapes=[pltpu.VMEM((12, RADIAL, AXIAL), F32), pltpu.SemaphoreType.DMA((4,))],
        compiler_params=params(6),
        name="place",
    )(received)
    return planes.reshape(1, 3, 4, RADIAL, AXIAL)


def solution(mesh):
    split_planes = P(None, "azim", None, None)
    return jax.shard_map(
        per_device,
        mesh=mesh,
        in_specs=(split_planes, split_planes) + (P(),) * 12,
        out_specs=P("tm", None, "azim", None, None),
        check_vma=False,
    )
```

```python
import ml_dtypes
import numpy as np
import jax
import jax.numpy as jnp
from jax import lax
from jax.experimental import pallas as pl
from jax.experimental.pallas import tpu as pltpu
from jax.sharding import PartitionSpec as P

SLICES = 8
AZIMUTH = 64
RADIAL, AXIAL = 96, 256
RADIAL_C, AXIAL_C = 48, 128
BLOCKS = 16
UNITS = 96
STEP = 0.1
HALF = 0.05
F32 = jnp.float32
BF16 = jnp.bfloat16


def azimuth_transform():
    points = np.arange(AZIMUTH)
    rows = np.zeros((2, UNITS, 3, AZIMUTH))
    scalars = np.zeros((128, 4))
    for k in range(64):
        angle = 2.0 * np.pi * k / AZIMUTH
        cos, sin = np.cos(angle * points) / 8.0, np.sin(angle * points) / 8.0
        rows[0, k, 0], rows[0, k, 1] = cos, sin
        rows[1, k, 1], rows[1, k, 0] = cos, -sin
        second = 2.0 * np.cos(angle) - 2.0
        scalars[k] = (second, second, 2.0 * np.sin(angle), -2.0)
    rows[0, 64, 2] = 1.0 / 8.0
    rows[1, 64, 2] = (-1.0) ** points / 8.0
    scalars[64] = (0.0, -4.0, 0.0, 0.0)
    for k in range(1, 32):
        angle = 2.0 * np.pi * k / AZIMUTH
        rows[0, 64 + k, 2] = np.sqrt(2.0) * np.cos(angle * points) / 8.0
        rows[1, 64 + k, 2] = -np.sqrt(2.0) * np.sin(angle * points) / 8.0
        second = 2.0 * np.cos(angle) - 2.0
        scalars[64 + k] = (second, second, 2.0 * np.sin(angle), 0.0)
    matrix = rows.reshape(192, 3, BLOCKS, 4).transpose(0, 2, 1, 3).reshape(192, 192)
    return matrix, scalars.astype(np.float32)


def split_constant(matrix):
    single = matrix.astype(np.float32)
    high = single.astype(ml_dtypes.bfloat16)
    low = (single - high.astype(np.float32)).astype(ml_dtypes.bfloat16)
    return np.concatenate([high, high, low], axis=1)


TRANSFORM, SCALARS = azimuth_transform()
TO_UNITS = split_constant(TRANSFORM)
FROM_UNITS = split_constant(TRANSFORM.T.copy())


def split(value):
    high = value.astype(BF16)
    return high, (value - high.astype(F32)).astype(BF16)


def dot(left, right):
    return jnp.dot(left, right, preferred_element_type=F32)


def axial(value, weights):
    high, low = split(value)
    depth = weights.shape[0] // 3
    products = dot(jnp.concatenate([high, low], axis=0), weights[:depth])
    return products[: value.shape[0]] + products[value.shape[0] :] + dot(high, weights[2 * depth :])


def radial(weights, value):
    high, low = split(value)
    return dot(weights, jnp.concatenate([high, low, high], axis=0))


def radial_stacked(weights, value):
    products = dot(weights, jnp.concatenate(split(value), axis=0))
    half = weights.shape[0] // 2
    return products[:half] + products[half:]


def gather_kernel(initial_ref, forcing_ref, send_ref, block_ref, sems):
    tm = lax.axis_index("tm")
    rows = pl.ds(pl.multiple_of((tm % 4) * 24, 8), 24)

    def copies(source_ref):
        for group in range(4):
            own = pl.ds(3 * group, 3)
            yield pltpu.make_async_copy(source_ref.at[own, rows, :], block_ref.at[own], sems.at[group])

    @pl.when(tm < 4)
    def _():
        for copy in copies(initial_ref):
            copy.start()

    @pl.when(tm >= 4)
    def _():
        for copy in copies(forcing_ref):
            copy.start()

    waits = list(copies(initial_ref))
    for plane in range(12):
        if plane % 3 == 0:
            waits[plane // 3].wait()
        for piece in range(6):
            half, row = piece // 3, (piece % 3) * 8
            values = block_ref[plane, row : row + 8, half * 128 : half * 128 + 128]
            group, first = piece // 2, (piece % 2) * 8
            send_ref[pl.ds(first * 40 + plane * 3 + group, 8, stride=40), :] = values


def to_units_kernel(transform_ref, received_ref, send_ref):
    columns = [received_ref[pl.ds(group, 192, stride=3), :] for group in range(3)]
    send_ref[UNITS * 8 :, :] = jnp.zeros((32 * 8, 128), F32)
    zero = jnp.zeros((UNITS, 128), F32)
    send_ref[pl.ds(6, UNITS, stride=8), :] = zero
    send_ref[pl.ds(7, UNITS, stride=8), :] = zero
    for group in range(3):
        units = radial(transform_ref[...], columns[group])
        for part in range(2):
            send_ref[pl.ds(part * 3 + group, UNITS, stride=8), :] = units[part * UNITS : (part + 1) * UNITS]


def column_of(row, size):
    at = lax.broadcasted_iota(jnp.int32, (size, size), 0) == lax.broadcasted_iota(jnp.int32, (size, size), 1)
    return jnp.sum(jnp.where(at, row, 0.0), axis=1, keepdims=True)


def identity_plus(value):
    size = value.shape[0]
    at = lax.broadcasted_iota(jnp.int32, (size, size), 0) == lax.broadcasted_iota(jnp.int32, (size, size), 1)
    return jnp.where(at, 1.0, 0.0) + value


def axial_weights(value):
    high, low = split(jnp.transpose(identity_plus(value)))
    return jnp.concatenate([high, high, low], axis=0)


def radial_weights(value):
    high, low = split(value)
    return jnp.concatenate([high, high, low], axis=1)


def stacked_weights(value):
    high, low = split(value)
    return jnp.concatenate(
        [jnp.concatenate([high, high], axis=1), jnp.concatenate([low, jnp.zeros_like(low)], axis=1)], axis=0
    )


OPERATORS = (
    ("axial", (6 * AXIAL, AXIAL), BF16),
    ("radial", (4 * RADIAL, 2 * RADIAL), BF16),
    ("axial_c", (6 * AXIAL_C, AXIAL_C), BF16),
    ("radial_c", (RADIAL + 2 * RADIAL_C, 3 * RADIAL_C), BF16),
    ("point", (5 * RADIAL, AXIAL), F32),
    ("point_c", (4 * RADIAL_C, AXIAL_C), F32),
)


def views(axial_ref, radial_ref, axial_c_ref, radial_c_ref, point_ref, point_c_ref):
    def parts(ref, *sizes):
        ends = np.cumsum(sizes)
        return [ref.at[int(end - size) : int(end), :] for size, end in zip(sizes, ends)]

    return (
        parts(axial_ref, *[3 * AXIAL] * 2)
        + parts(radial_ref, *[2 * RADIAL] * 2)
        + parts(axial_c_ref, *[3 * AXIAL_C] * 2)
        + parts(radial_c_ref, RADIAL, RADIAL_C, RADIAL_C)
        + parts(point_ref, *[RADIAL] * 5)
        + parts(point_c_ref, *[RADIAL_C] * 4)
    )


def operators_kernel(
    scalars_ref,
    forward_radial_ref,
    backward_radial_ref,
    forward_axial_ref,
    backward_axial_ref,
    forward_radial_c_ref,
    backward_radial_c_ref,
    forward_axial_c_ref,
    backward_axial_c_ref,
    decay_radial_ref,
    decay_axial_ref,
    advection_ref,
    diffusion_ref,
    *operator_refs,
):
    all_views = views(*operator_refs)
    (bz_ref, fz_ref, br_ref, fr_ref, bzc_ref, fzc_ref, br_narrow_ref, brc_ref, frc_ref) = all_views[:9]
    (cross_ref, first_ref, second_ref, spectrum_ref, inverse_ref) = all_views[9:14]
    (cross_c_ref, first_c_ref, second_c_ref, inverse_c_ref) = all_views[14:]
    unit = lax.axis_index("tm") * BLOCKS + lax.axis_index("azim")
    scalar = [scalars_ref[unit, n] for n in range(4)]

    bz_ref[...] = axial_weights(backward_axial_ref[...])
    fz_ref[...] = axial_weights(forward_axial_ref[...])
    br_ref[...] = stacked_weights(identity_plus(backward_radial_ref[...]))
    fr_ref[...] = stacked_weights(identity_plus(forward_radial_ref[...]))
    bzc_ref[...] = axial_weights(backward_axial_c_ref[...])
    fzc_ref[...] = axial_weights(forward_axial_c_ref[...])
    brc_ref[...] = radial_weights(identity_plus(backward_radial_c_ref[...]))
    frc_ref[...] = radial_weights(identity_plus(forward_radial_c_ref[...]))
    br_narrow_ref[...] = radial_weights(identity_plus(backward_radial_ref[...])[:, :RADIAL_C])

    diffusion = column_of(diffusion_ref[...], RADIAL)
    cross_ref[...] = scalar[2] * advection_ref[...] + scalar[3]
    first_ref[...] = jnp.broadcast_to(scalar[0] * diffusion, (RADIAL, AXIAL))
    second_ref[...] = jnp.broadcast_to(scalar[1] * diffusion, (RADIAL, AXIAL))
    pick_lane = jnp.where(
        lax.broadcasted_iota(jnp.int32, (AXIAL, AXIAL_C), 0)
        == 2 * lax.broadcasted_iota(jnp.int32, (AXIAL, AXIAL_C), 1),
        1.0,
        0.0,
    )
    pick_row = jnp.where(
        lax.broadcasted_iota(jnp.int32, (RADIAL_C, RADIAL), 1)
        == 2 * lax.broadcasted_iota(jnp.int32, (RADIAL_C, RADIAL), 0),
        1.0,
        0.0,
    )
    exact = lax.Precision.HIGHEST
    advection_c = jnp.dot(
        jnp.dot(pick_row, advection_ref[...], precision=exact, preferred_element_type=F32),
        pick_lane,
        precision=exact,
        preferred_element_type=F32,
    )
    diffusion_c = jnp.sum(pick_row * diffusion_ref[...], axis=1, keepdims=True)
    cross_c_ref[...] = scalar[2] * advection_c + scalar[3]
    first_c_ref[...] = jnp.broadcast_to(scalar[0] * diffusion_c, (RADIAL_C, AXIAL_C))
    second_c_ref[...] = jnp.broadcast_to(scalar[1] * diffusion_c, (RADIAL_C, AXIAL_C))
    spectrum = -(column_of(decay_radial_ref[...], RADIAL) + decay_axial_ref[...])
    spectrum_ref[...] = spectrum
    inverse_ref[...] = 1.0 / (1.0 - HALF * spectrum)
    inverse_c_ref[...] = 1.0 / (1.0 - STEP * spectrum[:RADIAL_C, :AXIAL_C])


def units_kernel(
    received_ref,
    axial_ref,
    radial_ref,
    axial_c_ref,
    radial_c_ref,
    point_ref,
    point_c_ref,
    out_ref,
    field_ref,
    coarse_ref,
    push_ref,
    ahead_ref,
    behind_ref,
    known_ref,
    const_ref,
    gain_ref,
    state_ref,
):
    all_views = views(axial_ref, radial_ref, axial_c_ref, radial_c_ref, point_ref, point_c_ref)
    (bz_ref, fz_ref, br_ref, fr_ref, bzc_ref, fzc_ref, br_narrow_ref, brc_ref, frc_ref) = all_views[:9]
    (cross_ref, first_ref, second_ref, spectrum_ref, inverse_ref) = all_views[9:14]
    (cross_c_ref, first_c_ref, second_c_ref, inverse_c_ref) = all_views[14:]

    for field in range(2):
        for part in range(2):
            for rows in range(4):
                source = (field * 4 + rows) * 16 * 8 + part * 3
                for piece in range(6):
                    half, row = piece // 3, (piece % 3) * 8
                    group, first = piece // 2, (piece % 2) * 8
                    field_ref[field, part, rows * 24 + row : rows * 24 + row + 8, half * 128 : half * 128 + 128] = (
                        received_ref[pl.ds(source + first * 8 + group, 8, stride=8), :]
                    )

    def forces(re, im, cross, first, second):
        return first * re - cross * im, second * im + cross * re

    def blocks(rows, size):
        return [rows[n : n + size] for n in range(0, rows.shape[0], size)]

    def fine_forces(planes):
        moved = []
        for re, im in zip(planes[::2], planes[1::2]):
            moved.append(lambda re=re, im=im: first_ref[...] * re - cross_ref[...] * im)
            moved.append(lambda re=re, im=im: second_ref[...] * im + cross_ref[...] * re)
        return moved

    def flat(states):
        return jnp.concatenate([state.reshape(-1, state.shape[-1]) for state in states], axis=0)

    def pairs(planes):
        return [jnp.stack(planes[n : n + 2]) for n in range(0, len(planes), 2)]

    def to_points(planes):
        inner = []
        for plane in planes:
            inner.append(axial(plane(), bz_ref[...]))
            yield
        points = []
        for plane in inner:
            points.append(radial_stacked(br_ref[...], plane))
            yield
        return points

    def to_modes(planes, finish=lambda part, plane: plane):
        inner = []
        for plane in planes:
            inner.append(axial(plane(), fz_ref[...]))
            yield
        modes = []
        for part, plane in enumerate(inner):
            modes.append(finish(part, radial_stacked(fr_ref[...], plane)))
            yield
        return modes

    def explicit(states):
        planes = [lambda state=state, part=part: state[part] for state in states for part in range(2)]
        points = yield from to_points(planes)
        return pairs((yield from to_modes(fine_forces(points))))

    def explicit_of_coarse(states):
        narrow = jnp.concatenate([bz_ref[n * AXIAL : n * AXIAL + AXIAL_C, :] for n in range(3)], axis=0)
        inner = axial(flat(states), narrow)
        yield
        planes = []
        for plane in blocks(inner, RADIAL_C):
            planes.append(radial(br_narrow_ref[...], plane))
            yield
        return pairs((yield from to_modes(fine_forces(planes))))

    def restricted_explicit(planes):
        points = yield from to_points(planes)
        rows = jnp.concatenate([fr_ref[:RADIAL_C, :], fr_ref[RADIAL : RADIAL + RADIAL_C, :]], axis=0)
        narrow = []
        for plane in fine_forces(points):
            narrow.append(radial_stacked(rows, plane()))
            yield
        inner = axial(jnp.concatenate(narrow, axis=0), fz_ref[:, :AXIAL_C])
        yield
        return inner.reshape(2, RADIAL_C, AXIAL_C)

    def coarse_explicit(modes):
        inner = axial(modes.reshape(2 * RADIAL_C, AXIAL_C), bzc_ref[...])
        yield
        both = radial(brc_ref[...], jnp.concatenate([inner[:RADIAL_C], inner[RADIAL_C:]], axis=1))
        yield
        re, im = forces(
            both[:, :AXIAL_C], both[:, AXIAL_C:], cross_c_ref[...], first_c_ref[...], second_c_ref[...]
        )
        both = radial(frc_ref[...], jnp.concatenate([re, im], axis=1))
        yield
        inner = axial(jnp.concatenate([both[:, :AXIAL_C], both[:, AXIAL_C:]], axis=0), fzc_ref[...])
        yield
        return inner.reshape(2, RADIAL_C, AXIAL_C)

    done = set()

    def side_by_side(*tasks):
        waiting = list(tasks)
        while waiting:
            ready = [task for task in waiting if all(need in done for need in task[0])]
            for task in reversed(ready):
                try:
                    next(task[2])
                except StopIteration:
                    done.update(task[1])
                    waiting.remove(task)

    def corner(value):
        return value[:, :RADIAL_C, :AXIAL_C]

    spectrum_c = spectrum_ref[:RADIAL_C, :AXIAL_C]
    start_c = field_ref[0, :, :RADIAL_C, :AXIAL_C]
    forcing_c = field_ref[1, :, :RADIAL_C, :AXIAL_C]
    coarse_ref[0] = start_c

    def first_iteration():
        known_ref[0] = (yield from explicit([field_ref[0]]))[0]
        spectrum = spectrum_ref[...]
        total0 = known_ref[0] + field_ref[1] + spectrum * field_ref[0]
        known_ref[3] = inverse_ref[...] * (field_ref[0] - HALF * spectrum * field_ref[0] + (0.5 * STEP) * total0)
        known_ref[1] = (yield from explicit([known_ref[3]]))[0]
        known_ref[4] = inverse_ref[...] * (
            known_ref[3]
            + HALF * (known_ref[1] - known_ref[0])
            - HALF * spectrum_ref[...] * field_ref[0]
            + (0.5 * STEP) * (known_ref[0] + field_ref[1] + spectrum_ref[...] * field_ref[0])
        )
        coarse_ref[9] = known_ref[4, :, :RADIAL_C, :AXIAL_C]
        done.add("S9")
        known_ref[2] = (yield from explicit([known_ref[4]]))[0]
        coarse_known = [known_ref[n, :, :RADIAL_C, :AXIAL_C] for n in range(5)]
        gain_ref[0] = (
            STEP
            * (
                (coarse_known[0] + spectrum_c * start_c) / 6.0
                + (2.0 / 3.0) * (coarse_known[1] + spectrum_c * coarse_known[3])
                + (coarse_known[2] + spectrum_c * coarse_known[4]) / 6.0
                + forcing_c
            )
            - STEP * spectrum_c * coarse_known[4]
        )
        coarse_ref[1] = inverse_c_ref[...] * (gain_ref[0] + start_c)
        gain_ref[10] = gain_ref[0]


    def chain(*places):
        for n in places:
            latest = coarse_ref[n - 1]
            push = yield from coarse_explicit(latest - coarse_ref[0])
            coarse_ref[n] = inverse_c_ref[...] * (gain_ref[10] + latest + STEP * push)

    def spread(places):
        states = [coarse_ref[n] for n in places]
        pushes = yield from explicit_of_coarse(states)
        damping = (0.25 * HALF) * spectrum_ref[:RADIAL_C, :AXIAL_C]
        for n, state, push in zip(places, states, pushes):
            push_ref[n] = corner(push)
            behind_ref[n] = (0.25 * HALF) * push
            ahead_ref[n] = (0.75 * HALF) * push
            damped = damping * state
            behind_ref[n, :, :RADIAL_C, :AXIAL_C] = (0.25 * HALF) * corner(push) - damped
            ahead_ref[n, :, :RADIAL_C, :AXIAL_C] = (0.75 * HALF) * corner(push) + damped + state

    def padded(value):
        return jnp.pad(value, ((0, 0), (0, RADIAL - RADIAL_C), (0, AXIAL - AXIAL_C)))

    def constants():
        spectrum = spectrum_ref[...]
        wide_start = padded(coarse_ref[0])
        wide_end = padded(coarse_ref[9])
        push_start = (ahead_ref[0] + behind_ref[0] - wide_start) * (1.0 / HALF)
        push_end = (ahead_ref[9] + behind_ref[9] - wide_end) * (1.0 / HALF)
        rhs_start = push_start + spectrum * wide_start
        rhs_end = push_end + spectrum * wide_end
        total0 = known_ref[0] + field_ref[1] + spectrum * field_ref[0]
        total1 = known_ref[1] + field_ref[1] + spectrum * known_ref[3]
        total2 = known_ref[2] + field_ref[1] + spectrum * known_ref[4]
        shared = -HALF * spectrum * (known_ref[3] - 0.5 * (wide_start + wide_end)) + STEP * (
            (5.0 / 24.0) * total0 + (1.0 / 3.0) * total1 - (1.0 / 24.0) * total2 - 0.375 * rhs_start - 0.125 * rhs_end
        )
        const_ref[0] = field_ref[0] - wide_start + shared
        const_ref[1] = known_ref[4] - wide_end + HALF * (known_ref[2] - push_end - known_ref[0] + push_start) + shared
        const_ref[2] = (
            -HALF * (known_ref[1] - 0.5 * (push_start + push_end))
            - HALF * spectrum * (known_ref[4] - wide_end)
            + STEP
            * (
                (-1.0 / 24.0) * total0
                + (1.0 / 3.0) * total1
                + (5.0 / 24.0) * total2
                - 0.125 * rhs_start
                - 0.375 * rhs_end
            )
        )
        coarse_known = [known_ref[n, :, :RADIAL_C, :AXIAL_C] for n in (0, 2)]
        gain_ref[8] = STEP * (forcing_c + (coarse_known[0] - push_ref[0]) / 6.0)
        gain_ref[9] = STEP * (forcing_c + (coarse_known[1] - push_ref[9]) / 6.0)
        return
        yield

    def sweep(n, kind):
        middles, pushes, endings = {}, {}, {}

        def middle(part):
            middles[part] = inverse_ref[...] * (const_ref[kind, part] + ahead_ref[n, part] + behind_ref[n + 1, part])
            return middles[part]

        def ending(part, push):
            pushes[part] = push[:RADIAL_C, :AXIAL_C]
            endings[part] = inverse_ref[...] * (
                middles[part] + HALF * push + const_ref[2, part] + behind_ref[n + 1, part] - behind_ref[n, part]
            )
            for half in range(2):
                for j in range(0 if half else 3, 6):
                    out_ref[n, pl.ds(part * 12 + half * 6 + j, 16, stride=24), :] = endings[part][
                        16 * j : 16 * j + 16, half * 128 : half * 128 + 128
                    ]
            return endings[part]

        points = yield from to_points([lambda part=part: middle(part) for part in range(2)])
        yield from to_modes(fine_forces(points), ending)
        last = yield from restricted_explicit([lambda part=part: endings[part] for part in range(2)])
        spectrum_c = spectrum_ref[:RADIAL_C, :AXIAL_C]
        for part in range(2):
            gain_ref[n, part] = (
                gain_ref[8 + kind, part]
                + (STEP / 6.0) * (push_ref[n, part] + spectrum_c * coarse_ref[n, part])
                + (STEP * 2.0 / 3.0) * (pushes[part] + spectrum_c * middles[part][:RADIAL_C, :AXIAL_C])
                + (STEP / 6.0) * last[part]
                - (STEP * 5.0 / 6.0) * spectrum_c * endings[part][:RADIAL_C, :AXIAL_C]
            )

    def chain_again(places):
        for n in places:
            state = state_ref[...]
            push = yield from coarse_explicit(state - coarse_ref[n])
            after = inverse_c_ref[...] * (gain_ref[n] + state + STEP * push)
            state_ref[...] = after
            for part in range(2):
                for j in range(3):
                    out_ref[n, pl.ds(part * 12 + j, 16, stride=24), :] = after[part, 16 * j : 16 * j + 16, :]

    def chaining(n):
        return ["S%d" % (n - 1)], ["S%d" % n], chain(n)

    def spreading(*places):
        return ["S%d" % n for n in places], ["E%d" % n for n in places], spread(places)

    def sweeping(n):
        return ["E%d" % n, "E%d" % (n + 1), "constants"], ["J%d" % n], sweep(n, min(n, 1))

    def chaining_again(n):
        return ["J%d" % n, "T%d" % n], ["T%d" % (n + 1)], chain_again([n])

    state_ref[...] = coarse_ref[0]
    done.update(["S0", "T0"])
    side_by_side(
        ([], ["first", "S1"], first_iteration()),
        *[chaining(n) for n in range(2, 9)],
        *[chaining_again(n) for n in range(8)],
        spreading(0),
        spreading(9),
        (["first", "E0", "E9"], ["constants"], constants()),
        *[spreading(n) for n in range(1, 9)],
        *[sweeping(n) for n in range(8)],
    )


def from_units_kernel(transform_ref, received_ref, send_ref):
    for pair in range(6):
        parts = []
        for part in range(2):
            parts.append(
                jnp.concatenate(
                    [received_ref[pl.ds(part * 12 + 2 * pair + n, UNITS, stride=24), :] for n in range(2)], axis=1
                )
            )
        planes = radial(transform_ref[...], jnp.concatenate(parts, axis=0))
        for n in range(2):
            send_ref[pl.ds(2 * pair + n, 192, stride=12), :] = planes[:, n * 128 : n * 128 + 128]


def place_kernel(received_ref, out_ref, planes_ref, sems):
    def copy(group):
        own = pl.ds(3 * group, 3)
        return pltpu.make_async_copy(planes_ref.at[own], out_ref.at[own], sems.at[group])

    for plane in range(12):
        for half in range(2):
            for j in range(6):
                planes_ref[plane, 16 * j : 16 * j + 16, half * 128 : half * 128 + 128] = received_ref[
                    pl.ds(plane * 12 + half * 6 + j, 16, stride=144), :
                ]
        if plane % 3 == 2:
            copy(plane // 3).start()
    for group in range(4):
        copy(group).wait()


VMEM = pl.BlockSpec(memory_space=pltpu.VMEM)
HBM = pl.BlockSpec(memory_space=pltpu.HBM)
SMEM = pl.BlockSpec(memory_space=pltpu.SMEM)


def params(mib):
    return pltpu.CompilerParams(vmem_limit_bytes=mib << 20)


def array(*shape):
    return jax.ShapeDtypeStruct(shape, F32)


def exchange(value, axes, peers):
    rows = value.shape[0] // peers
    moved = lax.all_to_all(value.reshape(peers, rows, 128), axes, 0, 0)
    return moved.reshape(value.shape)


def per_device(
    initial_state,
    forcing,
    forward_radial,
    backward_radial,
    forward_axial,
    backward_axial,
    forward_radial_coarse,
    backward_radial_coarse,
    forward_axial_coarse,
    backward_axial_coarse,
    decay_radial,
    decay_axial,
    advection,
    diffusion,
):
    operators = pl.pallas_call(
        operators_kernel,
        out_shape=[jax.ShapeDtypeStruct(shape, kind) for _, shape, kind in OPERATORS],
        in_specs=[SMEM] + [VMEM] * 12,
        out_specs=[VMEM] * len(OPERATORS),
        compiler_params=params(8),
        name="operators",
    )(
        jnp.asarray(SCALARS),
        forward_radial,
        backward_radial,
        forward_axial,
        backward_axial,
        forward_radial_coarse,
        backward_radial_coarse,
        forward_axial_coarse,
        backward_axial_coarse,
        decay_radial.reshape(1, RADIAL),
        decay_axial.reshape(1, AXIAL),
        advection,
        diffusion.reshape(1, RADIAL),
    )
    send = pl.pallas_call(
        gather_kernel,
        out_shape=array(BLOCKS * 40, 128),
        in_specs=[HBM, HBM],
        out_specs=VMEM,
        scratch_shapes=[pltpu.VMEM((12, 24, AXIAL), F32), pltpu.SemaphoreType.DMA((4,))],
        compiler_params=params(4),
        name="gather_points",
    )(
        *[
            pltpu.with_memory_space_constraint(field.reshape(12, RADIAL, AXIAL), pltpu.HBM)
            for field in (initial_state, forcing)
        ]
    )
    received = exchange(send, "azim", BLOCKS)
    received = received.reshape(BLOCKS, 40, 128)[:, :36].reshape(BLOCKS * 36, 128)
    send = pl.pallas_call(
        to_units_kernel,
        out_shape=array(128 * 8, 128),
        in_specs=[VMEM, VMEM],
        out_specs=VMEM,
        compiler_params=params(4),
        name="to_units",
    )(jnp.asarray(TO_UNITS), received)
    received = exchange(send, ("tm", "azim"), 128)

    fine, coarse = (2, RADIAL, AXIAL), (2, RADIAL_C, AXIAL_C)
    send = pl.pallas_call(
        units_kernel,
        out_shape=array(SLICES, 16 * 24, 128),
        in_specs=[VMEM] * (1 + len(OPERATORS)),
        out_specs=VMEM,
        scratch_shapes=[
            pltpu.VMEM((2,) + fine, F32),
            pltpu.VMEM((10,) + coarse, F32),
            pltpu.VMEM((10,) + coarse, F32),
            pltpu.VMEM((10,) + fine, F32),
            pltpu.VMEM((10,) + fine, F32),
            pltpu.VMEM((5,) + fine, F32),
            pltpu.VMEM((3,) + fine, F32),
            pltpu.VMEM((11,) + coarse, F32),
            pltpu.VMEM(coarse, F32),
        ],
        compiler_params=params(28),
        name="units",
    )(received, *operators)
    received = exchange(send.reshape(128 * 24, 128), ("tm", "azim"), 128)
    send = pl.pallas_call(
        from_units_kernel,
        out_shape=array(BLOCKS * 144, 128),
        in_specs=[VMEM, VMEM],
        out_specs=VMEM,
        compiler_params=params(8),
        name="from_units",
    )(jnp.asarray(FROM_UNITS), received)
    received = exchange(send, "azim", BLOCKS)
    planes = pl.pallas_call(
        place_kernel,
        out_shape=array(12, RADIAL, AXIAL),
        in_specs=[VMEM],
        out_specs=HBM,
        scratch_shapes=[pltpu.VMEM((12, RADIAL, AXIAL), F32), pltpu.SemaphoreType.DMA((4,))],
        compiler_params=params(6),
        name="place",
    )(received)
    return planes.reshape(1, 3, 4, RADIAL, AXIAL)


def solution(mesh):
    split_planes = P(None, "azim", None, None)
    return jax.shard_map(
        per_device,
        mesh=mesh,
        in_specs=(split_planes, split_planes) + (P(),) * 12,
        out_specs=P("tm", None, "azim", None, None),
        check_vma=False,
    )
```
